256 devices in a mesh: seq: 32 (over y, x, core), chan: 8 (over z).
Axes of the slice: x: 4, y: 4, z: 8, core: 2. Of those that a mesh axis runs over, the one named last changes fastest.
Arguments:
- inner_input: bfloat16 [32768, 8192], P('seq', 'chan'), may hold values from -6 to 6
- state_maps: bfloat16 [32768, 2, 8, 128], P('seq', None, 'chan'), may hold values from -6 to 6
- gate_input: bfloat16 [32768, 8192], P('seq', 'chan'), may hold values from -6 to 6
- step_input: float32 [32768, 128], P('seq', 'chan'), may hold values from -3 to 12
- log_decay_rate: float32 [128], P('chan'), may hold values from 0 to 2.78
- step_bias: float32 [128], P('chan'), may hold values from -17 to 0
- skip_gain: float32 [128], P('chan'), may hold values from 0.5 to 1.5
- conv_kernel: float32 [4, 8192], P(None, 'chan'), may hold values from -3 to 3
- map_kernel: float32 [4, 2, 8, 128], P(None, None, 'chan'), may hold values from -3 to 3
- norm_gain: float32 [8192], P('chan'), may hold values from 0.1 to 1.9
- out_weight: bfloat16 [8192, 2048], P('chan'), may hold values from -0.09375 to 0.09375
Outputs:
- mixed_out: bfloat16 [32768, 2048], P('seq', 'chan')
The draws below stay inside these ranges and needn't reach their ends.
All inputs are finite; a program needn't handle non-finite values.
Results may differ from the reference program's by a relative error of at most 0.011.
Values may be sent and summed in bfloat16 or wider, within the bound.
A program may use at most 128 MiB of HBM per device.

```python
import math
import jax
import jax.numpy as jnp
from jax import lax

HEADS = 128
HEAD_DIM = 64
STATE = 128
NGROUPS = 8
KCONV = 4
BLOCK = 256
DOUT = 2048
TOK_DEV = 1024
INNER = 8192
TOKEN_COUNT = 32768


def head_law(key):
    head_key = jax.random.fold_in(key, 11)
    first_key, second_key, tertiary_key = jax.random.split(head_key, 3)
    fast_share = 8
    fast_heads = jax.random.randint(first_key, (HEADS,), 0, 16) < fast_share
    log_decay_rate = jax.random.uniform(second_key, (HEADS,), jnp.float32, 0.0, math.log(16.0))
    spread = jnp.exp(jax.random.uniform(tertiary_key, (HEADS,), jnp.float32, -0.5, 0.5))
    fast_rate = 1.0 / min(40, TOK_DEV // 4)
    slow_rate = 0.7 / TOKEN_COUNT
    target = jnp.where(fast_heads, fast_rate, slow_rate) * spread / jnp.exp(log_decay_rate)
    return (log_decay_rate, jnp.log(jnp.expm1(target)))


def draw_log_decay_rate(key, part):
    return head_law(key)[0]


def draw_step_bias(key, part):
    return head_law(key)[1]


def draw_step_input(key, part):
    step_key = jax.random.fold_in(key, 23)
    first_key, second_key, tertiary_key = jax.random.split(step_key, 3)
    jitter = 0.5 * jnp.clip(jax.random.normal(first_key, (TOKEN_COUNT, HEADS), jnp.float32), -4.0, 4.0)
    slab_shift = jax.random.uniform(second_key, (TOKEN_COUNT // TOK_DEV, 1, HEADS), jnp.float32, -0.4, 0.4)
    baseline = (jitter.reshape(TOKEN_COUNT // TOK_DEV, TOK_DEV, HEADS) + slab_shift).reshape(TOKEN_COUNT, HEADS)
    surge_rows = jax.random.randint(tertiary_key, (3,), 0, TOKEN_COUNT)
    surge_mask = jnp.any(jnp.arange(TOKEN_COUNT)[:, None] == surge_rows[None, :], axis=1)
    boost_factor = jnp.where(surge_mask, math.log(0.43 * TOKEN_COUNT), 0.0).astype(jnp.float32)
    return baseline + boost_factor[:, None]


def raised(result, key, source, target, blocks, factor):
    owner, partner = [(jnp.arange(result.shape[dim]) // (result.shape[dim] // blocks)).reshape([-1 if axis == dim else 1 for axis in range(result.ndim)]) for dim in (source, target)]
    chosen = jax.random.permutation(key, blocks)[partner]
    strong = (owner == chosen) | (owner == (partner + blocks // 2) % blocks)
    return jnp.where(strong, factor * result, result)


def level_of(own_key, dims, shards, low, high):
    def one(axis_at, shards_of):
        draws = jax.random.uniform(jax.random.fold_in(jax.random.fold_in(own_key, 6), axis_at), (shards_of,), jnp.float32, low / len(shards), high / len(shards))
        return jnp.repeat(jnp.exp(draws), dims[axis_at] // shards_of).reshape((-1,) + (1,) * (len(dims) - axis_at - 1))

    loudness = one(*shards[0])
    for cut in shards[1:]:
        loudness = loudness * one(*cut)
    return loudness


def scatter_about(own_key, shape, deviation, most, cuts=(), dtype=jnp.bfloat16):
    entries = deviation * jax.random.normal(own_key, shape, jnp.float32)
    if cuts:
        entries = entries * level_of(own_key, shape, cuts, -0.22, 0.18)
    return jnp.clip(entries, -most, most).astype(dtype)


def bell_draw_with(own_key, dims, deviation, bound, cuts, heavy, held_as=jnp.bfloat16):
    result = deviation * jax.random.normal(own_key, dims, jnp.float32)
    if cuts:
        result = result * level_of(own_key, dims, cuts, -0.22, 0.18)
    return jnp.clip(raised(result, jax.random.fold_in(own_key, 3), *heavy), -bound, bound).astype(held_as)


def setup_inputs(seed: int = 0) -> dict:
    arg_keys = jax.random.split(jax.random.key(seed), 12)
    return {
        "inner_input": scatter_about(arg_keys[0], (TOKEN_COUNT, INNER), 1.0, 6.0, ((0, 32), (1, 8))),
        "state_maps": scatter_about(arg_keys[1], (TOKEN_COUNT, 2, NGROUPS, STATE), 1.0, 6.0, ((0, 32), (2, 8))),
        "gate_input": scatter_about(arg_keys[2], (TOKEN_COUNT, INNER), 1.0, 6.0, ((0, 32), (1, 8))),
        "step_input": draw_step_input(jax.random.fold_in(arg_keys[11], 71), 0),
        "log_decay_rate": draw_log_decay_rate(jax.random.fold_in(arg_keys[11], 71), 0),
        "step_bias": draw_step_bias(jax.random.fold_in(arg_keys[11], 71), 0),
        "skip_gain": jnp.clip(0.5 + 1.0 * jax.random.uniform(arg_keys[6], (HEADS,), jnp.float32) ** level_of(arg_keys[6], (HEADS,), ((0, 8),), -0.2, 0.2), 0.5, 1.5),
        "conv_kernel": scatter_about(arg_keys[7], (KCONV, INNER), 0.5, 3.0, ((1, 8),), jnp.float32),
        "map_kernel": scatter_about(arg_keys[8], (KCONV, 2, NGROUPS, STATE), 0.5, 3.0, ((2, 8),), jnp.float32),
        "norm_gain": jnp.clip(1.0 + 0.18 * jax.random.normal(arg_keys[9], (INNER,), jnp.float32), 0.1, 1.9),
        "out_weight": bell_draw_with(arg_keys[10], (INNER, DOUT), INNER ** -0.5, 0.09375, ((0, 8),), (0, 1, 8, 2.0)),
    }


step_limit = 0.5
epsilon = 1e-05

def conv_silu(padded, kernel, length):
    acc = jnp.zeros((length,) + padded.shape[1:], jnp.float32)
    for offset in range(kernel.shape[0]):
        acc = acc + kernel[offset] * padded[offset:offset + length].astype(jnp.float32)
    return jax.nn.silu(acc).astype(jnp.bfloat16)

def reference(inner_input, state_maps, gate_input, step_input, log_decay_rate, step_bias, skip_gain, conv_kernel, map_kernel, norm_gain, out_weight):
    per_group = HEADS // NGROUPS
    block_count = TOKEN_COUNT // BLOCK
    kernel_remainder = KCONV - 1
    rate = -jnp.exp(log_decay_rate)
    row_ids = lax.broadcasted_iota(jnp.int32, (BLOCK, BLOCK), 0)
    col_ids = lax.broadcasted_iota(jnp.int32, (BLOCK, BLOCK), 1)
    causal = row_ids >= col_ids

    def advance(carry, inputs):
        state, tail_inner, tail_maps = carry
        inner_rows, map_rows, gate_rows, step_rows = inputs
        inner_conv = conv_silu(jnp.concatenate([tail_inner, inner_rows], 0), conv_kernel, BLOCK)
        maps_conv = conv_silu(jnp.concatenate([tail_maps, map_rows], 0), map_kernel, BLOCK)
        step = jnp.minimum(jax.nn.softplus(step_rows + step_bias), step_limit)
        log_step = step * rate
        cumul = jnp.cumsum(log_step, axis=0).reshape(BLOCK, NGROUPS, per_group)
        step_group = step.reshape(BLOCK, NGROUPS, per_group)
        x_heads = inner_conv.reshape(BLOCK, NGROUPS, per_group, HEAD_DIM).astype(jnp.float32)
        b_rows = maps_conv[:, 0].astype(jnp.float32)
        c_rows = maps_conv[:, 1].astype(jnp.float32)
        scores = jnp.einsum('tgn,sgn->gts', c_rows, b_rows)
        cumul_t = cumul.transpose(1, 2, 0)
        gap = cumul_t[..., :, None] - cumul_t[..., None, :]
        decay = jnp.exp(jnp.where(causal, gap, -jnp.inf))
        mixing = (scores[:, None] * decay * step_group.transpose(1, 2, 0)[..., None, :]).astype(jnp.bfloat16)
        mixing = lax.optimization_barrier(mixing).astype(jnp.float32)
        y_local = jnp.einsum('gjts,sgjp->tgjp', mixing, x_heads)
        state_in = lax.optimization_barrier(state.astype(jnp.bfloat16)).astype(jnp.float32)
        y_carry = jnp.exp(cumul)[..., None] * jnp.einsum('tgn,gjpn->tgjp', c_rows, state_in)
        weighted = ((jnp.exp(cumul[-1:] - cumul) * step_group)[..., None] * b_rows[:, :, None, :]).astype(jnp.bfloat16)
        weighted = lax.optimization_barrier(weighted).astype(jnp.float32)
        updated_state = jnp.exp(cumul[-1])[..., None, None] * state + jnp.einsum('sgjp,sgjn->gjpn', x_heads, weighted)
        y_all = y_local + y_carry + skip_gain.reshape(NGROUPS, per_group)[:, :, None] * x_heads
        gated = y_all.reshape(BLOCK, NGROUPS, per_group * HEAD_DIM) * jax.nn.silu(gate_rows.reshape(BLOCK, NGROUPS, per_group * HEAD_DIM).astype(jnp.float32))
        square_mean = lax.optimization_barrier(jnp.mean(gated * gated, axis=-1, keepdims=True))
        normed = (gated * lax.rsqrt(square_mean + epsilon) * norm_gain.reshape(NGROUPS, -1)).astype(jnp.bfloat16).reshape(BLOCK, INNER)
        out_rows = jnp.dot(normed, out_weight, preferred_element_type=jnp.float32).astype(jnp.bfloat16)
        return ((updated_state, inner_rows[BLOCK - kernel_remainder:], map_rows[BLOCK - kernel_remainder:]), out_rows)
    start_state = jnp.zeros((NGROUPS, per_group, HEAD_DIM, STATE), jnp.float32)
    start_inner = jnp.zeros((kernel_remainder, INNER), jnp.bfloat16)
    start_maps = jnp.zeros((kernel_remainder, 2, NGROUPS, STATE), jnp.bfloat16)
    inputs = (inner_input.reshape(block_count, BLOCK, INNER), state_maps.reshape(block_count, BLOCK, 2, NGROUPS, STATE), gate_input.reshape(block_count, BLOCK, INNER), step_input.reshape(block_count, BLOCK, HEADS))
    final_carry, outputs = lax.scan(advance, (start_state, start_inner, start_maps), inputs)
    return outputs.reshape(TOKEN_COUNT, DOUT)
```

```python
import jax
import jax.numpy as jnp
from jax import lax
from jax.sharding import PartitionSpec as P

HEADS = 128
HEAD_DIM = 64
STATE = 128
NGROUPS = 8
BLOCK = 256


step_limit = 0.5
epsilon = 1e-05


def passed_along(x, axis, by):
    count = lax.axis_size(axis)
    pairs = [(i, i + by) for i in range(count) if 0 <= i + by < count]
    return lax.ppermute(x, axis, pairs)


def conv_silu(padded, kernel, length):
    acc = jnp.zeros((length,) + padded.shape[1:], jnp.float32)
    for offset in range(kernel.shape[0]):
        acc = acc + kernel[offset] * padded[offset : offset + length].astype(jnp.float32)
    return jax.nn.silu(acc).astype(jnp.bfloat16)


def local(
    inner_input,
    state_maps,
    gate_input,
    step_input,
    log_decay_rate,
    step_bias,
    skip_gain,
    conv_kernel,
    map_kernel,
    norm_gain,
    out_weight,
):
    row_count = inner_input.shape[0]
    kernel_remainder = conv_kernel.shape[0] - 1
    groups = state_maps.shape[2]
    per_group = HEADS // NGROUPS
    head_count = groups * per_group
    block_count = row_count // BLOCK
    tail_inner, tail_maps = passed_along(
        (inner_input[row_count - kernel_remainder :], state_maps[row_count - kernel_remainder :]),
        "seq",
        1,
    )
    inner_conv = conv_silu(
        jnp.concatenate((tail_inner, inner_input), axis=0), conv_kernel, row_count
    )
    maps_conv = conv_silu(jnp.concatenate((tail_maps, state_maps), axis=0), map_kernel, row_count)
    step = jnp.minimum(jax.nn.softplus(step_input + step_bias), step_limit)
    log_step = step * -jnp.exp(log_decay_rate)
    step_blocks = step.reshape(block_count, BLOCK, groups, per_group)
    cumul = jnp.cumsum(log_step.reshape(block_count, BLOCK, groups, per_group), axis=1)
    x_blocks = inner_conv.reshape(block_count, BLOCK, groups, per_group, HEAD_DIM)
    b_blocks = maps_conv[:, 0].reshape(block_count, BLOCK, groups, STATE)
    c_blocks = maps_conv[:, 1].reshape(block_count, BLOCK, groups, STATE)
    scores = jnp.einsum("ctgn,csgn->cgts", c_blocks, b_blocks, preferred_element_type=jnp.float32)
    cumul_t = cumul.transpose(0, 2, 3, 1)
    gap = cumul_t[..., :, None] - cumul_t[..., None, :]
    row_ids = lax.broadcasted_iota(jnp.int32, (BLOCK, BLOCK), 0)
    col_ids = lax.broadcasted_iota(jnp.int32, (BLOCK, BLOCK), 1)
    decay = jnp.exp(jnp.where(row_ids >= col_ids, gap, -jnp.inf))
    mixing = (scores[:, :, None] * decay * step_blocks.transpose(0, 2, 3, 1)[..., None, :]).astype(
        jnp.bfloat16
    )
    y_local = jnp.einsum("cgjts,csgjp->ctgjp", mixing, x_blocks, preferred_element_type=jnp.float32)
    weighted = (
        (jnp.exp(cumul[:, -1:] - cumul) * step_blocks)[..., None] * b_blocks[:, :, :, None, :]
    ).astype(jnp.bfloat16)
    block_states = jnp.einsum(
        "csgjp,csgjn->cgjpn", x_blocks, weighted, preferred_element_type=jnp.float32
    )
    block_decay = cumul[:, -1]
    running = jnp.zeros((groups, per_group, HEAD_DIM, STATE), jnp.float32)
    local_in = []
    for block_index in range(block_count):
        local_in.append(running)
        running = (
            jnp.exp(block_decay[block_index])[..., None, None] * running + block_states[block_index]
        )
    slab_decay = jnp.sum(block_decay, axis=0)
    device_index = lax.axis_index("seq")
    state_rows = groups * per_group * HEAD_DIM
    decay_hi = slab_decay.reshape(-1).astype(jnp.bfloat16)
    decay_rest = slab_decay.reshape(-1) - decay_hi.astype(jnp.float32)
    decay_mid = decay_rest.astype(jnp.bfloat16)
    decay_lo = (decay_rest - decay_mid.astype(jnp.float32)).astype(jnp.bfloat16)
    decay_rows = jnp.zeros((8, STATE), jnp.bfloat16)
    decay_rows = decay_rows.at[0:3, 0:head_count].set(jnp.stack((decay_hi, decay_mid, decay_lo)))
    packed = jnp.concatenate(
        (running.reshape(state_rows, STATE).astype(jnp.bfloat16), decay_rows), axis=0
    )
    gathered = lax.all_gather(packed, "seq", axis=0, tiled=False)
    decays = (
        jnp.sum(gathered[:, state_rows : state_rows + 3, 0:head_count].astype(jnp.float32), axis=1)
        .reshape(-1, groups, per_group)
    )
    before = jnp.cumsum(decays, axis=0) - decays
    through = before + decays
    mine = lax.dynamic_index_in_dim(before, device_index, 0, keepdims=False)
    shard_piece = (
        gathered[:, :state_rows].reshape((-1,) + running.shape).astype(jnp.float32)
    )
    piece_rows = shard_piece.shape[0]
    owners = lax.broadcasted_iota(jnp.int32, (piece_rows, 1, 1), 0)
    factors = jnp.exp(jnp.where(owners < device_index, mine[None] - through, -jnp.inf))
    entering = jnp.zeros_like(running) + jnp.einsum(
        "rgj,rgjpn->gjpn", factors, shard_piece, precision=lax.Precision.HIGHEST
    )
    leading = jnp.cumsum(block_decay, axis=0) - block_decay
    state_in = (
        jnp.exp(leading)[..., None, None] * entering[None] + jnp.stack(local_in, axis=0)
    ).astype(jnp.bfloat16)
    y_carry = jnp.exp(cumul)[..., None] * jnp.einsum(
        "ctgn,cgjpn->ctgjp", c_blocks, state_in, preferred_element_type=jnp.float32
    )
    y_all = y_local + y_carry + skip_gain.reshape(groups, per_group)[:, :, None] * x_blocks
    width = per_group * HEAD_DIM
    gated = y_all.reshape(row_count, groups, width) * jax.nn.silu(
        gate_input.reshape(row_count, groups, width).astype(jnp.float32)
    )
    square_mean = jnp.mean(gated * gated, axis=-1, keepdims=True)
    normed = (
        (gated * lax.rsqrt(square_mean + epsilon) * norm_gain.reshape(groups, width))
        .astype(jnp.bfloat16)
        .reshape(row_count, head_count * HEAD_DIM)
    )
    shares = lax.psum_scatter(
        lax.dot_general(
            out_weight, normed, (((0,), (1,)), ((), ())), preferred_element_type=jnp.float32
        ).astype(jnp.bfloat16),
        "chan",
        scatter_dimension=0,
        tiled=True,
    )
    return shares.T


def solution(mesh):
    return jax.shard_map(
        local,
        mesh=mesh,
        in_specs=(
            P("seq", "chan"),
            P("seq", None, "chan", None),
            P("seq", "chan"),
            P("seq", "chan"),
            P("chan"),
            P("chan"),
            P("chan"),
            P(None, "chan"),
            P(None, None, "chan", None),
            P("chan"),
            P("chan", None),
        ),
        out_specs=P("seq", "chan"),
        check_vma=False,
    )
```

```python
import jax
import jax.numpy as jnp
from jax import lax
from jax.sharding import PartitionSpec as P

HEADS = 128
HEAD_DIM = 64
STATE = 128
NGROUPS = 8
BLOCK = 256


step_limit = 0.5
epsilon = 1e-05


def passed_along(x, axis, by):
    count = lax.axis_size(axis)
    pairs = [(i, i + by) for i in range(count) if 0 <= i + by < count]
    return lax.ppermute(x, axis, pairs)


def conv_silu(padded, kernel, length):
    acc = jnp.zeros((length,) + padded.shape[1:], jnp.float32)
    for offset in range(kernel.shape[0]):
        acc = acc + kernel[offset] * padded[offset : offset + length].astype(jnp.float32)
    return jax.nn.silu(acc).astype(jnp.bfloat16)


def local(
    inner_input,
    state_maps,
    gate_input,
    step_input,
    log_decay_rate,
    step_bias,
    skip_gain,
    conv_kernel,
    map_kernel,
    norm_gain,
    out_weight,
):
    row_count = inner_input.shape[0]
    kernel_remainder = conv_kernel.shape[0] - 1
    groups = state_maps.shape[2]
    per_group = HEADS // NGROUPS
    head_count = groups * per_group
    block_count = row_count // BLOCK
    tail_inner, tail_maps = passed_along(
        (inner_input[row_count - kernel_remainder :], state_maps[row_count - kernel_remainder :]),
        "seq",
        1,
    )
    inner_conv = conv_silu(
        jnp.concatenate((tail_inner, inner_input), axis=0), conv_kernel, row_count
    )
    maps_conv = conv_silu(jnp.concatenate((tail_maps, state_maps), axis=0), map_kernel, row_count)
    step = jnp.minimum(jax.nn.softplus(step_input + step_bias), step_limit)
    log_step = step * -jnp.exp(log_decay_rate)
    step_blocks = step.reshape(block_count, BLOCK, groups, per_group)
    cumul = jnp.cumsum(log_step.reshape(block_count, BLOCK, groups, per_group), axis=1)
    x_blocks = inner_conv.reshape(block_count, BLOCK, groups, per_group, HEAD_DIM)
    b_blocks = maps_conv[:, 0].reshape(block_count, BLOCK, groups, STATE)
    c_blocks = maps_conv[:, 1].reshape(block_count, BLOCK, groups, STATE)
    scores = jnp.einsum("ctgn,csgn->cgts", c_blocks, b_blocks, preferred_element_type=jnp.float32)
    cumul_t = cumul.transpose(0, 2, 3, 1)
    gap = cumul_t[..., :, None] - cumul_t[..., None, :]
    row_ids = lax.broadcasted_iota(jnp.int32, (BLOCK, BLOCK), 0)
    col_ids = lax.broadcasted_iota(jnp.int32, (BLOCK, BLOCK), 1)
    decay = jnp.exp(jnp.where(row_ids >= col_ids, gap, -jnp.inf))
    mixing = (scores[:, :, None] * decay * step_blocks.transpose(0, 2, 3, 1)[..., None, :]).astype(
        jnp.bfloat16
    )
    y_local = jnp.einsum("cgjts,csgjp->ctgjp", mixing, x_blocks, preferred_element_type=jnp.float32)
    weighted = (
        (jnp.exp(cumul[:, -1:] - cumul) * step_blocks)[..., None] * b_blocks[:, :, :, None, :]
    ).astype(jnp.bfloat16)
    block_states = jnp.einsum(
        "csgjp,csgjn->cgjpn", x_blocks, weighted, preferred_element_type=jnp.float32
    )
    block_decay = cumul[:, -1]
    running = jnp.zeros((groups, per_group, HEAD_DIM, STATE), jnp.float32)
    local_in = []
    for block_index in range(block_count):
        local_in.append(running)
        running = (
            jnp.exp(block_decay[block_index])[..., None, None] * running + block_states[block_index]
        )
    slab_decay = jnp.sum(block_decay, axis=0)
    device_index = lax.axis_index("seq")
    state_rows = groups * per_group * HEAD_DIM
    decay_hi = slab_decay.reshape(-1).astype(jnp.bfloat16)
    decay_rest = slab_decay.reshape(-1) - decay_hi.astype(jnp.float32)
    decay_mid = decay_rest.astype(jnp.bfloat16)
    decay_lo = (decay_rest - decay_mid.astype(jnp.float32)).astype(jnp.bfloat16)
    decay_rows = jnp.zeros((8, STATE), jnp.bfloat16)
    decay_rows = decay_rows.at[0:3, 0:head_count].set(jnp.stack((decay_hi, decay_mid, decay_lo)))
    packed = jnp.concatenate(
        (running.reshape(state_rows, STATE).astype(jnp.bfloat16), decay_rows), axis=0
    )
    gathered = lax.all_gather(packed, "seq", axis=0, tiled=False)
    decays = (
        jnp.sum(gathered[:, state_rows : state_rows + 3, 0:head_count].astype(jnp.float32), axis=1)
        .reshape(-1, groups, per_group)
    )
    before = jnp.cumsum(decays, axis=0) - decays
    through = before + decays
    mine = lax.dynamic_index_in_dim(before, device_index, 0, keepdims=False)
    piece_rows = gathered.shape[0]
    owners = lax.broadcasted_iota(jnp.int32, (piece_rows, 1, 1), 0)
    factors = jnp.exp(jnp.where(owners < device_index, mine[None] - through, -jnp.inf))
    factor_rows = jnp.concatenate(
        (
            jnp.repeat(factors.reshape(piece_rows, head_count), HEAD_DIM, axis=1),
            jnp.zeros((piece_rows, gathered.shape[1] - state_rows), jnp.float32),
        ),
        axis=1,
    )
    entering = jnp.sum(factor_rows[:, :, None] * gathered.astype(jnp.float32), axis=0)
    entering = entering[:state_rows].reshape(running.shape)
    leading = jnp.cumsum(block_decay, axis=0) - block_decay
    state_in = (
        jnp.exp(leading)[..., None, None] * entering[None] + jnp.stack(local_in, axis=0)
    ).astype(jnp.bfloat16)
    width = per_group * HEAD_DIM
    y_pre = lax.optimization_barrier(
        y_local + skip_gain.reshape(groups, per_group)[:, :, None] * x_blocks
    )
    chunk_count = 2
    per_chunk = block_count // chunk_count
    outs = []
    for chunk in range(chunk_count):
        part = slice(chunk * per_chunk, (chunk + 1) * per_chunk)
        rows = per_chunk * BLOCK
        y_carry = jnp.exp(cumul[part])[..., None] * jnp.einsum(
            "ctgn,cgjpn->ctgjp", c_blocks[part], state_in[part], preferred_element_type=jnp.float32
        )
        y_all = y_pre[part] + y_carry
        gate_rows = gate_input[chunk * rows : (chunk + 1) * rows]
        gated = y_all.reshape(rows, groups, width) * jax.nn.silu(
            gate_rows.reshape(rows, groups, width).astype(jnp.float32)
        )
        square_mean = jnp.mean(gated * gated, axis=-1, keepdims=True)
        normed = (
            (gated * lax.rsqrt(square_mean + epsilon) * norm_gain.reshape(groups, width))
            .astype(jnp.bfloat16)
            .reshape(rows, head_count * HEAD_DIM)
        )
        shares = lax.psum_scatter(
            lax.dot_general(
                out_weight, normed, (((0,), (1,)), ((), ())), preferred_element_type=jnp.float32
            ).astype(jnp.bfloat16),
            "chan",
            scatter_dimension=0,
            tiled=True,
        )
        outs.append(shares.T)
    return jnp.concatenate(outs, axis=0)


def solution(mesh):
    return jax.shard_map(
        local,
        mesh=mesh,
        in_specs=(
            P("seq", "chan"),
            P("seq", None, "chan", None),
            P("seq", "chan"),
            P("seq", "chan"),
            P("chan"),
            P("chan"),
            P("chan"),
            P(None, "chan"),
            P(None, None, "chan", None),
            P("chan"),
            P("chan", None),
        ),
        out_specs=P("seq", "chan"),
        check_vma=False,
    )
```

```python
import jax
import jax.numpy as jnp
from jax import lax
from jax.sharding import PartitionSpec as P

HEADS = 128
HEAD_DIM = 64
STATE = 128
NGROUPS = 8
BLOCK = 256


step_limit = 0.5
epsilon = 1e-05


def passed_along(x, axis, by):
    count = lax.axis_size(axis)
    pairs = [(i, i + by) for i in range(count) if 0 <= i + by < count]
    return lax.ppermute(x, axis, pairs)


def conv_silu(padded, kernel, length):
    acc = jnp.zeros((length,) + padded.shape[1:], jnp.float32)
    for offset in range(kernel.shape[0]):
        acc = acc + kernel[offset] * padded[offset : offset + length].astype(jnp.float32)
    return jax.nn.silu(acc).astype(jnp.bfloat16)


def local(
    inner_input,
    state_maps,
    gate_input,
    step_input,
    log_decay_rate,
    step_bias,
    skip_gain,
    conv_kernel,
    map_kernel,
    norm_gain,
    out_weight,
):
    row_count = inner_input.shape[0]
    kernel_remainder = conv_kernel.shape[0] - 1
    groups = state_maps.shape[2]
    per_group = HEADS // NGROUPS
    head_count = groups * per_group
    block_count = row_count // BLOCK
    tail_inner, tail_maps = passed_along(
        (inner_input[row_count - kernel_remainder :], state_maps[row_count - kernel_remainder :]),
        "seq",
        1,
    )
    inner_conv = conv_silu(
        jnp.concatenate((tail_inner, inner_input), axis=0), conv_kernel, row_count
    )
    maps_conv = conv_silu(jnp.concatenate((tail_maps, state_maps), axis=0), map_kernel, row_count)
    step = jnp.minimum(jax.nn.softplus(step_input + step_bias), step_limit)
    log_step = step * -jnp.exp(log_decay_rate)
    step_blocks = step.reshape(block_count, BLOCK, groups, per_group)
    cumul = jnp.cumsum(log_step.reshape(block_count, BLOCK, groups, per_group), axis=1)
    x_blocks = inner_conv.reshape(block_count, BLOCK, groups, per_group, HEAD_DIM)
    b_blocks = maps_conv[:, 0].reshape(block_count, BLOCK, groups, STATE)
    c_blocks = maps_conv[:, 1].reshape(block_count, BLOCK, groups, STATE)
    scores = jnp.einsum("ctgn,csgn->cgts", c_blocks, b_blocks, preferred_element_type=jnp.float32)
    cumul_t = cumul.transpose(0, 2, 3, 1)
    gap = cumul_t[..., :, None] - cumul_t[..., None, :]
    row_ids = lax.broadcasted_iota(jnp.int32, (BLOCK, BLOCK), 0)
    col_ids = lax.broadcasted_iota(jnp.int32, (BLOCK, BLOCK), 1)
    decay = jnp.exp(jnp.where(row_ids >= col_ids, gap, -jnp.inf))
    mixing = (scores[:, :, None] * decay * step_blocks.transpose(0, 2, 3, 1)[..., None, :]).astype(
        jnp.bfloat16
    )
    y_local = jnp.einsum("cgjts,csgjp->ctgjp", mixing, x_blocks, preferred_element_type=jnp.float32)
    weighted = (
        (jnp.exp(cumul[:, -1:] - cumul) * step_blocks)[..., None] * b_blocks[:, :, :, None, :]
    ).astype(jnp.bfloat16)
    block_states = jnp.einsum(
        "csgjp,csgjn->cgjpn", x_blocks, weighted, preferred_element_type=jnp.float32
    )
    block_decay = cumul[:, -1]
    running = jnp.zeros((groups, per_group, HEAD_DIM, STATE), jnp.float32)
    local_in = []
    for block_index in range(block_count):
        local_in.append(running)
        running = (
            jnp.exp(block_decay[block_index])[..., None, None] * running + block_states[block_index]
        )
    slab_decay = jnp.sum(block_decay, axis=0)
    device_index = lax.axis_index("seq")
    state_rows = groups * per_group * HEAD_DIM
    decay_hi = slab_decay.reshape(-1).astype(jnp.bfloat16)
    decay_rest = slab_decay.reshape(-1) - decay_hi.astype(jnp.float32)
    decay_mid = decay_rest.astype(jnp.bfloat16)
    decay_lo = (decay_rest - decay_mid.astype(jnp.float32)).astype(jnp.bfloat16)
    decay_rows = jnp.zeros((8, STATE), jnp.bfloat16)
    decay_rows = decay_rows.at[0:3, 0:head_count].set(jnp.stack((decay_hi, decay_mid, decay_lo)))
    packed = jnp.concatenate(
        (running.reshape(state_rows, STATE).astype(jnp.bfloat16), decay_rows), axis=0
    )
    gathered = lax.all_gather(packed, "seq", axis=0, tiled=False)
    decays = (
        jnp.sum(gathered[:, state_rows : state_rows + 3, 0:head_count].astype(jnp.float32), axis=1)
        .reshape(-1, groups, per_group)
    )
    before = jnp.cumsum(decays, axis=0) - decays
    through = before + decays
    mine = lax.dynamic_index_in_dim(before, device_index, 0, keepdims=False)
    piece_rows = gathered.shape[0]
    owners = lax.broadcasted_iota(jnp.int32, (piece_rows, 1, 1), 0)
    factors = jnp.exp(jnp.where(owners < device_index, mine[None] - through, -jnp.inf))
    factor_rows = jnp.concatenate(
        (
            jnp.repeat(factors.reshape(piece_rows, head_count), HEAD_DIM, axis=1),
            jnp.zeros((piece_rows, gathered.shape[1] - state_rows), jnp.float32),
        ),
        axis=1,
    )
    entering = jnp.sum(factor_rows[:, :, None] * gathered.astype(jnp.float32), axis=0)
    entering = entering[:state_rows].reshape(running.shape)
    leading = jnp.cumsum(block_decay, axis=0) - block_decay
    state_in = (
        jnp.exp(leading)[..., None, None] * entering[None] + jnp.stack(local_in, axis=0)
    ).astype(jnp.bfloat16)
    width = per_group * HEAD_DIM
    y_pre = lax.optimization_barrier(
        y_local + skip_gain.reshape(groups, per_group)[:, :, None] * x_blocks
    )
    chunk_count = 1
    per_chunk = block_count // chunk_count
    outs = []
    for chunk in range(chunk_count):
        part = slice(chunk * per_chunk, (chunk + 1) * per_chunk)
        rows = per_chunk * BLOCK
        y_carry = jnp.exp(cumul[part])[..., None] * jnp.einsum(
            "ctgn,cgjpn->ctgjp", c_blocks[part], state_in[part], preferred_element_type=jnp.float32
        )
        y_all = y_pre[part] + y_carry
        gate_rows = gate_input[chunk * rows : (chunk + 1) * rows]
        gated = y_all.reshape(rows, groups, width) * jax.nn.silu(
            gate_rows.reshape(rows, groups, width).astype(jnp.float32)
        )
        square_mean = jnp.mean(gated * gated, axis=-1, keepdims=True)
        normed = (
            (gated * lax.rsqrt(square_mean + epsilon) * norm_gain.reshape(groups, width))
            .astype(jnp.bfloat16)
            .reshape(rows, head_count * HEAD_DIM)
        )
        shares = lax.psum_scatter(
            lax.dot_general(
                out_weight, normed, (((0,), (1,)), ((), ())), preferred_element_type=jnp.float32
            ).astype(jnp.bfloat16),
            "chan",
            scatter_dimension=0,
            tiled=True,
        )
        outs.append(shares.T)
    return jnp.concatenate(outs, axis=0)


def solution(mesh):
    return jax.shard_map(
        local,
        mesh=mesh,
        in_specs=(
            P("seq", "chan"),
            P("seq", None, "chan", None),
            P("seq", "chan"),
            P("seq", "chan"),
            P("chan"),
            P("chan"),
            P("chan"),
            P(None, "chan"),
            P(None, None, "chan", None),
            P("chan"),
            P("chan", None),
        ),
        out_specs=P("seq", "chan"),
        check_vma=False,
    )
```

```python
import jax
import jax.numpy as jnp
from jax import lax
from jax.sharding import PartitionSpec as P

HEADS = 128
HEAD_DIM = 64
STATE = 128
NGROUPS = 8
BLOCK = 256


step_limit = 0.5
epsilon = 1e-05


def passed_along(x, axis, by):
    count = lax.axis_size(axis)
    pairs = [(i, i + by) for i in range(count) if 0 <= i + by < count]
    return lax.ppermute(x, axis, pairs)


def conv_silu(padded, kernel, length):
    acc = jnp.zeros((length,) + padded.shape[1:], jnp.float32)
    for offset in range(kernel.shape[0]):
        acc = acc + kernel[offset] * padded[offset : offset + length].astype(jnp.float32)
    return jax.nn.silu(acc).astype(jnp.bfloat16)


def local(
    inner_input,
    state_maps,
    gate_input,
    step_input,
    log_decay_rate,
    step_bias,
    skip_gain,
    conv_kernel,
    map_kernel,
    norm_gain,
    out_weight,
):
    row_count = inner_input.shape[0]
    kernel_remainder = conv_kernel.shape[0] - 1
    groups = state_maps.shape[2]
    per_group = HEADS // NGROUPS
    head_count = groups * per_group
    block_count = row_count // BLOCK
    tail_inner, tail_maps = passed_along(
        (inner_input[row_count - kernel_remainder :], state_maps[row_count - kernel_remainder :]),
        "seq",
        1,
    )
    inner_conv = conv_silu(
        jnp.concatenate((tail_inner, inner_input), axis=0), conv_kernel, row_count
    )
    maps_conv = conv_silu(jnp.concatenate((tail_maps, state_maps), axis=0), map_kernel, row_count)
    step = jnp.minimum(jax.nn.softplus(step_input + step_bias), step_limit)
    log_step = step * -jnp.exp(log_decay_rate)
    step_blocks = step.reshape(block_count, BLOCK, groups, per_group)
    cumul = jnp.cumsum(log_step.reshape(block_count, BLOCK, groups, per_group), axis=1)
    x_blocks = inner_conv.reshape(block_count, BLOCK, groups, per_group, HEAD_DIM)
    b_blocks = maps_conv[:, 0].reshape(block_count, BLOCK, groups, STATE)
    c_blocks = maps_conv[:, 1].reshape(block_count, BLOCK, groups, STATE)
    scores = jnp.einsum("ctgn,csgn->cgts", c_blocks, b_blocks, preferred_element_type=jnp.float32)
    cumul_t = cumul.transpose(0, 2, 3, 1)
    gap = cumul_t[..., :, None] - cumul_t[..., None, :]
    row_ids = lax.broadcasted_iota(jnp.int32, (BLOCK, BLOCK), 0)
    col_ids = lax.broadcasted_iota(jnp.int32, (BLOCK, BLOCK), 1)
    decay = jnp.exp(jnp.where(row_ids >= col_ids, gap, -jnp.inf))
    mixing = (scores[:, :, None] * decay * step_blocks.transpose(0, 2, 3, 1)[..., None, :]).astype(
        jnp.bfloat16
    )
    y_local = jnp.einsum("cgjts,csgjp->ctgjp", mixing, x_blocks, preferred_element_type=jnp.float32)
    weighted = (
        (jnp.exp(cumul[:, -1:] - cumul) * step_blocks)[..., None] * b_blocks[:, :, :, None, :]
    ).astype(jnp.bfloat16)
    block_states = jnp.einsum(
        "csgjp,csgjn->cgjpn", x_blocks, weighted, preferred_element_type=jnp.float32
    )
    block_decay = cumul[:, -1]
    running = jnp.zeros((groups, per_group, HEAD_DIM, STATE), jnp.float32)
    local_in = []
    for block_index in range(block_count):
        local_in.append(running)
        running = (
            jnp.exp(block_decay[block_index])[..., None, None] * running + block_states[block_index]
        )
    slab_decay = jnp.sum(block_decay, axis=0)
    seq_count = lax.axis_size("seq")
    carried_decay = passed_along(slab_decay, "seq", 1)
    carried_state = passed_along(running.astype(jnp.bfloat16), "seq", 1).astype(jnp.float32)
    distance = 1
    while distance < seq_count:
        earlier_decay = passed_along(carried_decay, "seq", distance)
        earlier_state = passed_along(carried_state.astype(jnp.bfloat16), "seq", distance)
        carried_state = (
            jnp.exp(carried_decay)[..., None, None] * earlier_state.astype(jnp.float32)
            + carried_state
        )
        carried_decay = earlier_decay + carried_decay
        distance *= 2
    entering = carried_state
    leading = jnp.cumsum(block_decay, axis=0) - block_decay
    state_in = (
        jnp.exp(leading)[..., None, None] * entering[None] + jnp.stack(local_in, axis=0)
    ).astype(jnp.bfloat16)
    width = per_group * HEAD_DIM
    y_pre = lax.optimization_barrier(
        y_local + skip_gain.reshape(groups, per_group)[:, :, None] * x_blocks
    )
    chunk_count = 1
    per_chunk = block_count // chunk_count
    outs = []
    for chunk in range(chunk_count):
        part = slice(chunk * per_chunk, (chunk + 1) * per_chunk)
        rows = per_chunk * BLOCK
        y_carry = jnp.exp(cumul[part])[..., None] * jnp.einsum(
            "ctgn,cgjpn->ctgjp", c_blocks[part], state_in[part], preferred_element_type=jnp.float32
        )
        y_all = y_pre[part] + y_carry
        gate_rows = gate_input[chunk * rows : (chunk + 1) * rows]
        gated = y_all.reshape(rows, groups, width) * jax.nn.silu(
            gate_rows.reshape(rows, groups, width).astype(jnp.float32)
        )
        square_mean = jnp.mean(gated * gated, axis=-1, keepdims=True)
        normed = (
            (gated * lax.rsqrt(square_mean + epsilon) * norm_gain.reshape(groups, width))
            .astype(jnp.bfloat16)
            .reshape(rows, head_count * HEAD_DIM)
        )
        shares = lax.psum_scatter(
            lax.dot_general(
                out_weight, normed, (((0,), (1,)), ((), ())), preferred_element_type=jnp.float32
            ).astype(jnp.bfloat16),
            "chan",
            scatter_dimension=0,
            tiled=True,
        )
        outs.append(shares.T)
    return jnp.concatenate(outs, axis=0)


def solution(mesh):
    return jax.shard_map(
        local,
        mesh=mesh,
        in_specs=(
            P("seq", "chan"),
            P("seq", None, "chan", None),
            P("seq", "chan"),
            P("seq", "chan"),
            P("chan"),
            P("chan"),
            P("chan"),
            P(None, "chan"),
            P(None, None, "chan", None),
            P("chan"),
            P("chan", None),
        ),
        out_specs=P("seq", "chan"),
        check_vma=False,
    )
```

```python
import functools

import jax
import jax.numpy as jnp
from jax import lax
from jax.experimental import pallas as pl
from jax.experimental.pallas import tpu as pltpu
from jax.sharding import PartitionSpec as P

HEADS = 128
HEAD_DIM = 64
STATE = 128
NGROUPS = 8
BLOCK = 256


step_limit = 0.5
epsilon = 1e-05


def passed_along(x, axis, by):
    count = lax.axis_size(axis)
    pairs = [(i, i + by) for i in range(count) if 0 <= i + by < count]
    return lax.ppermute(x, axis, pairs)


def conv_silu(padded, kernel, length):
    acc = jnp.zeros((length,) + padded.shape[1:], jnp.float32)
    for offset in range(kernel.shape[0]):
        acc = acc + kernel[offset] * padded[offset : offset + length].astype(jnp.float32)
    return jax.nn.silu(acc).astype(jnp.bfloat16)


MESH = pl.DeviceIdType.MESH


def scan_distances(count):
    distances = []
    distance = 1
    while distance < count:
        distances.append(distance)
        distance *= 2
    return distances


def state_scan_kernel(count, state_ref, decay_ref, out_ref, cur_d, send_s, send_d, recv_s, recv_d, ssem, rsem):
    me = lax.axis_index("seq")
    chan = lax.axis_index("chan")
    distances = scan_distances(count)
    rounds = [1] + distances
    barrier = pltpu.get_barrier_semaphore()
    peers = jnp.int32(0)
    for distance in distances:
        for target in (me + distance, me - distance):
            valid = jnp.logical_and(target >= 0, target < count)

            @pl.when(valid)
            def _():
                pl.semaphore_signal(barrier, 1, device_id=(target, chan), device_id_type=MESH)

            peers = peers + valid.astype(jnp.int32)
    pl.semaphore_wait(barrier, peers)

    outgoing = []
    for index, distance in enumerate(rounds):
        if index == 0:
            send_s[index] = state_ref[...].astype(jnp.bfloat16)
            send_d[index] = decay_ref[...]
        else:
            send_s[index] = out_ref[...].astype(jnp.bfloat16)
            send_d[index] = cur_d[...]
        pair = []
        for part, (src, dst) in enumerate(((send_s, recv_s), (send_d, recv_d))):
            pair.append(
                lambda target, src=src, dst=dst, part=part, index=index: pltpu.make_async_remote_copy(
                    src_ref=src.at[index],
                    dst_ref=dst.at[index],
                    send_sem=ssem.at[index, part],
                    recv_sem=rsem.at[index, part],
                    device_id=(target, chan),
                    device_id_type=MESH,
                )
            )
        sends = me + distance < count
        receives = me - distance >= 0

        @pl.when(sends)
        def _():
            for make in pair:
                make(me + distance).start()

        outgoing.append((sends, pair, distance))

        @pl.when(receives)
        def _():
            for make in pair:
                make(me - distance).wait_recv()
            if index == 0:
                out_ref[...] = recv_s[index].astype(jnp.float32)
                cur_d[...] = recv_d[index]
            else:
                scale = jnp.exp(cur_d[:, 0:1, :])
                out_ref[...] = scale * recv_s[index].astype(jnp.float32) + out_ref[...]
                cur_d[...] = recv_d[index] + cur_d[...]

        if index == 0:

            @pl.when(jnp.logical_not(receives))
            def _():
                out_ref[...] = jnp.zeros_like(out_ref)
                cur_d[...] = jnp.zeros_like(cur_d)

    for sends, pair, distance in outgoing:

        @pl.when(sends)
        def _():
            for make in pair:
                make(me + distance).wait_send()


def state_scan(state, decay):
    count = lax.axis_size("seq")
    rounds = 1 + len(scan_distances(count))
    heads, rows, width = state.shape
    return pl.pallas_call(
        functools.partial(state_scan_kernel, count),
        out_shape=jax.ShapeDtypeStruct(state.shape, jnp.float32),
        in_specs=[pl.BlockSpec(memory_space=pltpu.VMEM)] * 2,
        out_specs=pl.BlockSpec(memory_space=pltpu.VMEM),
        scratch_shapes=[
            pltpu.VMEM(decay.shape, jnp.float32),
            pltpu.VMEM((rounds,) + state.shape, jnp.bfloat16),
            pltpu.VMEM((rounds,) + decay.shape, jnp.float32),
            pltpu.VMEM((rounds,) + state.shape, jnp.bfloat16),
            pltpu.VMEM((rounds,) + decay.shape, jnp.float32),
            pltpu.SemaphoreType.DMA((rounds, 2)),
            pltpu.SemaphoreType.DMA((rounds, 2)),
        ],
        compiler_params=pltpu.CompilerParams(collective_id=0, has_side_effects=True),
        name="state_scan",
    )(state, decay)


def local(
    inner_input,
    state_maps,
    gate_input,
    step_input,
    log_decay_rate,
    step_bias,
    skip_gain,
    conv_kernel,
    map_kernel,
    norm_gain,
    out_weight,
):
    row_count = inner_input.shape[0]
    kernel_remainder = conv_kernel.shape[0] - 1
    groups = state_maps.shape[2]
    per_group = HEADS // NGROUPS
    head_count = groups * per_group
    block_count = row_count // BLOCK
    tail_inner, tail_maps = passed_along(
        (inner_input[row_count - kernel_remainder :], state_maps[row_count - kernel_remainder :]),
        "seq",
        1,
    )
    inner_conv = conv_silu(
        jnp.concatenate((tail_inner, inner_input), axis=0), conv_kernel, row_count
    )
    maps_conv = conv_silu(jnp.concatenate((tail_maps, state_maps), axis=0), map_kernel, row_count)
    step = jnp.minimum(jax.nn.softplus(step_input + step_bias), step_limit)
    log_step = step * -jnp.exp(log_decay_rate)
    step_blocks = step.reshape(block_count, BLOCK, groups, per_group)
    cumul = jnp.cumsum(log_step.reshape(block_count, BLOCK, groups, per_group), axis=1)
    x_blocks = inner_conv.reshape(block_count, BLOCK, groups, per_group, HEAD_DIM)
    b_blocks = maps_conv[:, 0].reshape(block_count, BLOCK, groups, STATE)
    c_blocks = maps_conv[:, 1].reshape(block_count, BLOCK, groups, STATE)
    scores = jnp.einsum("ctgn,csgn->cgts", c_blocks, b_blocks, preferred_element_type=jnp.float32)
    cumul_t = cumul.transpose(0, 2, 3, 1)
    gap = cumul_t[..., :, None] - cumul_t[..., None, :]
    row_ids = lax.broadcasted_iota(jnp.int32, (BLOCK, BLOCK), 0)
    col_ids = lax.broadcasted_iota(jnp.int32, (BLOCK, BLOCK), 1)
    decay = jnp.exp(jnp.where(row_ids >= col_ids, gap, -jnp.inf))
    mixing = (scores[:, :, None] * decay * step_blocks.transpose(0, 2, 3, 1)[..., None, :]).astype(
        jnp.bfloat16
    )
    y_local = jnp.einsum("cgjts,csgjp->ctgjp", mixing, x_blocks, preferred_element_type=jnp.float32)
    weighted = (
        (jnp.exp(cumul[:, -1:] - cumul) * step_blocks)[..., None] * b_blocks[:, :, :, None, :]
    ).astype(jnp.bfloat16)
    block_states = jnp.einsum(
        "csgjp,csgjn->cgjpn", x_blocks, weighted, preferred_element_type=jnp.float32
    )
    block_decay = cumul[:, -1]
    running = jnp.zeros((groups, per_group, HEAD_DIM, STATE), jnp.float32)
    local_in = []
    for block_index in range(block_count):
        local_in.append(running)
        running = (
            jnp.exp(block_decay[block_index])[..., None, None] * running + block_states[block_index]
        )
    slab_decay = jnp.sum(block_decay, axis=0)
    state_shape = (groups * per_group, HEAD_DIM, STATE)
    decay_tile = jnp.broadcast_to(
        slab_decay.reshape(groups * per_group, 1, 1), (groups * per_group, 8, STATE)
    )
    entering = state_scan(running.reshape(state_shape), decay_tile).reshape(running.shape)
    leading = jnp.cumsum(block_decay, axis=0) - block_decay
    state_in = (
        jnp.exp(leading)[..., None, None] * entering[None] + jnp.stack(local_in, axis=0)
    ).astype(jnp.bfloat16)
    width = per_group * HEAD_DIM
    y_pre = lax.optimization_barrier(
        y_local + skip_gain.reshape(groups, per_group)[:, :, None] * x_blocks
    )
    chunk_count = 1
    per_chunk = block_count // chunk_count
    outs = []
    for chunk in range(chunk_count):
        part = slice(chunk * per_chunk, (chunk + 1) * per_chunk)
        rows = per_chunk * BLOCK
        y_carry = jnp.exp(cumul[part])[..., None] * jnp.einsum(
            "ctgn,cgjpn->ctgjp", c_blocks[part], state_in[part], preferred_element_type=jnp.float32
        )
        y_all = y_pre[part] + y_carry
        gate_rows = gate_input[chunk * rows : (chunk + 1) * rows]
        gated = y_all.reshape(rows, groups, width) * jax.nn.silu(
            gate_rows.reshape(rows, groups, width).astype(jnp.float32)
        )
        square_mean = jnp.mean(gated * gated, axis=-1, keepdims=True)
        normed = (
            (gated * lax.rsqrt(square_mean + epsilon) * norm_gain.reshape(groups, width))
            .astype(jnp.bfloat16)
            .reshape(rows, head_count * HEAD_DIM)
        )
        shares = lax.psum_scatter(
            lax.dot_general(
                out_weight, normed, (((0,), (1,)), ((), ())), preferred_element_type=jnp.float32
            ).astype(jnp.bfloat16),
            "chan",
            scatter_dimension=0,
            tiled=True,
        )
        outs.append(shares.T)
    return jnp.concatenate(outs, axis=0)


def solution(mesh):
    return jax.shard_map(
        local,
        mesh=mesh,
        in_specs=(
            P("seq", "chan"),
            P("seq", None, "chan", None),
            P("seq", "chan"),
            P("seq", "chan"),
            P("chan"),
            P("chan"),
            P("chan"),
            P(None, "chan"),
            P(None, None, "chan", None),
            P("chan"),
            P("chan", None),
        ),
        out_specs=P("seq", "chan"),
        check_vma=False,
    )
```

```python
import functools

import jax
import jax.numpy as jnp
from jax import lax
from jax.experimental import pallas as pl
from jax.experimental.pallas import tpu as pltpu
from jax.sharding import PartitionSpec as P

HEADS = 128
HEAD_DIM = 64
STATE = 128
NGROUPS = 8
BLOCK = 256


step_limit = 0.5
epsilon = 1e-05


def passed_along(x, axis, by):
    count = lax.axis_size(axis)
    pairs = [(i, i + by) for i in range(count) if 0 <= i + by < count]
    return lax.ppermute(x, axis, pairs)


def conv_silu(padded, kernel, length):
    acc = jnp.zeros((length,) + padded.shape[1:], jnp.float32)
    for offset in range(kernel.shape[0]):
        acc = acc + kernel[offset] * padded[offset : offset + length].astype(jnp.float32)
    return jax.nn.silu(acc).astype(jnp.bfloat16)


MESH = pl.DeviceIdType.MESH


def scan_distances(count):
    distances = []
    distance = 1
    while distance < count:
        distances.append(distance)
        distance *= 2
    return distances


def state_scan_kernel(count, state_ref, decay_ref, out_ref, cur_d, send_s, send_d, recv_s, recv_d, ssem, rsem):
    me = lax.axis_index("seq")
    chan = lax.axis_index("chan")
    distances = scan_distances(count)
    barrier = pltpu.get_barrier_semaphore()
    peers = jnp.int32(0)
    for distance in distances:
        for target in (me + distance, me - distance):
            valid = jnp.logical_and(target >= 0, target < count)

            @pl.when(valid)
            def _():
                pl.semaphore_signal(barrier, 1, device_id=(target, chan), device_id_type=MESH)

            peers = peers + valid.astype(jnp.int32)
    pl.semaphore_wait(barrier, peers)

    rounds = [[1, 2]] + [[distance] for distance in distances[1:]]
    outgoing = []
    slot = 0
    for index, round_distances in enumerate(rounds):
        if index == 0:
            send_s[index] = state_ref[...].astype(jnp.bfloat16)
            send_d[index] = decay_ref[...]
        else:
            send_s[index] = out_ref[...].astype(jnp.bfloat16)
            send_d[index] = cur_d[...]
        for distance in round_distances:
            pair = []
            for part, (src, dst) in enumerate(((send_s, recv_s), (send_d, recv_d))):
                pair.append(
                    lambda target, src=src, dst=dst, part=part, index=index, slot=slot: (
                        pltpu.make_async_remote_copy(
                            src_ref=src.at[index],
                            dst_ref=dst.at[slot],
                            send_sem=ssem.at[slot, part],
                            recv_sem=rsem.at[slot, part],
                            device_id=(target, chan),
                            device_id_type=MESH,
                        )
                    )
                )
            sends = me + distance < count

            @pl.when(sends)
            def _():
                for make in pair:
                    make(me + distance).start()

            outgoing.append((sends, pair, distance, slot))
            slot += 1

        for sends, pair, distance, at in outgoing[-len(round_distances):]:
            receives = me - distance >= 0
            first = index == 0 and distance == 1

            @pl.when(receives)
            def _():
                for make in pair:
                    make(me - distance).wait_recv()
                if first:
                    out_ref[...] = recv_s[at].astype(jnp.float32)
                    cur_d[...] = recv_d[at]
                else:
                    scale = jnp.exp(cur_d[:, 0:1, :])
                    out_ref[...] = scale * recv_s[at].astype(jnp.float32) + out_ref[...]
                    cur_d[...] = recv_d[at] + cur_d[...]

            if first:

                @pl.when(jnp.logical_not(receives))
                def _():
                    out_ref[...] = jnp.zeros_like(out_ref)
                    cur_d[...] = jnp.zeros_like(cur_d)

    for sends, pair, distance, at in outgoing:

        @pl.when(sends)
        def _():
            for make in pair:
                make(me + distance).wait_send()


def state_scan(state, decay):
    count = lax.axis_size("seq")
    rounds = len(scan_distances(count))
    slots = rounds + 1
    return pl.pallas_call(
        functools.partial(state_scan_kernel, count),
        out_shape=jax.ShapeDtypeStruct(state.shape, jnp.float32),
        in_specs=[pl.BlockSpec(memory_space=pltpu.VMEM)] * 2,
        out_specs=pl.BlockSpec(memory_space=pltpu.VMEM),
        scratch_shapes=[
            pltpu.VMEM(decay.shape, jnp.float32),
            pltpu.VMEM((rounds,) + state.shape, jnp.bfloat16),
            pltpu.VMEM((rounds,) + decay.shape, jnp.float32),
            pltpu.VMEM((slots,) + state.shape, jnp.bfloat16),
            pltpu.VMEM((slots,) + decay.shape, jnp.float32),
            pltpu.SemaphoreType.DMA((slots, 2)),
            pltpu.SemaphoreType.DMA((slots, 2)),
        ],
        compiler_params=pltpu.CompilerParams(collective_id=0, has_side_effects=True),
        name="state_scan",
    )(state, decay)


def local(
    inner_input,
    state_maps,
    gate_input,
    step_input,
    log_decay_rate,
    step_bias,
    skip_gain,
    conv_kernel,
    map_kernel,
    norm_gain,
    out_weight,
):
    row_count = inner_input.shape[0]
    kernel_remainder = conv_kernel.shape[0] - 1
    groups = state_maps.shape[2]
    per_group = HEADS // NGROUPS
    head_count = groups * per_group
    block_count = row_count // BLOCK
    tail_inner, tail_maps = passed_along(
        (inner_input[row_count - kernel_remainder :], state_maps[row_count - kernel_remainder :]),
        "seq",
        1,
    )
    inner_conv = conv_silu(
        jnp.concatenate((tail_inner, inner_input), axis=0), conv_kernel, row_count
    )
    maps_conv = conv_silu(jnp.concatenate((tail_maps, state_maps), axis=0), map_kernel, row_count)
    step = jnp.minimum(jax.nn.softplus(step_input + step_bias), step_limit)
    log_step = step * -jnp.exp(log_decay_rate)
    step_blocks = step.reshape(block_count, BLOCK, groups, per_group)
    cumul = jnp.cumsum(log_step.reshape(block_count, BLOCK, groups, per_group), axis=1)
    x_blocks = inner_conv.reshape(block_count, BLOCK, groups, per_group, HEAD_DIM)
    b_blocks = maps_conv[:, 0].reshape(block_count, BLOCK, groups, STATE)
    c_blocks = maps_conv[:, 1].reshape(block_count, BLOCK, groups, STATE)
    scores = jnp.einsum("ctgn,csgn->cgts", c_blocks, b_blocks, preferred_element_type=jnp.float32)
    cumul_t = cumul.transpose(0, 2, 3, 1)
    gap = cumul_t[..., :, None] - cumul_t[..., None, :]
    row_ids = lax.broadcasted_iota(jnp.int32, (BLOCK, BLOCK), 0)
    col_ids = lax.broadcasted_iota(jnp.int32, (BLOCK, BLOCK), 1)
    decay = jnp.exp(jnp.where(row_ids >= col_ids, gap, -jnp.inf))
    mixing = (scores[:, :, None] * decay * step_blocks.transpose(0, 2, 3, 1)[..., None, :]).astype(
        jnp.bfloat16
    )
    y_local = jnp.einsum("cgjts,csgjp->ctgjp", mixing, x_blocks, preferred_element_type=jnp.float32)
    weighted = (
        (jnp.exp(cumul[:, -1:] - cumul) * step_blocks)[..., None] * b_blocks[:, :, :, None, :]
    ).astype(jnp.bfloat16)
    block_states = jnp.einsum(
        "csgjp,csgjn->cgjpn", x_blocks, weighted, preferred_element_type=jnp.float32
    )
    block_decay = cumul[:, -1]
    running = jnp.zeros((groups, per_group, HEAD_DIM, STATE), jnp.float32)
    local_in = []
    for block_index in range(block_count):
        local_in.append(running)
        running = (
            jnp.exp(block_decay[block_index])[..., None, None] * running + block_states[block_index]
        )
    slab_decay = jnp.sum(block_decay, axis=0)
    state_shape = (groups * per_group, HEAD_DIM, STATE)
    decay_tile = jnp.broadcast_to(
        slab_decay.reshape(groups * per_group, 1, 1), (groups * per_group, 8, STATE)
    )
    entering = state_scan(running.reshape(state_shape), decay_tile).reshape(running.shape)
    leading = jnp.cumsum(block_decay, axis=0) - block_decay
    state_in = (
        jnp.exp(leading)[..., None, None] * entering[None] + jnp.stack(local_in, axis=0)
    ).astype(jnp.bfloat16)
    width = per_group * HEAD_DIM
    y_pre = lax.optimization_barrier(
        y_local + skip_gain.reshape(groups, per_group)[:, :, None] * x_blocks
    )
    chunk_count = 1
    per_chunk = block_count // chunk_count
    outs = []
    for chunk in range(chunk_count):
        part = slice(chunk * per_chunk, (chunk + 1) * per_chunk)
        rows = per_chunk * BLOCK
        y_carry = jnp.exp(cumul[part])[..., None] * jnp.einsum(
            "ctgn,cgjpn->ctgjp", c_blocks[part], state_in[part], preferred_element_type=jnp.float32
        )
        y_all = y_pre[part] + y_carry
        gate_rows = gate_input[chunk * rows : (chunk + 1) * rows]
        gated = y_all.reshape(rows, groups, width) * jax.nn.silu(
            gate_rows.reshape(rows, groups, width).astype(jnp.float32)
        )
        square_mean = jnp.mean(gated * gated, axis=-1, keepdims=True)
        normed = (
            (gated * lax.rsqrt(square_mean + epsilon) * norm_gain.reshape(groups, width))
            .astype(jnp.bfloat16)
            .reshape(rows, head_count * HEAD_DIM)
        )
        shares = lax.psum_scatter(
            lax.dot_general(
                out_weight, normed, (((0,), (1,)), ((), ())), preferred_element_type=jnp.float32
            ).astype(jnp.bfloat16),
            "chan",
            scatter_dimension=0,
            tiled=True,
        )
        outs.append(shares.T)
    return jnp.concatenate(outs, axis=0)


def solution(mesh):
    return jax.shard_map(
        local,
        mesh=mesh,
        in_specs=(
            P("seq", "chan"),
            P("seq", None, "chan", None),
            P("seq", "chan"),
            P("seq", "chan"),
            P("chan"),
            P("chan"),
            P("chan"),
            P(None, "chan"),
            P(None, None, "chan", None),
            P("chan"),
            P("chan", None),
        ),
        out_specs=P("seq", "chan"),
        check_vma=False,
    )
```

```python
import functools

import jax
import jax.numpy as jnp
from jax import lax
from jax.experimental import pallas as pl
from jax.experimental.pallas import tpu as pltpu
from jax.sharding import PartitionSpec as P

HEADS = 128
HEAD_DIM = 64
STATE = 128
NGROUPS = 8
BLOCK = 256


step_limit = 0.5
epsilon = 1e-05


def passed_along(x, axis, by):
    count = lax.axis_size(axis)
    pairs = [(i, i + by) for i in range(count) if 0 <= i + by < count]
    return lax.ppermute(x, axis, pairs)


def conv_silu(padded, kernel, length):
    acc = jnp.zeros((length,) + padded.shape[1:], jnp.float32)
    for offset in range(kernel.shape[0]):
        acc = acc + kernel[offset] * padded[offset : offset + length].astype(jnp.float32)
    return jax.nn.silu(acc).astype(jnp.bfloat16)


MESH = pl.DeviceIdType.MESH


def scan_distances(count):
    distances = []
    distance = 1
    while distance < count:
        distances.append(distance)
        distance *= 2
    return distances


def scale_add(out, decay, incoming, base):
    for head in range(out.shape[0]):
        out[head] = jnp.exp(decay[head : head + 1, :]) * incoming[head] + base[head]


def state_scan_kernel(
    count, state_ref, decay_ref, out_ref,
    own_s, own_d, pair_s, pair_d, cur_s, cur_d, send_s, send_d, recv_s, recv_d, back_s, ssem, rsem,
):
    me = lax.axis_index("seq")
    chan = lax.axis_index("chan")
    core = me % 2
    chip = me // 2
    chips = count // 2
    half = state_ref.shape[0] // 2
    partner = me + 1 - 2 * core
    distances = scan_distances(chips)

    barrier = pltpu.get_barrier_semaphore()
    pl.semaphore_signal(barrier, 1, device_id=(partner, chan), device_id_type=MESH)
    peers = jnp.int32(1)
    for distance in distances:
        for target in (chip + distance, chip - distance):
            valid = jnp.logical_and(target >= 0, target < chips)

            @pl.when(valid)
            def _(target=target):
                pl.semaphore_signal(
                    barrier, 1, device_id=(2 * target + core, chan), device_id_type=MESH
                )

            peers = peers + valid.astype(jnp.int32)
    pl.semaphore_wait(barrier, peers)

    def remote(src, dst, slot, part, target):
        return pltpu.make_async_remote_copy(
            src_ref=src, dst_ref=dst, send_sem=ssem.at[slot, part], recv_sem=rsem.at[slot, part],
            device_id=(target, chan), device_id_type=MESH,
        )

    own_s[...] = state_ref[...].astype(jnp.bfloat16)
    own_d[...] = decay_ref[...]
    first = [
        lambda t: remote(own_s, pair_s, 0, 0, t),
        lambda t: remote(own_s.at[0:half], pair_s.at[0:half], 0, 0, t),
    ]
    first_d = lambda t: remote(own_d, pair_d, 0, 1, t)

    @pl.when(core == 0)
    def _():
        first[0](partner).start()
        first_d(partner).start()
        first[1](partner).wait_recv()
        first_d(partner).wait_recv()
        cur_d[...] = own_d[0:half] + pair_d[0:half]
        scale_add(cur_s, pair_d[0:half], state_ref.at[0:half], pair_s[0:half].astype(jnp.float32))

    @pl.when(core == 1)
    def _():
        first[1](partner).start()
        first_d(partner).start()
        first[0](partner).wait_recv()
        first_d(partner).wait_recv()
        cur_d[...] = own_d[half:] + pair_d[half:]
        scale_add(
            cur_s, own_d[half:], pair_s[half:].astype(jnp.float32), state_ref.at[half:]
        )

    rounds = [[1, 2]] + [[distance] for distance in distances[1:]]
    outgoing = []
    slot = 0
    for index, round_distances in enumerate(rounds):
        send_s[index] = cur_s[...].astype(jnp.bfloat16)
        send_d[index] = cur_d[...]
        start = slot
        for distance in round_distances:
            makers = (
                lambda t, index=index, slot=slot: remote(send_s.at[index], recv_s.at[slot], slot + 1, 0, t),
                lambda t, index=index, slot=slot: remote(send_d.at[index], recv_d.at[slot], slot + 1, 1, t),
            )
            sends = chip + distance < chips

            @pl.when(sends)
            def _(makers=makers, distance=distance):
                for make in makers:
                    make(2 * (chip + distance) + core).start()

            outgoing.append((sends, makers, distance))
            slot += 1
        for at in range(start, slot):
            sends, makers, distance = outgoing[at]
            receives = chip - distance >= 0
            opening = index == 0 and distance == 1

            @pl.when(receives)
            def _(makers=makers, distance=distance, at=at, opening=opening):
                for make in makers:
                    make(2 * (chip - distance) + core).wait_recv()
                if opening:
                    cur_s[...] = recv_s[at].astype(jnp.float32)
                    cur_d[...] = recv_d[at]
                else:
                    scale_add(cur_s, cur_d[...], recv_s.at[at], cur_s)
                    cur_d[...] = recv_d[at] + cur_d[...]

            if opening:

                @pl.when(jnp.logical_not(receives))
                def _():
                    cur_s[...] = jnp.zeros_like(cur_s)
                    cur_d[...] = jnp.zeros_like(cur_d)

    last = len(outgoing) + 1
    own_half = send_s.at[len(rounds)]
    own_half[...] = cur_s[...].astype(jnp.bfloat16)
    final = remote(own_half, back_s, last, 0, partner)
    final.start()
    final.wait_recv()

    @pl.when(core == 0)
    def _():
        out_ref[0:half] = cur_s[...]
        out_ref[half:] = back_s[...].astype(jnp.float32)

    @pl.when(core == 1)
    def _():
        out_ref[0:half] = back_s[...].astype(jnp.float32)
        out_ref[half:] = cur_s[...]
        scale_add(out_ref, pair_d[...], out_ref, pair_s)

    final.wait_send()

    @pl.when(core == 0)
    def _():
        first[0](partner).wait_send()
        first_d(partner).wait_send()

    @pl.when(core == 1)
    def _():
        first[1](partner).wait_send()
        first_d(partner).wait_send()

    for sends, makers, distance in outgoing:

        @pl.when(sends)
        def _(makers=makers, distance=distance):
            for make in makers:
                make(2 * (chip + distance) + core).wait_send()


def state_scan(state, decay):
    count = lax.axis_size("seq")
    rounds = len(scan_distances(count // 2))
    heads = state.shape[0]
    half_shape = (heads // 2,) + state.shape[1:]
    half_decay = (heads // 2,) + decay.shape[1:]
    return pl.pallas_call(
        functools.partial(state_scan_kernel, count),
        out_shape=jax.ShapeDtypeStruct(state.shape, jnp.float32),
        in_specs=[pl.BlockSpec(memory_space=pltpu.VMEM)] * 2,
        out_specs=pl.BlockSpec(memory_space=pltpu.VMEM),
        scratch_shapes=[
            pltpu.VMEM(state.shape, jnp.bfloat16),
            pltpu.VMEM(decay.shape, jnp.float32),
            pltpu.VMEM(state.shape, jnp.bfloat16),
            pltpu.VMEM(decay.shape, jnp.float32),
            pltpu.VMEM(half_shape, jnp.float32),
            pltpu.VMEM(half_decay, jnp.float32),
            pltpu.VMEM((rounds + 1,) + half_shape, jnp.bfloat16),
            pltpu.VMEM((rounds,) + half_decay, jnp.float32),
            pltpu.VMEM((rounds + 1,) + half_shape, jnp.bfloat16),
            pltpu.VMEM((rounds + 1,) + half_decay, jnp.float32),
            pltpu.VMEM(half_shape, jnp.bfloat16),
            pltpu.SemaphoreType.DMA((rounds + 3, 2)),
            pltpu.SemaphoreType.DMA((rounds + 3, 2)),
        ],
        compiler_params=pltpu.CompilerParams(collective_id=0, has_side_effects=True),
        name="state_scan",
    )(state, decay)

def local(
    inner_input,
    state_maps,
    gate_input,
    step_input,
    log_decay_rate,
    step_bias,
    skip_gain,
    conv_kernel,
    map_kernel,
    norm_gain,
    out_weight,
):
    row_count = inner_input.shape[0]
    kernel_remainder = conv_kernel.shape[0] - 1
    groups = state_maps.shape[2]
    per_group = HEADS // NGROUPS
    head_count = groups * per_group
    block_count = row_count // BLOCK
    tail_inner, tail_maps = passed_along(
        (inner_input[row_count - kernel_remainder :], state_maps[row_count - kernel_remainder :]),
        "seq",
        1,
    )
    inner_conv = conv_silu(
        jnp.concatenate((tail_inner, inner_input), axis=0), conv_kernel, row_count
    )
    maps_conv = conv_silu(jnp.concatenate((tail_maps, state_maps), axis=0), map_kernel, row_count)
    step = jnp.minimum(jax.nn.softplus(step_input + step_bias), step_limit)
    log_step = step * -jnp.exp(log_decay_rate)
    step_blocks = step.reshape(block_count, BLOCK, groups, per_group)
    cumul = jnp.cumsum(log_step.reshape(block_count, BLOCK, groups, per_group), axis=1)
    x_blocks = inner_conv.reshape(block_count, BLOCK, groups, per_group, HEAD_DIM)
    b_blocks = maps_conv[:, 0].reshape(block_count, BLOCK, groups, STATE)
    c_blocks = maps_conv[:, 1].reshape(block_count, BLOCK, groups, STATE)
    scores = jnp.einsum("ctgn,csgn->cgts", c_blocks, b_blocks, preferred_element_type=jnp.float32)
    cumul_t = cumul.transpose(0, 2, 3, 1)
    gap = cumul_t[..., :, None] - cumul_t[..., None, :]
    row_ids = lax.broadcasted_iota(jnp.int32, (BLOCK, BLOCK), 0)
    col_ids = lax.broadcasted_iota(jnp.int32, (BLOCK, BLOCK), 1)
    decay = jnp.exp(jnp.where(row_ids >= col_ids, gap, -jnp.inf))
    mixing = (scores[:, :, None] * decay * step_blocks.transpose(0, 2, 3, 1)[..., None, :]).astype(
        jnp.bfloat16
    )
    y_local = jnp.einsum("cgjts,csgjp->ctgjp", mixing, x_blocks, preferred_element_type=jnp.float32)
    weighted = (
        (jnp.exp(cumul[:, -1:] - cumul) * step_blocks)[..., None] * b_blocks[:, :, :, None, :]
    ).astype(jnp.bfloat16)
    block_states = jnp.einsum(
        "csgjp,csgjn->cgjpn", x_blocks, weighted, preferred_element_type=jnp.float32
    )
    block_decay = cumul[:, -1]
    running = jnp.zeros((groups, per_group, HEAD_DIM, STATE), jnp.float32)
    local_in = []
    for block_index in range(block_count):
        local_in.append(running)
        running = (
            jnp.exp(block_decay[block_index])[..., None, None] * running + block_states[block_index]
        )
    slab_decay = jnp.sum(block_decay, axis=0)
    state_shape = (groups * per_group, HEAD_DIM, STATE)
    decay_tile = jnp.broadcast_to(slab_decay.reshape(groups * per_group, 1), (groups * per_group, STATE))
    entering = state_scan(running.reshape(state_shape), decay_tile).reshape(running.shape)
    leading = jnp.cumsum(block_decay, axis=0) - block_decay
    state_in = (
        jnp.exp(leading)[..., None, None] * entering[None] + jnp.stack(local_in, axis=0)
    ).astype(jnp.bfloat16)
    width = per_group * HEAD_DIM
    y_pre = lax.optimization_barrier(
        y_local + skip_gain.reshape(groups, per_group)[:, :, None] * x_blocks
    )
    chunk_count = 1
    per_chunk = block_count // chunk_count
    outs = []
    for chunk in range(chunk_count):
        part = slice(chunk * per_chunk, (chunk + 1) * per_chunk)
        rows = per_chunk * BLOCK
        y_carry = jnp.exp(cumul[part])[..., None] * jnp.einsum(
            "ctgn,cgjpn->ctgjp", c_blocks[part], state_in[part], preferred_element_type=jnp.float32
        )
        y_all = y_pre[part] + y_carry
        gate_rows = gate_input[chunk * rows : (chunk + 1) * rows]
        gated = y_all.reshape(rows, groups, width) * jax.nn.silu(
            gate_rows.reshape(rows, groups, width).astype(jnp.float32)
        )
        square_mean = jnp.mean(gated * gated, axis=-1, keepdims=True)
        normed = (
            (gated * lax.rsqrt(square_mean + epsilon) * norm_gain.reshape(groups, width))
            .astype(jnp.bfloat16)
            .reshape(rows, head_count * HEAD_DIM)
        )
        shares = lax.psum_scatter(
            lax.dot_general(
                out_weight, normed, (((0,), (1,)), ((), ())), preferred_element_type=jnp.float32
            ).astype(jnp.bfloat16),
            "chan",
            scatter_dimension=0,
            tiled=True,
        )
        outs.append(shares.T)
    return jnp.concatenate(outs, axis=0)


def solution(mesh):
    return jax.shard_map(
        local,
        mesh=mesh,
        in_specs=(
            P("seq", "chan"),
            P("seq", None, "chan", None),
            P("seq", "chan"),
            P("seq", "chan"),
            P("chan"),
            P("chan"),
            P("chan"),
            P(None, "chan"),
            P(None, None, "chan", None),
            P("chan"),
            P("chan", None),
        ),
        out_specs=P("seq", "chan"),
        check_vma=False,
    )
```

```python
import functools

import jax
import jax.numpy as jnp
from jax import lax
from jax.experimental import pallas as pl
from jax.experimental.pallas import tpu as pltpu
from jax.sharding import PartitionSpec as P

HEADS = 128
HEAD_DIM = 64
STATE = 128
NGROUPS = 8
BLOCK = 256


step_limit = 0.5
epsilon = 1e-05


def passed_along(x, axis, by):
    count = lax.axis_size(axis)
    pairs = [(i, i + by) for i in range(count) if 0 <= i + by < count]
    return lax.ppermute(x, axis, pairs)


def conv_silu(padded, kernel, length):
    acc = jnp.zeros((length,) + padded.shape[1:], jnp.float32)
    for offset in range(kernel.shape[0]):
        acc = acc + kernel[offset] * padded[offset : offset + length].astype(jnp.float32)
    return jax.nn.silu(acc).astype(jnp.bfloat16)


MESH = pl.DeviceIdType.MESH


def scan_distances(count):
    distances = []
    distance = 1
    while distance < count:
        distances.append(distance)
        distance *= 2
    return distances


def scale_add(out, decay, incoming, base):
    for head in range(out.shape[0]):
        out[head] = jnp.exp(decay[head : head + 1, :]) * incoming[head] + base[head]


def state_scan_kernel(
    count, state_ref, decay_ref, out_ref,
    own_s, own_d, pair_s, pair_d, cur_s, cur_d, send_s, send_d, recv_s, recv_d, back_s, ssem, rsem,
):
    me = lax.axis_index("seq")
    chan = lax.axis_index("chan")
    core = me % 2
    chip = me // 2
    chips = count // 2
    half = state_ref.shape[0] // 2
    partner = me + 1 - 2 * core
    distances = scan_distances(chips)

    barrier = pltpu.get_barrier_semaphore()
    pl.semaphore_signal(barrier, 1, device_id=(partner, chan), device_id_type=MESH)
    peers = jnp.int32(1)
    for distance in distances:
        for target in (chip + distance, chip - distance):
            valid = jnp.logical_and(target >= 0, target < chips)

            @pl.when(valid)
            def _(target=target):
                pl.semaphore_signal(
                    barrier, 1, device_id=(2 * target + core, chan), device_id_type=MESH
                )

            peers = peers + valid.astype(jnp.int32)
    pl.semaphore_wait(barrier, peers)

    def remote(src, dst, slot, part, target):
        return pltpu.make_async_remote_copy(
            src_ref=src, dst_ref=dst, send_sem=ssem.at[slot, part], recv_sem=rsem.at[slot, part],
            device_id=(target, chan), device_id_type=MESH,
        )

    own_s[...] = state_ref[...].astype(jnp.bfloat16)
    own_d[...] = decay_ref[...]
    first = [
        lambda t: remote(own_s, pair_s, 0, 0, t),
        lambda t: remote(own_s.at[0:half], pair_s.at[0:half], 0, 0, t),
    ]
    first_d = lambda t: remote(own_d, pair_d, 0, 1, t)

    @pl.when(core == 0)
    def _():
        first[0](partner).start()
        first_d(partner).start()
        first[1](partner).wait_recv()
        first_d(partner).wait_recv()
        cur_d[...] = own_d[0:half] + pair_d[0:half]
        scale_add(cur_s, pair_d[0:half], state_ref.at[0:half], pair_s[0:half].astype(jnp.float32))

    @pl.when(core == 1)
    def _():
        first[1](partner).start()
        first_d(partner).start()
        first[0](partner).wait_recv()
        first_d(partner).wait_recv()
        cur_d[...] = own_d[half:] + pair_d[half:]
        scale_add(
            cur_s, own_d[half:], pair_s[half:].astype(jnp.float32), state_ref.at[half:]
        )

    rounds = [[1, 2]] + [[distance] for distance in distances[1:]]
    outgoing = []
    slot = 0
    for index, round_distances in enumerate(rounds):
        send_s[index] = cur_s[...].astype(jnp.bfloat16)
        send_d[index] = cur_d[...]
        start = slot
        for distance in round_distances:
            makers = (
                lambda t, index=index, slot=slot: remote(send_s.at[index], recv_s.at[slot], slot + 1, 0, t),
                lambda t, index=index, slot=slot: remote(send_d.at[index], recv_d.at[slot], slot + 1, 1, t),
            )
            sends = chip + distance < chips

            @pl.when(sends)
            def _(makers=makers, distance=distance):
                for make in makers:
                    make(2 * (chip + distance) + core).start()

            outgoing.append((sends, makers, distance))
            slot += 1
        for at in range(start, slot):
            sends, makers, distance = outgoing[at]
            receives = chip - distance >= 0
            opening = index == 0 and distance == 1

            @pl.when(receives)
            def _(makers=makers, distance=distance, at=at, opening=opening):
                for make in makers:
                    make(2 * (chip - distance) + core).wait_recv()
                if opening:
                    cur_s[...] = recv_s[at].astype(jnp.float32)
                    cur_d[...] = recv_d[at]
                else:
                    scale_add(cur_s, cur_d[...], recv_s.at[at], cur_s)
                    cur_d[...] = recv_d[at] + cur_d[...]

            if opening:

                @pl.when(jnp.logical_not(receives))
                def _():
                    cur_s[...] = jnp.zeros_like(cur_s)
                    cur_d[...] = jnp.zeros_like(cur_d)

    last = len(outgoing) + 1
    own_half = send_s.at[len(rounds)]
    own_half[...] = cur_s[...].astype(jnp.bfloat16)
    final = remote(own_half, back_s, last, 0, partner)
    final.start()
    final.wait_recv()

    @pl.when(core == 0)
    def _():
        out_ref[0:half] = cur_s[...]
        out_ref[half:] = back_s[...].astype(jnp.float32)

    @pl.when(core == 1)
    def _():
        out_ref[0:half] = back_s[...].astype(jnp.float32)
        out_ref[half:] = cur_s[...]
        scale_add(out_ref, pair_d[...], out_ref, pair_s)

    final.wait_send()

    @pl.when(core == 0)
    def _():
        first[0](partner).wait_send()
        first_d(partner).wait_send()

    @pl.when(core == 1)
    def _():
        first[1](partner).wait_send()
        first_d(partner).wait_send()

    for sends, makers, distance in outgoing:

        @pl.when(sends)
        def _(makers=makers, distance=distance):
            for make in makers:
                make(2 * (chip + distance) + core).wait_send()


def state_scan(state, decay):
    count = lax.axis_size("seq")
    rounds = len(scan_distances(count // 2))
    heads = state.shape[0]
    half_shape = (heads // 2,) + state.shape[1:]
    half_decay = (heads // 2,) + decay.shape[1:]
    return pl.pallas_call(
        functools.partial(state_scan_kernel, count),
        out_shape=jax.ShapeDtypeStruct(state.shape, jnp.float32),
        in_specs=[pl.BlockSpec(memory_space=pltpu.VMEM)] * 2,
        out_specs=pl.BlockSpec(memory_space=pltpu.VMEM),
        scratch_shapes=[
            pltpu.VMEM(state.shape, jnp.bfloat16),
            pltpu.VMEM(decay.shape, jnp.float32),
            pltpu.VMEM(state.shape, jnp.bfloat16),
            pltpu.VMEM(decay.shape, jnp.float32),
            pltpu.VMEM(half_shape, jnp.float32),
            pltpu.VMEM(half_decay, jnp.float32),
            pltpu.VMEM((rounds + 1,) + half_shape, jnp.bfloat16),
            pltpu.VMEM((rounds,) + half_decay, jnp.float32),
            pltpu.VMEM((rounds + 1,) + half_shape, jnp.bfloat16),
            pltpu.VMEM((rounds + 1,) + half_decay, jnp.float32),
            pltpu.VMEM(half_shape, jnp.bfloat16),
            pltpu.SemaphoreType.DMA((rounds + 3, 2)),
            pltpu.SemaphoreType.DMA((rounds + 3, 2)),
        ],
        compiler_params=pltpu.CompilerParams(collective_id=0, has_side_effects=True),
        name="state_scan",
    )(state, decay)

def ring_kernel(count, pieces, normed_ref, weight_ref, out_ref, send_buf, recv_buf, ssem, rsem):
    me = lax.axis_index("chan")
    seq = lax.axis_index("seq")
    width = out_ref.shape[1]
    rows = normed_ref.shape[0] // (2 * pieces)
    targets = (lax.rem(me + 1, count), lax.rem(me + count - 1, count))

    barrier = pltpu.get_barrier_semaphore()
    for target in targets:
        pl.semaphore_signal(barrier, 1, device_id=(seq, target), device_id_type=MESH)
    pl.semaphore_wait(barrier, 2)

    def copy(direction, step, piece):
        return pltpu.make_async_remote_copy(
            src_ref=send_buf.at[direction, step, piece],
            dst_ref=recv_buf.at[direction, step, piece],
            send_sem=ssem.at[direction, step, piece],
            recv_sem=rsem.at[direction, step, piece],
            device_id=(seq, targets[direction]),
            device_id_type=MESH,
        )

    def block(direction, step):
        if direction == 0:
            return lax.rem(me + 2 * count - 1 - step, count)
        return lax.rem(me + 1 + step, count)

    def partial(direction, step, piece):
        start = (direction * pieces + piece) * rows
        column = pl.multiple_of(block(direction, step) * width, width)
        return jnp.dot(
            normed_ref[pl.ds(start, rows), :],
            weight_ref[:, pl.ds(column, width)],
            preferred_element_type=jnp.float32,
        )

    def run_step(step, first, last):
        for piece in range(pieces):
            for direction in range(2):
                value = partial(direction, step, piece)
                if not first:
                    copy(direction, step - 1, piece).wait_recv()
                    value = value + recv_buf[direction, step - 1, piece].astype(jnp.float32)
                if last:
                    start = (direction * pieces + piece) * rows
                    out_ref[pl.ds(start, rows), :] = value.astype(out_ref.dtype)
                else:
                    send_buf[direction, step, piece] = value.astype(send_buf.dtype)
                    copy(direction, step, piece).start()

    run_step(0, True, False)

    def middle(step, carry):
        run_step(step, False, False)
        return carry

    lax.fori_loop(1, count - 1, middle, 0)
    run_step(count - 1, False, True)

    def drain(step, carry):
        for piece in range(pieces):
            for direction in range(2):
                copy(direction, step, piece).wait_send()
        return carry

    lax.fori_loop(0, count - 1, drain, 0)


def ring_projection(normed, weight):
    count = lax.axis_size("chan")
    pieces = 4
    tokens = normed.shape[0]
    width = weight.shape[1] // count
    rows = tokens // (2 * pieces)
    buffers = (2, count - 1, pieces, rows, width)
    return pl.pallas_call(
        functools.partial(ring_kernel, count, pieces),
        out_shape=jax.ShapeDtypeStruct((tokens, width), jnp.bfloat16),
        in_specs=[pl.BlockSpec(memory_space=pltpu.VMEM)] * 2,
        out_specs=pl.BlockSpec(memory_space=pltpu.VMEM),
        scratch_shapes=[
            pltpu.VMEM(buffers, jnp.bfloat16),
            pltpu.VMEM(buffers, jnp.bfloat16),
            pltpu.SemaphoreType.DMA(buffers[:3]),
            pltpu.SemaphoreType.DMA(buffers[:3]),
        ],
        compiler_params=pltpu.CompilerParams(collective_id=1, has_side_effects=True),
        name="ring_projection",
    )(normed, weight)

def local(
    inner_input,
    state_maps,
    gate_input,
    step_input,
    log_decay_rate,
    step_bias,
    skip_gain,
    conv_kernel,
    map_kernel,
    norm_gain,
    out_weight,
):
    row_count = inner_input.shape[0]
    kernel_remainder = conv_kernel.shape[0] - 1
    groups = state_maps.shape[2]
    per_group = HEADS // NGROUPS
    head_count = groups * per_group
    block_count = row_count // BLOCK
    tail_inner, tail_maps = passed_along(
        (inner_input[row_count - kernel_remainder :], state_maps[row_count - kernel_remainder :]),
        "seq",
        1,
    )
    inner_conv = conv_silu(
        jnp.concatenate((tail_inner, inner_input), axis=0), conv_kernel, row_count
    )
    maps_conv = conv_silu(jnp.concatenate((tail_maps, state_maps), axis=0), map_kernel, row_count)
    step = jnp.minimum(jax.nn.softplus(step_input + step_bias), step_limit)
    log_step = step * -jnp.exp(log_decay_rate)
    step_blocks = step.reshape(block_count, BLOCK, groups, per_group)
    cumul = jnp.cumsum(log_step.reshape(block_count, BLOCK, groups, per_group), axis=1)
    x_blocks = inner_conv.reshape(block_count, BLOCK, groups, per_group, HEAD_DIM)
    b_blocks = maps_conv[:, 0].reshape(block_count, BLOCK, groups, STATE)
    c_blocks = maps_conv[:, 1].reshape(block_count, BLOCK, groups, STATE)
    scores = jnp.einsum("ctgn,csgn->cgts", c_blocks, b_blocks, preferred_element_type=jnp.float32)
    cumul_t = cumul.transpose(0, 2, 3, 1)
    gap = cumul_t[..., :, None] - cumul_t[..., None, :]
    row_ids = lax.broadcasted_iota(jnp.int32, (BLOCK, BLOCK), 0)
    col_ids = lax.broadcasted_iota(jnp.int32, (BLOCK, BLOCK), 1)
    decay = jnp.exp(jnp.where(row_ids >= col_ids, gap, -jnp.inf))
    mixing = (scores[:, :, None] * decay * step_blocks.transpose(0, 2, 3, 1)[..., None, :]).astype(
        jnp.bfloat16
    )
    y_local = jnp.einsum("cgjts,csgjp->ctgjp", mixing, x_blocks, preferred_element_type=jnp.float32)
    weighted = (
        (jnp.exp(cumul[:, -1:] - cumul) * step_blocks)[..., None] * b_blocks[:, :, :, None, :]
    ).astype(jnp.bfloat16)
    block_states = jnp.einsum(
        "csgjp,csgjn->cgjpn", x_blocks, weighted, preferred_element_type=jnp.float32
    )
    block_decay = cumul[:, -1]
    running = jnp.zeros((groups, per_group, HEAD_DIM, STATE), jnp.float32)
    local_in = []
    for block_index in range(block_count):
        local_in.append(running)
        running = (
            jnp.exp(block_decay[block_index])[..., None, None] * running + block_states[block_index]
        )
    slab_decay = jnp.sum(block_decay, axis=0)
    state_shape = (groups * per_group, HEAD_DIM, STATE)
    decay_tile = jnp.broadcast_to(slab_decay.reshape(groups * per_group, 1), (groups * per_group, STATE))
    entering = state_scan(running.reshape(state_shape), decay_tile).reshape(running.shape)
    leading = jnp.cumsum(block_decay, axis=0) - block_decay
    state_in = (
        jnp.exp(leading)[..., None, None] * entering[None] + jnp.stack(local_in, axis=0)
    ).astype(jnp.bfloat16)
    width = per_group * HEAD_DIM
    y_pre = lax.optimization_barrier(
        y_local + skip_gain.reshape(groups, per_group)[:, :, None] * x_blocks
    )
    chunk_count = 1
    per_chunk = block_count // chunk_count
    outs = []
    for chunk in range(chunk_count):
        part = slice(chunk * per_chunk, (chunk + 1) * per_chunk)
        rows = per_chunk * BLOCK
        y_carry = jnp.exp(cumul[part])[..., None] * jnp.einsum(
            "ctgn,cgjpn->ctgjp", c_blocks[part], state_in[part], preferred_element_type=jnp.float32
        )
        y_all = y_pre[part] + y_carry
        gate_rows = gate_input[chunk * rows : (chunk + 1) * rows]
        gated = y_all.reshape(rows, groups, width) * jax.nn.silu(
            gate_rows.reshape(rows, groups, width).astype(jnp.float32)
        )
        square_mean = jnp.mean(gated * gated, axis=-1, keepdims=True)
        normed = (
            (gated * lax.rsqrt(square_mean + epsilon) * norm_gain.reshape(groups, width))
            .astype(jnp.bfloat16)
            .reshape(rows, head_count * HEAD_DIM)
        )
        outs.append(ring_projection(normed, out_weight))
    return jnp.concatenate(outs, axis=0)


def solution(mesh):
    return jax.shard_map(
        local,
        mesh=mesh,
        in_specs=(
            P("seq", "chan"),
            P("seq", None, "chan", None),
            P("seq", "chan"),
            P("seq", "chan"),
            P("chan"),
            P("chan"),
            P("chan"),
            P(None, "chan"),
            P(None, None, "chan", None),
            P("chan"),
            P("chan", None),
        ),
        out_specs=P("seq", "chan"),
        check_vma=False,
    )
```

```python
import functools

import jax
import jax.numpy as jnp
from jax import lax
from jax.experimental import pallas as pl
from jax.experimental.pallas import tpu as pltpu
from jax.sharding import PartitionSpec as P

HEADS = 128
HEAD_DIM = 64
STATE = 128
NGROUPS = 8
BLOCK = 256


step_limit = 0.5
epsilon = 1e-05


def passed_along(x, axis, by):
    count = lax.axis_size(axis)
    pairs = [(i, i + by) for i in range(count) if 0 <= i + by < count]
    return lax.ppermute(x, axis, pairs)


def conv_silu(padded, kernel, length):
    acc = jnp.zeros((length,) + padded.shape[1:], jnp.float32)
    for offset in range(kernel.shape[0]):
        acc = acc + kernel[offset] * padded[offset : offset + length].astype(jnp.float32)
    return jax.nn.silu(acc).astype(jnp.bfloat16)


MESH = pl.DeviceIdType.MESH


def scan_distances(count):
    distances = []
    distance = 1
    while distance < count:
        distances.append(distance)
        distance *= 2
    return distances


def scale_add(out, decay, incoming, base):
    for head in range(out.shape[0]):
        out[head] = jnp.exp(decay[head : head + 1, :]) * incoming[head] + base[head]


def state_scan_kernel(
    count, state_ref, decay_ref, out_ref,
    own_s, own_d, pair_s, pair_d, cur_s, cur_d, send_s, send_d, recv_s, recv_d, back_s, ssem, rsem,
):
    me = lax.axis_index("seq")
    chan = lax.axis_index("chan")
    core = me % 2
    chip = me // 2
    chips = count // 2
    half = state_ref.shape[0] // 2
    partner = me + 1 - 2 * core
    distances = scan_distances(chips)

    barrier = pltpu.get_barrier_semaphore()
    pl.semaphore_signal(barrier, 1, device_id=(partner, chan), device_id_type=MESH)
    peers = jnp.int32(1)
    for distance in distances:
        for target in (chip + distance, chip - distance):
            valid = jnp.logical_and(target >= 0, target < chips)

            @pl.when(valid)
            def _(target=target):
                pl.semaphore_signal(
                    barrier, 1, device_id=(2 * target + core, chan), device_id_type=MESH
                )

            peers = peers + valid.astype(jnp.int32)
    pl.semaphore_wait(barrier, peers)

    def remote(src, dst, slot, part, target):
        return pltpu.make_async_remote_copy(
            src_ref=src, dst_ref=dst, send_sem=ssem.at[slot, part], recv_sem=rsem.at[slot, part],
            device_id=(target, chan), device_id_type=MESH,
        )

    own_s[...] = state_ref[...].astype(jnp.bfloat16)
    own_d[...] = decay_ref[...]
    first = [
        lambda t: remote(own_s, pair_s, 0, 0, t),
        lambda t: remote(own_s.at[0:half], pair_s.at[0:half], 0, 0, t),
    ]
    first_d = lambda t: remote(own_d, pair_d, 0, 1, t)

    @pl.when(core == 0)
    def _():
        first[0](partner).start()
        first_d(partner).start()
        first[1](partner).wait_recv()
        first_d(partner).wait_recv()
        cur_d[...] = own_d[0:half] + pair_d[0:half]
        scale_add(cur_s, pair_d[0:half], state_ref.at[0:half], pair_s[0:half].astype(jnp.float32))

    @pl.when(core == 1)
    def _():
        first[1](partner).start()
        first_d(partner).start()
        first[0](partner).wait_recv()
        first_d(partner).wait_recv()
        cur_d[...] = own_d[half:] + pair_d[half:]
        scale_add(
            cur_s, own_d[half:], pair_s[half:].astype(jnp.float32), state_ref.at[half:]
        )

    rounds = [[1, 2]] + [[distance] for distance in distances[1:]]
    outgoing = []
    slot = 0
    for index, round_distances in enumerate(rounds):
        send_s[index] = cur_s[...].astype(jnp.bfloat16)
        send_d[index] = cur_d[...]
        start = slot
        for distance in round_distances:
            makers = (
                lambda t, index=index, slot=slot: remote(send_s.at[index], recv_s.at[slot], slot + 1, 0, t),
                lambda t, index=index, slot=slot: remote(send_d.at[index], recv_d.at[slot], slot + 1, 1, t),
            )
            sends = chip + distance < chips

            @pl.when(sends)
            def _(makers=makers, distance=distance):
                for make in makers:
                    make(2 * (chip + distance) + core).start()

            outgoing.append((sends, makers, distance))
            slot += 1
        for at in range(start, slot):
            sends, makers, distance = outgoing[at]
            receives = chip - distance >= 0
            opening = index == 0 and distance == 1

            @pl.when(receives)
            def _(makers=makers, distance=distance, at=at, opening=opening):
                for make in makers:
                    make(2 * (chip - distance) + core).wait_recv()
                if opening:
                    cur_s[...] = recv_s[at].astype(jnp.float32)
                    cur_d[...] = recv_d[at]
                else:
                    scale_add(cur_s, cur_d[...], recv_s.at[at], cur_s)
                    cur_d[...] = recv_d[at] + cur_d[...]

            if opening:

                @pl.when(jnp.logical_not(receives))
                def _():
                    cur_s[...] = jnp.zeros_like(cur_s)
                    cur_d[...] = jnp.zeros_like(cur_d)

    last = len(outgoing) + 1
    own_half = send_s.at[len(rounds)]
    own_half[...] = cur_s[...].astype(jnp.bfloat16)
    final = remote(own_half, back_s, last, 0, partner)
    final.start()
    final.wait_recv()

    @pl.when(core == 0)
    def _():
        out_ref[0:half] = cur_s[...]
        out_ref[half:] = back_s[...].astype(jnp.float32)

    @pl.when(core == 1)
    def _():
        out_ref[0:half] = back_s[...].astype(jnp.float32)
        out_ref[half:] = cur_s[...]
        scale_add(out_ref, pair_d[...], out_ref, pair_s)

    final.wait_send()

    @pl.when(core == 0)
    def _():
        first[0](partner).wait_send()
        first_d(partner).wait_send()

    @pl.when(core == 1)
    def _():
        first[1](partner).wait_send()
        first_d(partner).wait_send()

    for sends, makers, distance in outgoing:

        @pl.when(sends)
        def _(makers=makers, distance=distance):
            for make in makers:
                make(2 * (chip + distance) + core).wait_send()


def state_scan(state, decay):
    count = lax.axis_size("seq")
    rounds = len(scan_distances(count // 2))
    heads = state.shape[0]
    half_shape = (heads // 2,) + state.shape[1:]
    half_decay = (heads // 2,) + decay.shape[1:]
    return pl.pallas_call(
        functools.partial(state_scan_kernel, count),
        out_shape=jax.ShapeDtypeStruct(state.shape, jnp.float32),
        in_specs=[pl.BlockSpec(memory_space=pltpu.VMEM)] * 2,
        out_specs=pl.BlockSpec(memory_space=pltpu.VMEM),
        scratch_shapes=[
            pltpu.VMEM(state.shape, jnp.bfloat16),
            pltpu.VMEM(decay.shape, jnp.float32),
            pltpu.VMEM(state.shape, jnp.bfloat16),
            pltpu.VMEM(decay.shape, jnp.float32),
            pltpu.VMEM(half_shape, jnp.float32),
            pltpu.VMEM(half_decay, jnp.float32),
            pltpu.VMEM((rounds + 1,) + half_shape, jnp.bfloat16),
            pltpu.VMEM((rounds,) + half_decay, jnp.float32),
            pltpu.VMEM((rounds + 1,) + half_shape, jnp.bfloat16),
            pltpu.VMEM((rounds + 1,) + half_decay, jnp.float32),
            pltpu.VMEM(half_shape, jnp.bfloat16),
            pltpu.SemaphoreType.DMA((rounds + 3, 2)),
            pltpu.SemaphoreType.DMA((rounds + 3, 2)),
        ],
        compiler_params=pltpu.CompilerParams(collective_id=0, has_side_effects=True),
        name="state_scan",
    )(state, decay)

def ring_kernel(count, pieces, normed_ref, weight_ref, out_ref, send_buf, recv_buf, ssem, rsem):
    me = lax.axis_index("chan")
    seq = lax.axis_index("seq")
    width = out_ref.shape[1]
    rows = normed_ref.shape[1] // (2 * pieces)
    targets = (lax.rem(me + 1, count), lax.rem(me + count - 1, count))

    barrier = pltpu.get_barrier_semaphore()
    for target in targets:
        pl.semaphore_signal(barrier, 1, device_id=(seq, target), device_id_type=MESH)
    pl.semaphore_wait(barrier, 2)

    def copy(direction, step, piece):
        return pltpu.make_async_remote_copy(
            src_ref=send_buf.at[direction, step, piece],
            dst_ref=recv_buf.at[direction, step, piece],
            send_sem=ssem.at[direction, step, piece],
            recv_sem=rsem.at[direction, step, piece],
            device_id=(seq, targets[direction]),
            device_id_type=MESH,
        )

    def block(direction, step):
        if direction == 0:
            return lax.rem(me + 2 * count - 1 - step, count)
        return lax.rem(me + 1 + step, count)

    def partial(direction, step, piece):
        start = (direction * pieces + piece) * rows
        column = pl.multiple_of(block(direction, step) * width, width)
        return lax.dot_general(
            normed_ref[:, pl.ds(start, rows)],
            weight_ref[:, pl.ds(column, width)],
            (((0,), (0,)), ((), ())),
            preferred_element_type=jnp.float32,
        )

    def run_step(step, first, last):
        for piece in range(pieces):
            for direction in range(2):
                value = partial(direction, step, piece)
                if not first:
                    copy(direction, step - 1, piece).wait_recv()
                    value = value + recv_buf[direction, step - 1, piece].astype(jnp.float32)
                if last:
                    start = (direction * pieces + piece) * rows
                    out_ref[pl.ds(start, rows), :] = value.astype(out_ref.dtype)
                else:
                    send_buf[direction, step, piece] = value.astype(send_buf.dtype)
                    copy(direction, step, piece).start()

    run_step(0, True, False)

    def middle(step, carry):
        run_step(step, False, False)
        return carry

    lax.fori_loop(1, count - 1, middle, 0)
    run_step(count - 1, False, True)

    def drain(step, carry):
        for piece in range(pieces):
            for direction in range(2):
                copy(direction, step, piece).wait_send()
        return carry

    lax.fori_loop(0, count - 1, drain, 0)


def ring_projection(normed, weight):
    count = lax.axis_size("chan")
    pieces = 4
    tokens = normed.shape[1]
    width = weight.shape[1] // count
    rows = tokens // (2 * pieces)
    buffers = (2, count - 1, pieces, rows, width)
    return pl.pallas_call(
        functools.partial(ring_kernel, count, pieces),
        out_shape=jax.ShapeDtypeStruct((tokens, width), jnp.bfloat16),
        in_specs=[pl.BlockSpec(memory_space=pltpu.VMEM)] * 2,
        out_specs=pl.BlockSpec(memory_space=pltpu.VMEM),
        scratch_shapes=[
            pltpu.VMEM(buffers, jnp.bfloat16),
            pltpu.VMEM(buffers, jnp.bfloat16),
            pltpu.SemaphoreType.DMA(buffers[:3]),
            pltpu.SemaphoreType.DMA(buffers[:3]),
        ],
        compiler_params=pltpu.CompilerParams(collective_id=1, has_side_effects=True),
        name="ring_projection",
    )(normed, weight)

def local(
    inner_input,
    state_maps,
    gate_input,
    step_input,
    log_decay_rate,
    step_bias,
    skip_gain,
    conv_kernel,
    map_kernel,
    norm_gain,
    out_weight,
):
    row_count = inner_input.shape[0]
    kernel_remainder = conv_kernel.shape[0] - 1
    groups = state_maps.shape[2]
    per_group = HEADS // NGROUPS
    head_count = groups * per_group
    block_count = row_count // BLOCK
    tail_inner, tail_maps = passed_along(
        (inner_input[row_count - kernel_remainder :], state_maps[row_count - kernel_remainder :]),
        "seq",
        1,
    )
    inner_conv = conv_silu(
        jnp.concatenate((tail_inner, inner_input), axis=0), conv_kernel, row_count
    )
    maps_conv = conv_silu(jnp.concatenate((tail_maps, state_maps), axis=0), map_kernel, row_count)
    step = jnp.minimum(jax.nn.softplus(step_input + step_bias), step_limit)
    log_step = step * -jnp.exp(log_decay_rate)
    step_blocks = step.reshape(block_count, BLOCK, groups, per_group)
    cumul = jnp.cumsum(log_step.reshape(block_count, BLOCK, groups, per_group), axis=1)
    x_blocks = inner_conv.reshape(block_count, BLOCK, groups, per_group, HEAD_DIM)
    b_blocks = maps_conv[:, 0].reshape(block_count, BLOCK, groups, STATE)
    c_blocks = maps_conv[:, 1].reshape(block_count, BLOCK, groups, STATE)
    scores = jnp.einsum("ctgn,csgn->cgts", c_blocks, b_blocks, preferred_element_type=jnp.float32)
    cumul_t = cumul.transpose(0, 2, 3, 1)
    gap = cumul_t[..., :, None] - cumul_t[..., None, :]
    row_ids = lax.broadcasted_iota(jnp.int32, (BLOCK, BLOCK), 0)
    col_ids = lax.broadcasted_iota(jnp.int32, (BLOCK, BLOCK), 1)
    decay = jnp.exp(jnp.where(row_ids >= col_ids, gap, -jnp.inf))
    mixing = (scores[:, :, None] * decay * step_blocks.transpose(0, 2, 3, 1)[..., None, :]).astype(
        jnp.bfloat16
    )
    y_local = jnp.einsum("cgjts,csgjp->ctgjp", mixing, x_blocks, preferred_element_type=jnp.float32)
    weighted = (
        (jnp.exp(cumul[:, -1:] - cumul) * step_blocks)[..., None] * b_blocks[:, :, :, None, :]
    ).astype(jnp.bfloat16)
    block_states = jnp.einsum(
        "csgjp,csgjn->cgjpn", x_blocks, weighted, preferred_element_type=jnp.float32
    )
    block_decay = cumul[:, -1]
    running = jnp.zeros((groups, per_group, HEAD_DIM, STATE), jnp.float32)
    local_in = []
    for block_index in range(block_count):
        local_in.append(running)
        running = (
            jnp.exp(block_decay[block_index])[..., None, None] * running + block_states[block_index]
        )
    slab_decay = jnp.sum(block_decay, axis=0)
    state_shape = (groups * per_group, HEAD_DIM, STATE)
    decay_tile = jnp.broadcast_to(slab_decay.reshape(groups * per_group, 1), (groups * per_group, STATE))
    entering = state_scan(running.reshape(state_shape), decay_tile).reshape(running.shape)
    leading = jnp.cumsum(block_decay, axis=0) - block_decay
    state_in = (
        jnp.exp(leading)[..., None, None] * entering[None] + jnp.stack(local_in, axis=0)
    ).astype(jnp.bfloat16)
    width = per_group * HEAD_DIM
    y_pre = lax.optimization_barrier(
        y_local + skip_gain.reshape(groups, per_group)[:, :, None] * x_blocks
    )
    chunk_count = 1
    per_chunk = block_count // chunk_count
    outs = []
    for chunk in range(chunk_count):
        part = slice(chunk * per_chunk, (chunk + 1) * per_chunk)
        rows = per_chunk * BLOCK
        y_carry = jnp.exp(cumul[part])[..., None] * jnp.einsum(
            "ctgn,cgjpn->ctgjp", c_blocks[part], state_in[part], preferred_element_type=jnp.float32
        )
        y_all = y_pre[part] + y_carry
        gate_rows = gate_input[chunk * rows : (chunk + 1) * rows]
        gated = y_all.reshape(rows, groups, width) * jax.nn.silu(
            gate_rows.reshape(rows, groups, width).astype(jnp.float32)
        )
        square_mean = jnp.mean(gated * gated, axis=-1, keepdims=True)
        normed = (
            (gated * lax.rsqrt(square_mean + epsilon) * norm_gain.reshape(groups, width))
            .astype(jnp.bfloat16)
            .reshape(rows, head_count * HEAD_DIM)
        )
        outs.append(ring_projection(normed.T, out_weight))
    return jnp.concatenate(outs, axis=0)


def solution(mesh):
    return jax.shard_map(
        local,
        mesh=mesh,
        in_specs=(
            P("seq", "chan"),
            P("seq", None, "chan", None),
            P("seq", "chan"),
            P("seq", "chan"),
            P("chan"),
            P("chan"),
            P("chan"),
            P(None, "chan"),
            P(None, None, "chan", None),
            P("chan"),
            P("chan", None),
        ),
        out_specs=P("seq", "chan"),
        check_vma=False,
    )
```

```python
import functools

import jax
import jax.numpy as jnp
from jax import lax
from jax.experimental import pallas as pl
from jax.experimental.pallas import tpu as pltpu
from jax.sharding import PartitionSpec as P

HEADS = 128
HEAD_DIM = 64
STATE = 128
NGROUPS = 8
BLOCK = 256


step_limit = 0.5
epsilon = 1e-05


def passed_along(x, axis, by):
    count = lax.axis_size(axis)
    pairs = [(i, i + by) for i in range(count) if 0 <= i + by < count]
    return lax.ppermute(x, axis, pairs)


def conv_silu(padded, kernel, length):
    acc = jnp.zeros((length,) + padded.shape[1:], jnp.float32)
    for offset in range(kernel.shape[0]):
        acc = acc + kernel[offset] * padded[offset : offset + length].astype(jnp.float32)
    return jax.nn.silu(acc).astype(jnp.bfloat16)


MESH = pl.DeviceIdType.MESH


def scan_distances(count):
    distances = []
    distance = 1
    while distance < count:
        distances.append(distance)
        distance *= 2
    return distances


def scale_add(out, decay, incoming, base):
    for head in range(out.shape[0]):
        out[head] = jnp.exp(decay[head : head + 1, :]) * incoming[head] + base[head]


def state_scan_kernel(
    count, state_ref, decay_ref, out_ref,
    own_s, own_d, pair_s, pair_d, cur_s, cur_d, send_s, send_d, recv_s, recv_d, back_s, ssem, rsem,
):
    me = lax.axis_index("seq")
    chan = lax.axis_index("chan")
    core = me % 2
    chip = me // 2
    chips = count // 2
    half = state_ref.shape[0] // 2
    partner = me + 1 - 2 * core
    distances = scan_distances(chips)

    barrier = pltpu.get_barrier_semaphore()
    pl.semaphore_signal(barrier, 1, device_id=(partner, chan), device_id_type=MESH)
    peers = jnp.int32(1)
    for distance in distances:
        for target in (chip + distance, chip - distance):
            valid = jnp.logical_and(target >= 0, target < chips)

            @pl.when(valid)
            def _(target=target):
                pl.semaphore_signal(
                    barrier, 1, device_id=(2 * target + core, chan), device_id_type=MESH
                )

            peers = peers + valid.astype(jnp.int32)
    pl.semaphore_wait(barrier, peers)

    def remote(src, dst, slot, part, target):
        return pltpu.make_async_remote_copy(
            src_ref=src, dst_ref=dst, send_sem=ssem.at[slot, part], recv_sem=rsem.at[slot, part],
            device_id=(target, chan), device_id_type=MESH,
        )

    own_s[...] = state_ref[...].astype(jnp.bfloat16)
    own_d[...] = decay_ref[...]
    first = [
        lambda t: remote(own_s, pair_s, 0, 0, t),
        lambda t: remote(own_s.at[0:half], pair_s.at[0:half], 0, 0, t),
    ]
    first_d = lambda t: remote(own_d, pair_d, 0, 1, t)

    @pl.when(core == 0)
    def _():
        first[0](partner).start()
        first_d(partner).start()
        first[1](partner).wait_recv()
        first_d(partner).wait_recv()
        cur_d[...] = own_d[0:half] + pair_d[0:half]
        scale_add(cur_s, pair_d[0:half], state_ref.at[0:half], pair_s[0:half].astype(jnp.float32))

    @pl.when(core == 1)
    def _():
        first[1](partner).start()
        first_d(partner).start()
        first[0](partner).wait_recv()
        first_d(partner).wait_recv()
        cur_d[...] = own_d[half:] + pair_d[half:]
        scale_add(
            cur_s, own_d[half:], pair_s[half:].astype(jnp.float32), state_ref.at[half:]
        )

    rounds = [[1, 2]] + [[distance] for distance in distances[1:]]
    outgoing = []
    slot = 0
    for index, round_distances in enumerate(rounds):
        send_s[index] = cur_s[...].astype(jnp.bfloat16)
        send_d[index] = cur_d[...]
        start = slot
        for distance in round_distances:
            makers = (
                lambda t, index=index, slot=slot: remote(send_s.at[index], recv_s.at[slot], slot + 1, 0, t),
                lambda t, index=index, slot=slot: remote(send_d.at[index], recv_d.at[slot], slot + 1, 1, t),
            )
            sends = chip + distance < chips

            @pl.when(sends)
            def _(makers=makers, distance=distance):
                for make in makers:
                    make(2 * (chip + distance) + core).start()

            outgoing.append((sends, makers, distance))
            slot += 1
        for at in range(start, slot):
            sends, makers, distance = outgoing[at]
            receives = chip - distance >= 0
            opening = index == 0 and distance == 1

            @pl.when(receives)
            def _(makers=makers, distance=distance, at=at, opening=opening):
                for make in makers:
                    make(2 * (chip - distance) + core).wait_recv()
                if opening:
                    cur_s[...] = recv_s[at].astype(jnp.float32)
                    cur_d[...] = recv_d[at]
                else:
                    scale_add(cur_s, cur_d[...], recv_s.at[at], cur_s)
                    cur_d[...] = recv_d[at] + cur_d[...]

            if opening:

                @pl.when(jnp.logical_not(receives))
                def _():
                    cur_s[...] = jnp.zeros_like(cur_s)
                    cur_d[...] = jnp.zeros_like(cur_d)

    last = len(outgoing) + 1
    own_half = send_s.at[len(rounds)]
    own_half[...] = cur_s[...].astype(jnp.bfloat16)
    final = remote(own_half, back_s, last, 0, partner)
    final.start()
    final.wait_recv()

    @pl.when(core == 0)
    def _():
        out_ref[0:half] = cur_s[...]
        out_ref[half:] = back_s[...].astype(jnp.float32)

    @pl.when(core == 1)
    def _():
        out_ref[0:half] = back_s[...].astype(jnp.float32)
        out_ref[half:] = cur_s[...]
        scale_add(out_ref, pair_d[...], out_ref, pair_s)

    final.wait_send()

    @pl.when(core == 0)
    def _():
        first[0](partner).wait_send()
        first_d(partner).wait_send()

    @pl.when(core == 1)
    def _():
        first[1](partner).wait_send()
        first_d(partner).wait_send()

    for sends, makers, distance in outgoing:

        @pl.when(sends)
        def _(makers=makers, distance=distance):
            for make in makers:
                make(2 * (chip + distance) + core).wait_send()


def state_scan(state, decay):
    count = lax.axis_size("seq")
    rounds = len(scan_distances(count // 2))
    heads = state.shape[0]
    half_shape = (heads // 2,) + state.shape[1:]
    half_decay = (heads // 2,) + decay.shape[1:]
    return pl.pallas_call(
        functools.partial(state_scan_kernel, count),
        out_shape=jax.ShapeDtypeStruct(state.shape, jnp.float32),
        in_specs=[pl.BlockSpec(memory_space=pltpu.VMEM)] * 2,
        out_specs=pl.BlockSpec(memory_space=pltpu.VMEM),
        scratch_shapes=[
            pltpu.VMEM(state.shape, jnp.bfloat16),
            pltpu.VMEM(decay.shape, jnp.float32),
            pltpu.VMEM(state.shape, jnp.bfloat16),
            pltpu.VMEM(decay.shape, jnp.float32),
            pltpu.VMEM(half_shape, jnp.float32),
            pltpu.VMEM(half_decay, jnp.float32),
            pltpu.VMEM((rounds + 1,) + half_shape, jnp.bfloat16),
            pltpu.VMEM((rounds,) + half_decay, jnp.float32),
            pltpu.VMEM((rounds + 1,) + half_shape, jnp.bfloat16),
            pltpu.VMEM((rounds + 1,) + half_decay, jnp.float32),
            pltpu.VMEM(half_shape, jnp.bfloat16),
            pltpu.SemaphoreType.DMA((rounds + 3, 2)),
            pltpu.SemaphoreType.DMA((rounds + 3, 2)),
        ],
        compiler_params=pltpu.CompilerParams(collective_id=0, has_side_effects=True),
        name="state_scan",
    )(state, decay)

def ring_kernel(count, pieces, normed_ref, weight_ref, out_ref, send_buf, recv_buf, ssem, rsem):
    me = lax.axis_index("chan")
    seq = lax.axis_index("seq")
    width = out_ref.shape[1]
    rows = normed_ref.shape[1] // (2 * pieces)
    targets = (lax.rem(me + 1, count), lax.rem(me + count - 1, count))

    barrier = pltpu.get_barrier_semaphore()
    for target in targets:
        pl.semaphore_signal(barrier, 1, device_id=(seq, target), device_id_type=MESH)
    pl.semaphore_wait(barrier, 2)

    def copy(direction, step, piece):
        return pltpu.make_async_remote_copy(
            src_ref=send_buf.at[direction, step, piece],
            dst_ref=recv_buf.at[direction, step, piece],
            send_sem=ssem.at[direction, step, piece],
            recv_sem=rsem.at[direction, step, piece],
            device_id=(seq, targets[direction]),
            device_id_type=MESH,
        )

    def block(direction, step):
        if direction == 0:
            return lax.rem(me + 2 * count - 1 - step, count)
        return lax.rem(me + 1 + step, count)

    def partial(direction, step, piece):
        start = (direction * pieces + piece) * rows
        column = pl.multiple_of(block(direction, step) * width, width)
        return lax.dot_general(
            normed_ref[:, pl.ds(start, rows)],
            weight_ref[:, pl.ds(column, width)],
            (((0,), (0,)), ((), ())),
            preferred_element_type=jnp.float32,
        )

    def run_step(step, first, last):
        for piece in range(pieces):
            for direction in range(2):
                value = partial(direction, step, piece)
                if not first:
                    copy(direction, step - 1, piece).wait_recv()
                    value = value + recv_buf[direction, step - 1, piece].astype(jnp.float32)
                if last:
                    start = (direction * pieces + piece) * rows
                    out_ref[pl.ds(start, rows), :] = value.astype(out_ref.dtype)
                else:
                    send_buf[direction, step, piece] = value.astype(send_buf.dtype)
                    copy(direction, step, piece).start()

    run_step(0, True, False)

    def middle(step, carry):
        run_step(step, False, False)
        return carry

    lax.fori_loop(1, count - 1, middle, 0)
    run_step(count - 1, False, True)

    def drain(step, carry):
        for piece in range(pieces):
            for direction in range(2):
                copy(direction, step, piece).wait_send()
        return carry

    lax.fori_loop(0, count - 1, drain, 0)


def ring_projection(normed, weight):
    count = lax.axis_size("chan")
    pieces = 8
    tokens = normed.shape[1]
    width = weight.shape[1] // count
    rows = tokens // (2 * pieces)
    buffers = (2, count - 1, pieces, rows, width)
    return pl.pallas_call(
        functools.partial(ring_kernel, count, pieces),
        out_shape=jax.ShapeDtypeStruct((tokens, width), jnp.bfloat16),
        in_specs=[pl.BlockSpec(memory_space=pltpu.VMEM)] * 2,
        out_specs=pl.BlockSpec(memory_space=pltpu.VMEM),
        scratch_shapes=[
            pltpu.VMEM(buffers, jnp.bfloat16),
            pltpu.VMEM(buffers, jnp.bfloat16),
            pltpu.SemaphoreType.DMA(buffers[:3]),
            pltpu.SemaphoreType.DMA(buffers[:3]),
        ],
        compiler_params=pltpu.CompilerParams(collective_id=1, has_side_effects=True),
        name="ring_projection",
    )(normed, weight)

def local(
    inner_input,
    state_maps,
    gate_input,
    step_input,
    log_decay_rate,
    step_bias,
    skip_gain,
    conv_kernel,
    map_kernel,
    norm_gain,
    out_weight,
):
    row_count = inner_input.shape[0]
    kernel_remainder = conv_kernel.shape[0] - 1
    groups = state_maps.shape[2]
    per_group = HEADS // NGROUPS
    head_count = groups * per_group
    block_count = row_count // BLOCK
    tail_inner, tail_maps = passed_along(
        (inner_input[row_count - kernel_remainder :], state_maps[row_count - kernel_remainder :]),
        "seq",
        1,
    )
    inner_conv = conv_silu(
        jnp.concatenate((tail_inner, inner_input), axis=0), conv_kernel, row_count
    )
    maps_conv = conv_silu(jnp.concatenate((tail_maps, state_maps), axis=0), map_kernel, row_count)
    step = jnp.minimum(jax.nn.softplus(step_input + step_bias), step_limit)
    log_step = step * -jnp.exp(log_decay_rate)
    step_blocks = step.reshape(block_count, BLOCK, groups, per_group)
    cumul = jnp.cumsum(log_step.reshape(block_count, BLOCK, groups, per_group), axis=1)
    x_blocks = inner_conv.reshape(block_count, BLOCK, groups, per_group, HEAD_DIM)
    b_blocks = maps_conv[:, 0].reshape(block_count, BLOCK, groups, STATE)
    c_blocks = maps_conv[:, 1].reshape(block_count, BLOCK, groups, STATE)
    scores = jnp.einsum("ctgn,csgn->cgts", c_blocks, b_blocks, preferred_element_type=jnp.float32)
    cumul_t = cumul.transpose(0, 2, 3, 1)
    gap = cumul_t[..., :, None] - cumul_t[..., None, :]
    row_ids = lax.broadcasted_iota(jnp.int32, (BLOCK, BLOCK), 0)
    col_ids = lax.broadcasted_iota(jnp.int32, (BLOCK, BLOCK), 1)
    decay = jnp.exp(jnp.where(row_ids >= col_ids, gap, -jnp.inf))
    mixing = (scores[:, :, None] * decay * step_blocks.transpose(0, 2, 3, 1)[..., None, :]).astype(
        jnp.bfloat16
    )
    y_local = jnp.einsum("cgjts,csgjp->ctgjp", mixing, x_blocks, preferred_element_type=jnp.float32)
    weighted = (
        (jnp.exp(cumul[:, -1:] - cumul) * step_blocks)[..., None] * b_blocks[:, :, :, None, :]
    ).astype(jnp.bfloat16)
    block_states = jnp.einsum(
        "csgjp,csgjn->cgjpn", x_blocks, weighted, preferred_element_type=jnp.float32
    )
    block_decay = cumul[:, -1]
    running = jnp.zeros((groups, per_group, HEAD_DIM, STATE), jnp.float32)
    local_in = []
    for block_index in range(block_count):
        local_in.append(running)
        running = (
            jnp.exp(block_decay[block_index])[..., None, None] * running + block_states[block_index]
        )
    slab_decay = jnp.sum(block_decay, axis=0)
    state_shape = (groups * per_group, HEAD_DIM, STATE)
    decay_tile = jnp.broadcast_to(slab_decay.reshape(groups * per_group, 1), (groups * per_group, STATE))
    entering = state_scan(running.reshape(state_shape), decay_tile).reshape(running.shape)
    leading = jnp.cumsum(block_decay, axis=0) - block_decay
    state_in = (
        jnp.exp(leading)[..., None, None] * entering[None] + jnp.stack(local_in, axis=0)
    ).astype(jnp.bfloat16)
    width = per_group * HEAD_DIM
    y_pre = lax.optimization_barrier(
        y_local + skip_gain.reshape(groups, per_group)[:, :, None] * x_blocks
    )
    chunk_count = 1
    per_chunk = block_count // chunk_count
    outs = []
    for chunk in range(chunk_count):
        part = slice(chunk * per_chunk, (chunk + 1) * per_chunk)
        rows = per_chunk * BLOCK
        y_carry = jnp.exp(cumul[part])[..., None] * jnp.einsum(
            "ctgn,cgjpn->ctgjp", c_blocks[part], state_in[part], preferred_element_type=jnp.float32
        )
        y_all = y_pre[part] + y_carry
        gate_rows = gate_input[chunk * rows : (chunk + 1) * rows]
        gated = y_all.reshape(rows, groups, width) * jax.nn.silu(
            gate_rows.reshape(rows, groups, width).astype(jnp.float32)
        )
        square_mean = jnp.mean(gated * gated, axis=-1, keepdims=True)
        normed = (
            (gated * lax.rsqrt(square_mean + epsilon) * norm_gain.reshape(groups, width))
            .astype(jnp.bfloat16)
            .reshape(rows, head_count * HEAD_DIM)
        )
        outs.append(ring_projection(normed.T, out_weight))
    return jnp.concatenate(outs, axis=0)


def solution(mesh):
    return jax.shard_map(
        local,
        mesh=mesh,
        in_specs=(
            P("seq", "chan"),
            P("seq", None, "chan", None),
            P("seq", "chan"),
            P("seq", "chan"),
            P("chan"),
            P("chan"),
            P("chan"),
            P(None, "chan"),
            P(None, None, "chan", None),
            P("chan"),
            P("chan", None),
        ),
        out_specs=P("seq", "chan"),
        check_vma=False,
    )
```

```python
import functools

import jax
import jax.numpy as jnp
from jax import lax
from jax.experimental import pallas as pl
from jax.experimental.pallas import tpu as pltpu
from jax.sharding import PartitionSpec as P

HEADS = 128
HEAD_DIM = 64
STATE = 128
NGROUPS = 8
BLOCK = 256


step_limit = 0.5
epsilon = 1e-05


def passed_along(x, axis, by):
    count = lax.axis_size(axis)
    pairs = [(i, i + by) for i in range(count) if 0 <= i + by < count]
    return lax.ppermute(x, axis, pairs)


def conv_silu(padded, kernel, length):
    acc = jnp.zeros((length,) + padded.shape[1:], jnp.float32)
    for offset in range(kernel.shape[0]):
        acc = acc + kernel[offset] * padded[offset : offset + length].astype(jnp.float32)
    return jax.nn.silu(acc).astype(jnp.bfloat16)


MESH = pl.DeviceIdType.MESH


def scan_distances(count):
    distances = []
    distance = 1
    while distance < count:
        distances.append(distance)
        distance *= 2
    return distances


def scale_add(out, decay, incoming, base):
    for head in range(out.shape[0]):
        out[head] = jnp.exp(decay[head : head + 1, :]) * incoming[head] + base[head]


def state_scan_kernel(
    count, state_ref, decay_ref, out_ref,
    own_s, own_d, pair_s, pair_d, cur_s, cur_d, send_s, send_d, recv_s, recv_d, back_s, ssem, rsem,
):
    me = lax.axis_index("seq")
    chan = lax.axis_index("chan")
    core = me % 2
    chip = me // 2
    chips = count // 2
    half = state_ref.shape[0] // 2
    partner = me + 1 - 2 * core
    distances = scan_distances(chips)

    barrier = pltpu.get_barrier_semaphore()
    pl.semaphore_signal(barrier, 1, device_id=(partner, chan), device_id_type=MESH)
    peers = jnp.int32(1)
    for distance in distances:
        for target in (chip + distance, chip - distance):
            valid = jnp.logical_and(target >= 0, target < chips)

            @pl.when(valid)
            def _(target=target):
                pl.semaphore_signal(
                    barrier, 1, device_id=(2 * target + core, chan), device_id_type=MESH
                )

            peers = peers + valid.astype(jnp.int32)
    pl.semaphore_wait(barrier, peers)

    def remote(src, dst, slot, part, target):
        return pltpu.make_async_remote_copy(
            src_ref=src, dst_ref=dst, send_sem=ssem.at[slot, part], recv_sem=rsem.at[slot, part],
            device_id=(target, chan), device_id_type=MESH,
        )

    own_s[...] = state_ref[...].astype(jnp.bfloat16)
    own_d[...] = decay_ref[...]
    first = [
        lambda t: remote(own_s, pair_s, 0, 0, t),
        lambda t: remote(own_s.at[0:half], pair_s.at[0:half], 0, 0, t),
    ]
    first_d = lambda t: remote(own_d, pair_d, 0, 1, t)

    @pl.when(core == 0)
    def _():
        first[0](partner).start()
        first_d(partner).start()
        first[1](partner).wait_recv()
        first_d(partner).wait_recv()
        cur_d[...] = own_d[0:half] + pair_d[0:half]
        scale_add(cur_s, pair_d[0:half], state_ref.at[0:half], pair_s[0:half].astype(jnp.float32))

    @pl.when(core == 1)
    def _():
        first[1](partner).start()
        first_d(partner).start()
        first[0](partner).wait_recv()
        first_d(partner).wait_recv()
        cur_d[...] = own_d[half:] + pair_d[half:]
        scale_add(
            cur_s, own_d[half:], pair_s[half:].astype(jnp.float32), state_ref.at[half:]
        )

    rounds = [[1, 2]] + [[distance] for distance in distances[1:]]
    outgoing = []
    slot = 0
    for index, round_distances in enumerate(rounds):
        send_s[index] = cur_s[...].astype(jnp.bfloat16)
        send_d[index] = cur_d[...]
        start = slot
        for distance in round_distances:
            makers = (
                lambda t, index=index, slot=slot: remote(send_s.at[index], recv_s.at[slot], slot + 1, 0, t),
                lambda t, index=index, slot=slot: remote(send_d.at[index], recv_d.at[slot], slot + 1, 1, t),
            )
            sends = chip + distance < chips

            @pl.when(sends)
            def _(makers=makers, distance=distance):
                for make in makers:
                    make(2 * (chip + distance) + core).start()

            outgoing.append((sends, makers, distance))
            slot += 1
        for at in range(start, slot):
            sends, makers, distance = outgoing[at]
            receives = chip - distance >= 0
            opening = index == 0 and distance == 1

            @pl.when(receives)
            def _(makers=makers, distance=distance, at=at, opening=opening):
                for make in makers:
                    make(2 * (chip - distance) + core).wait_recv()
                if opening:
                    cur_s[...] = recv_s[at].astype(jnp.float32)
                    cur_d[...] = recv_d[at]
                else:
                    scale_add(cur_s, cur_d[...], recv_s.at[at], cur_s)
                    cur_d[...] = recv_d[at] + cur_d[...]

            if opening:

                @pl.when(jnp.logical_not(receives))
                def _():
                    cur_s[...] = jnp.zeros_like(cur_s)
                    cur_d[...] = jnp.zeros_like(cur_d)

    last = len(outgoing) + 1
    own_half = send_s.at[len(rounds)]
    own_half[...] = cur_s[...].astype(jnp.bfloat16)
    final = remote(own_half, back_s, last, 0, partner)
    final.start()
    final.wait_recv()

    @pl.when(core == 0)
    def _():
        out_ref[0:half] = cur_s[...]
        out_ref[half:] = back_s[...].astype(jnp.float32)

    @pl.when(core == 1)
    def _():
        out_ref[0:half] = back_s[...].astype(jnp.float32)
        out_ref[half:] = cur_s[...]
        scale_add(out_ref, pair_d[...], out_ref, pair_s)

    final.wait_send()

    @pl.when(core == 0)
    def _():
        first[0](partner).wait_send()
        first_d(partner).wait_send()

    @pl.when(core == 1)
    def _():
        first[1](partner).wait_send()
        first_d(partner).wait_send()

    for sends, makers, distance in outgoing:

        @pl.when(sends)
        def _(makers=makers, distance=distance):
            for make in makers:
                make(2 * (chip + distance) + core).wait_send()


def state_scan(state, decay):
    count = lax.axis_size("seq")
    rounds = len(scan_distances(count // 2))
    heads = state.shape[0]
    half_shape = (heads // 2,) + state.shape[1:]
    half_decay = (heads // 2,) + decay.shape[1:]
    return pl.pallas_call(
        functools.partial(state_scan_kernel, count),
        out_shape=jax.ShapeDtypeStruct(state.shape, jnp.float32),
        in_specs=[pl.BlockSpec(memory_space=pltpu.VMEM)] * 2,
        out_specs=pl.BlockSpec(memory_space=pltpu.VMEM),
        scratch_shapes=[
            pltpu.VMEM(state.shape, jnp.bfloat16),
            pltpu.VMEM(decay.shape, jnp.float32),
            pltpu.VMEM(state.shape, jnp.bfloat16),
            pltpu.VMEM(decay.shape, jnp.float32),
            pltpu.VMEM(half_shape, jnp.float32),
            pltpu.VMEM(half_decay, jnp.float32),
            pltpu.VMEM((rounds + 1,) + half_shape, jnp.bfloat16),
            pltpu.VMEM((rounds,) + half_decay, jnp.float32),
            pltpu.VMEM((rounds + 1,) + half_shape, jnp.bfloat16),
            pltpu.VMEM((rounds + 1,) + half_decay, jnp.float32),
            pltpu.VMEM(half_shape, jnp.bfloat16),
            pltpu.SemaphoreType.DMA((rounds + 3, 2)),
            pltpu.SemaphoreType.DMA((rounds + 3, 2)),
        ],
        compiler_params=pltpu.CompilerParams(collective_id=0, has_side_effects=True),
        name="state_scan",
    )(state, decay)

def ring_kernel(count, pieces, normed_ref, weight_ref, out_ref, send_buf, recv_buf, ssem, rsem):
    me = lax.axis_index("chan")
    seq = lax.axis_index("seq")
    width = out_ref.shape[1]
    rows = normed_ref.shape[1] // (2 * pieces)
    targets = (lax.rem(me + 1, count), lax.rem(me + count - 1, count))

    barrier = pltpu.get_barrier_semaphore()
    for target in targets:
        pl.semaphore_signal(barrier, 1, device_id=(seq, target), device_id_type=MESH)
    pl.semaphore_wait(barrier, 2)

    def copy(direction, step, piece):
        return pltpu.make_async_remote_copy(
            src_ref=send_buf.at[direction, step, piece],
            dst_ref=recv_buf.at[direction, step, piece],
            send_sem=ssem.at[direction, step, piece],
            recv_sem=rsem.at[direction, step, piece],
            device_id=(seq, targets[direction]),
            device_id_type=MESH,
        )

    def block(direction, step):
        if direction == 0:
            return lax.rem(me + 2 * count - 1 - step, count)
        return lax.rem(me + 1 + step, count)

    def partial(direction, step, piece):
        start = (direction * pieces + piece) * rows
        column = pl.multiple_of(block(direction, step) * width, width)
        return lax.dot_general(
            normed_ref[:, pl.ds(start, rows)],
            weight_ref[:, pl.ds(column, width)],
            (((0,), (0,)), ((), ())),
            preferred_element_type=jnp.float32,
        )

    def run_step(step, first, last):
        for piece in range(pieces):
            for direction in range(2):
                value = partial(direction, step, piece)
                if not first:
                    copy(direction, step - 1, piece).wait_recv()
                    value = value + recv_buf[direction, step - 1, piece].astype(jnp.float32)
                if last:
                    start = (direction * pieces + piece) * rows
                    out_ref[pl.ds(start, rows), :] = value.astype(out_ref.dtype)
                else:
                    send_buf[direction, step, piece] = value.astype(send_buf.dtype)
                    copy(direction, step, piece).start()

    run_step(0, True, False)

    def middle(step, carry):
        run_step(step, False, False)
        return carry

    lax.fori_loop(1, count - 1, middle, 0)
    run_step(count - 1, False, True)

    def drain(step, carry):
        for piece in range(pieces):
            for direction in range(2):
                copy(direction, step, piece).wait_send()
        return carry

    lax.fori_loop(0, count - 1, drain, 0)


def ring_projection(normed, weight):
    count = lax.axis_size("chan")
    pieces = 2
    tokens = normed.shape[1]
    width = weight.shape[1] // count
    rows = tokens // (2 * pieces)
    buffers = (2, count - 1, pieces, rows, width)
    return pl.pallas_call(
        functools.partial(ring_kernel, count, pieces),
        out_shape=jax.ShapeDtypeStruct((tokens, width), jnp.bfloat16),
        in_specs=[pl.BlockSpec(memory_space=pltpu.VMEM)] * 2,
        out_specs=pl.BlockSpec(memory_space=pltpu.VMEM),
        scratch_shapes=[
            pltpu.VMEM(buffers, jnp.bfloat16),
            pltpu.VMEM(buffers, jnp.bfloat16),
            pltpu.SemaphoreType.DMA(buffers[:3]),
            pltpu.SemaphoreType.DMA(buffers[:3]),
        ],
        compiler_params=pltpu.CompilerParams(collective_id=1, has_side_effects=True),
        name="ring_projection",
    )(normed, weight)

def local(
    inner_input,
    state_maps,
    gate_input,
    step_input,
    log_decay_rate,
    step_bias,
    skip_gain,
    conv_kernel,
    map_kernel,
    norm_gain,
    out_weight,
):
    row_count = inner_input.shape[0]
    kernel_remainder = conv_kernel.shape[0] - 1
    groups = state_maps.shape[2]
    per_group = HEADS // NGROUPS
    head_count = groups * per_group
    block_count = row_count // BLOCK
    tail_inner, tail_maps = passed_along(
        (inner_input[row_count - kernel_remainder :], state_maps[row_count - kernel_remainder :]),
        "seq",
        1,
    )
    inner_conv = conv_silu(
        jnp.concatenate((tail_inner, inner_input), axis=0), conv_kernel, row_count
    )
    maps_conv = conv_silu(jnp.concatenate((tail_maps, state_maps), axis=0), map_kernel, row_count)
    step = jnp.minimum(jax.nn.softplus(step_input + step_bias), step_limit)
    log_step = step * -jnp.exp(log_decay_rate)
    step_blocks = step.reshape(block_count, BLOCK, groups, per_group)
    cumul = jnp.cumsum(log_step.reshape(block_count, BLOCK, groups, per_group), axis=1)
    x_blocks = inner_conv.reshape(block_count, BLOCK, groups, per_group, HEAD_DIM)
    b_blocks = maps_conv[:, 0].reshape(block_count, BLOCK, groups, STATE)
    c_blocks = maps_conv[:, 1].reshape(block_count, BLOCK, groups, STATE)
    scores = jnp.einsum("ctgn,csgn->cgts", c_blocks, b_blocks, preferred_element_type=jnp.float32)
    cumul_t = cumul.transpose(0, 2, 3, 1)
    gap = cumul_t[..., :, None] - cumul_t[..., None, :]
    row_ids = lax.broadcasted_iota(jnp.int32, (BLOCK, BLOCK), 0)
    col_ids = lax.broadcasted_iota(jnp.int32, (BLOCK, BLOCK), 1)
    decay = jnp.exp(jnp.where(row_ids >= col_ids, gap, -jnp.inf))
    mixing = (scores[:, :, None] * decay * step_blocks.transpose(0, 2, 3, 1)[..., None, :]).astype(
        jnp.bfloat16
    )
    y_local = jnp.einsum("cgjts,csgjp->ctgjp", mixing, x_blocks, preferred_element_type=jnp.float32)
    weighted = (
        (jnp.exp(cumul[:, -1:] - cumul) * step_blocks)[..., None] * b_blocks[:, :, :, None, :]
    ).astype(jnp.bfloat16)
    block_states = jnp.einsum(
        "csgjp,csgjn->cgjpn", x_blocks, weighted, preferred_element_type=jnp.float32
    )
    block_decay = cumul[:, -1]
    running = jnp.zeros((groups, per_group, HEAD_DIM, STATE), jnp.float32)
    local_in = []
    for block_index in range(block_count):
        local_in.append(running)
        running = (
            jnp.exp(block_decay[block_index])[..., None, None] * running + block_states[block_index]
        )
    slab_decay = jnp.sum(block_decay, axis=0)
    state_shape = (groups * per_group, HEAD_DIM, STATE)
    decay_tile = jnp.broadcast_to(slab_decay.reshape(groups * per_group, 1), (groups * per_group, STATE))
    entering = state_scan(running.reshape(state_shape), decay_tile).reshape(running.shape)
    leading = jnp.cumsum(block_decay, axis=0) - block_decay
    state_in = (
        jnp.exp(leading)[..., None, None] * entering[None] + jnp.stack(local_in, axis=0)
    ).astype(jnp.bfloat16)
    width = per_group * HEAD_DIM
    y_pre = lax.optimization_barrier(
        y_local + skip_gain.reshape(groups, per_group)[:, :, None] * x_blocks
    )
    chunk_count = 1
    per_chunk = block_count // chunk_count
    outs = []
    for chunk in range(chunk_count):
        part = slice(chunk * per_chunk, (chunk + 1) * per_chunk)
        rows = per_chunk * BLOCK
        y_carry = jnp.exp(cumul[part])[..., None] * jnp.einsum(
            "ctgn,cgjpn->ctgjp", c_blocks[part], state_in[part], preferred_element_type=jnp.float32
        )
        y_all = y_pre[part] + y_carry
        gate_rows = gate_input[chunk * rows : (chunk + 1) * rows]
        gated = y_all.reshape(rows, groups, width) * jax.nn.silu(
            gate_rows.reshape(rows, groups, width).astype(jnp.float32)
        )
        square_mean = jnp.mean(gated * gated, axis=-1, keepdims=True)
        normed = (
            (gated * lax.rsqrt(square_mean + epsilon) * norm_gain.reshape(groups, width))
            .astype(jnp.bfloat16)
            .reshape(rows, head_count * HEAD_DIM)
        )
        outs.append(ring_projection(normed.T, out_weight))
    return jnp.concatenate(outs, axis=0)


def solution(mesh):
    return jax.shard_map(
        local,
        mesh=mesh,
        in_specs=(
            P("seq", "chan"),
            P("seq", None, "chan", None),
            P("seq", "chan"),
            P("seq", "chan"),
            P("chan"),
            P("chan"),
            P("chan"),
            P(None, "chan"),
            P(None, None, "chan", None),
            P("chan"),
            P("chan", None),
        ),
        out_specs=P("seq", "chan"),
        check_vma=False,
    )
```

```python
import functools

import jax
import jax.numpy as jnp
from jax import lax
from jax.experimental import pallas as pl
from jax.experimental.pallas import tpu as pltpu
from jax.sharding import PartitionSpec as P

HEADS = 128
HEAD_DIM = 64
STATE = 128
NGROUPS = 8
BLOCK = 256


step_limit = 0.5
epsilon = 1e-05


def passed_along(x, axis, by):
    count = lax.axis_size(axis)
    pairs = [(i, i + by) for i in range(count) if 0 <= i + by < count]
    return lax.ppermute(x, axis, pairs)


def conv_silu(padded, kernel, length):
    acc = jnp.zeros((length,) + padded.shape[1:], jnp.float32)
    for offset in range(kernel.shape[0]):
        acc = acc + kernel[offset] * padded[offset : offset + length].astype(jnp.float32)
    return jax.nn.silu(acc).astype(jnp.bfloat16)


MESH = pl.DeviceIdType.MESH


def scan_distances(count):
    distances = []
    distance = 1
    while distance < count:
        distances.append(distance)
        distance *= 2
    return distances


def scale_add(out, decay, incoming, base):
    for head in range(out.shape[0]):
        out[head] = jnp.exp(decay[head : head + 1, :]) * incoming[head] + base[head]


def state_scan_kernel(
    count, state_ref, decay_ref, out_ref,
    own_s, own_d, pair_s, pair_d, cur_s, cur_d, send_s, send_d, recv_s, recv_d, back_s, ssem, rsem,
):
    me = lax.axis_index("seq")
    chan = lax.axis_index("chan")
    core = me % 2
    chip = me // 2
    chips = count // 2
    half = state_ref.shape[0] // 2
    partner = me + 1 - 2 * core
    distances = scan_distances(chips)

    barrier = pltpu.get_barrier_semaphore()
    pl.semaphore_signal(barrier, 1, device_id=(partner, chan), device_id_type=MESH)
    peers = jnp.int32(1)
    for distance in distances:
        for target in (chip + distance, chip - distance):
            valid = jnp.logical_and(target >= 0, target < chips)

            @pl.when(valid)
            def _(target=target):
                pl.semaphore_signal(
                    barrier, 1, device_id=(2 * target + core, chan), device_id_type=MESH
                )

            peers = peers + valid.astype(jnp.int32)
    pl.semaphore_wait(barrier, peers)

    def remote(src, dst, slot, part, target):
        return pltpu.make_async_remote_copy(
            src_ref=src, dst_ref=dst, send_sem=ssem.at[slot, part], recv_sem=rsem.at[slot, part],
            device_id=(target, chan), device_id_type=MESH,
        )

    own_s[...] = state_ref[...].astype(jnp.bfloat16)
    own_d[...] = decay_ref[...]
    first = [
        lambda t: remote(own_s, pair_s, 0, 0, t),
        lambda t: remote(own_s.at[0:half], pair_s.at[0:half], 0, 0, t),
    ]
    first_d = lambda t: remote(own_d, pair_d, 0, 1, t)

    @pl.when(core == 0)
    def _():
        first[0](partner).start()
        first_d(partner).start()
        first[1](partner).wait_recv()
        first_d(partner).wait_recv()
        cur_d[...] = own_d[0:half] + pair_d[0:half]
        scale_add(cur_s, pair_d[0:half], state_ref.at[0:half], pair_s[0:half].astype(jnp.float32))

    @pl.when(core == 1)
    def _():
        first[1](partner).start()
        first_d(partner).start()
        first[0](partner).wait_recv()
        first_d(partner).wait_recv()
        cur_d[...] = own_d[half:] + pair_d[half:]
        scale_add(
            cur_s, own_d[half:], pair_s[half:].astype(jnp.float32), state_ref.at[half:]
        )

    rounds = [[1, 2]] + [[distance] for distance in distances[1:]]
    outgoing = []
    slot = 0
    for index, round_distances in enumerate(rounds):
        send_s[index] = cur_s[...].astype(jnp.bfloat16)
        send_d[index] = cur_d[...]
        start = slot
        for distance in round_distances:
            makers = (
                lambda t, index=index, slot=slot: remote(send_s.at[index], recv_s.at[slot], slot + 1, 0, t),
                lambda t, index=index, slot=slot: remote(send_d.at[index], recv_d.at[slot], slot + 1, 1, t),
            )
            sends = chip + distance < chips

            @pl.when(sends)
            def _(makers=makers, distance=distance):
                for make in makers:
                    make(2 * (chip + distance) + core).start()

            outgoing.append((sends, makers, distance))
            slot += 1
        for at in range(start, slot):
            sends, makers, distance = outgoing[at]
            receives = chip - distance >= 0
            opening = index == 0 and distance == 1

            @pl.when(receives)
            def _(makers=makers, distance=distance, at=at, opening=opening):
                for make in makers:
                    make(2 * (chip - distance) + core).wait_recv()
                if opening:
                    cur_s[...] = recv_s[at].astype(jnp.float32)
                    cur_d[...] = recv_d[at]
                else:
                    scale_add(cur_s, cur_d[...], recv_s.at[at], cur_s)
                    cur_d[...] = recv_d[at] + cur_d[...]

            if opening:

                @pl.when(jnp.logical_not(receives))
                def _():
                    cur_s[...] = jnp.zeros_like(cur_s)
                    cur_d[...] = jnp.zeros_like(cur_d)

    last = len(outgoing) + 1
    own_half = send_s.at[len(rounds)]
    own_half[...] = cur_s[...].astype(jnp.bfloat16)
    final = remote(own_half, back_s, last, 0, partner)
    final.start()
    final.wait_recv()

    @pl.when(core == 0)
    def _():
        out_ref[0:half] = cur_s[...]
        out_ref[half:] = back_s[...].astype(jnp.float32)

    @pl.when(core == 1)
    def _():
        out_ref[0:half] = back_s[...].astype(jnp.float32)
        out_ref[half:] = cur_s[...]
        scale_add(out_ref, pair_d[...], out_ref, pair_s)

    final.wait_send()

    @pl.when(core == 0)
    def _():
        first[0](partner).wait_send()
        first_d(partner).wait_send()

    @pl.when(core == 1)
    def _():
        first[1](partner).wait_send()
        first_d(partner).wait_send()

    for sends, makers, distance in outgoing:

        @pl.when(sends)
        def _(makers=makers, distance=distance):
            for make in makers:
                make(2 * (chip + distance) + core).wait_send()


def state_scan(state, decay):
    count = lax.axis_size("seq")
    rounds = len(scan_distances(count // 2))
    heads = state.shape[0]
    half_shape = (heads // 2,) + state.shape[1:]
    half_decay = (heads // 2,) + decay.shape[1:]
    return pl.pallas_call(
        functools.partial(state_scan_kernel, count),
        out_shape=jax.ShapeDtypeStruct(state.shape, jnp.float32),
        in_specs=[pl.BlockSpec(memory_space=pltpu.VMEM)] * 2,
        out_specs=pl.BlockSpec(memory_space=pltpu.VMEM),
        scratch_shapes=[
            pltpu.VMEM(state.shape, jnp.bfloat16),
            pltpu.VMEM(decay.shape, jnp.float32),
            pltpu.VMEM(state.shape, jnp.bfloat16),
            pltpu.VMEM(decay.shape, jnp.float32),
            pltpu.VMEM(half_shape, jnp.float32),
            pltpu.VMEM(half_decay, jnp.float32),
            pltpu.VMEM((rounds + 1,) + half_shape, jnp.bfloat16),
            pltpu.VMEM((rounds,) + half_decay, jnp.float32),
            pltpu.VMEM((rounds + 1,) + half_shape, jnp.bfloat16),
            pltpu.VMEM((rounds + 1,) + half_decay, jnp.float32),
            pltpu.VMEM(half_shape, jnp.bfloat16),
            pltpu.SemaphoreType.DMA((rounds + 3, 2)),
            pltpu.SemaphoreType.DMA((rounds + 3, 2)),
        ],
        compiler_params=pltpu.CompilerParams(collective_id=0, has_side_effects=True),
        name="state_scan",
    )(state, decay)

def ring_kernel(count, pieces, normed_ref, weight_ref, out_ref, send_buf, recv_buf, ssem, rsem):
    me = lax.axis_index("chan")
    seq = lax.axis_index("seq")
    width = out_ref.shape[1]
    rows = normed_ref.shape[1] // (2 * pieces)
    targets = (lax.rem(me + 1, count), lax.rem(me + count - 1, count))

    barrier = pltpu.get_barrier_semaphore()
    for target in targets:
        pl.semaphore_signal(barrier, 1, device_id=(seq, target), device_id_type=MESH)
    pl.semaphore_wait(barrier, 2)

    def copy(direction, step, piece):
        return pltpu.make_async_remote_copy(
            src_ref=send_buf.at[direction, step, piece],
            dst_ref=recv_buf.at[direction, step, piece],
            send_sem=ssem.at[direction, step, piece],
            recv_sem=rsem.at[direction, step, piece],
            device_id=(seq, targets[direction]),
            device_id_type=MESH,
        )

    def block(direction, step):
        if direction == 0:
            return lax.rem(me + 2 * count - 1 - step, count)
        return lax.rem(me + 1 + step, count)

    def partial(direction, step, piece):
        start = (direction * pieces + piece) * rows
        column = pl.multiple_of(block(direction, step) * width, width)
        return lax.dot_general(
            normed_ref[:, pl.ds(start, rows)],
            weight_ref[:, pl.ds(column, width)],
            (((0,), (0,)), ((), ())),
            preferred_element_type=jnp.float32,
        )

    def run_step(step, first, last):
        for piece in range(pieces):
            for direction in range(2):
                value = partial(direction, step, piece)
                if not first:
                    copy(direction, step - 1, piece).wait_recv()
                    value = value + recv_buf[direction, step - 1, piece].astype(jnp.float32)
                if last:
                    start = (direction * pieces + piece) * rows
                    out_ref[pl.ds(start, rows), :] = value.astype(out_ref.dtype)
                else:
                    send_buf[direction, step, piece] = value.astype(send_buf.dtype)
                    copy(direction, step, piece).start()

    run_step(0, True, False)

    def middle(step, carry):
        run_step(step, False, False)
        return carry

    lax.fori_loop(1, count - 1, middle, 0)
    run_step(count - 1, False, True)

    def drain(step, carry):
        for piece in range(pieces):
            for direction in range(2):
                copy(direction, step, piece).wait_send()
        return carry

    lax.fori_loop(0, count - 1, drain, 0)


def ring_projection(normed, weight):
    count = lax.axis_size("chan")
    pieces = 2
    tokens = normed.shape[1]
    width = weight.shape[1] // count
    rows = tokens // (2 * pieces)
    buffers = (2, count - 1, pieces, rows, width)
    return pl.pallas_call(
        functools.partial(ring_kernel, count, pieces),
        out_shape=jax.ShapeDtypeStruct((tokens, width), jnp.bfloat16),
        in_specs=[pl.BlockSpec(memory_space=pltpu.VMEM)] * 2,
        out_specs=pl.BlockSpec(memory_space=pltpu.VMEM),
        scratch_shapes=[
            pltpu.VMEM(buffers, jnp.bfloat16),
            pltpu.VMEM(buffers, jnp.bfloat16),
            pltpu.SemaphoreType.DMA(buffers[:3]),
            pltpu.SemaphoreType.DMA(buffers[:3]),
        ],
        compiler_params=pltpu.CompilerParams(collective_id=1, has_side_effects=True),
        name="ring_projection",
    )(normed, weight)

def local(
    inner_input,
    state_maps,
    gate_input,
    step_input,
    log_decay_rate,
    step_bias,
    skip_gain,
    conv_kernel,
    map_kernel,
    norm_gain,
    out_weight,
):
    row_count = inner_input.shape[0]
    kernel_remainder = conv_kernel.shape[0] - 1
    groups = state_maps.shape[2]
    per_group = HEADS // NGROUPS
    head_count = groups * per_group
    block_count = row_count // BLOCK
    tail_inner, tail_maps = passed_along(
        (inner_input[row_count - kernel_remainder :], state_maps[row_count - kernel_remainder :]),
        "seq",
        1,
    )
    inner_conv = conv_silu(
        jnp.concatenate((tail_inner, inner_input), axis=0), conv_kernel, row_count
    )
    maps_conv = conv_silu(jnp.concatenate((tail_maps, state_maps), axis=0), map_kernel, row_count)
    step = jnp.minimum(jax.nn.softplus(step_input + step_bias), step_limit)
    log_step = step * -jnp.exp(log_decay_rate)
    step_blocks = step.reshape(block_count, BLOCK, groups, per_group)
    cumul = jnp.cumsum(log_step.reshape(block_count, BLOCK, groups, per_group), axis=1)
    x_blocks = inner_conv.reshape(block_count, BLOCK, groups, per_group, HEAD_DIM)
    b_blocks = maps_conv[:, 0].reshape(block_count, BLOCK, groups, STATE)
    c_blocks = maps_conv[:, 1].reshape(block_count, BLOCK, groups, STATE)
    scores = jnp.einsum("ctgn,csgn->cgts", c_blocks, b_blocks, preferred_element_type=jnp.float32)
    cumul_t = cumul.transpose(0, 2, 3, 1)
    gap = cumul_t[..., :, None] - cumul_t[..., None, :]
    row_ids = lax.broadcasted_iota(jnp.int32, (BLOCK, BLOCK), 0)
    col_ids = lax.broadcasted_iota(jnp.int32, (BLOCK, BLOCK), 1)
    decay = jnp.exp(jnp.where(row_ids >= col_ids, gap, -jnp.inf))
    mixing = (scores[:, :, None] * decay * step_blocks.transpose(0, 2, 3, 1)[..., None, :]).astype(
        jnp.bfloat16
    )
    y_local = jnp.einsum("cgjts,csgjp->ctgjp", mixing, x_blocks, preferred_element_type=jnp.float32)
    weighted = (
        (jnp.exp(cumul[:, -1:] - cumul) * step_blocks)[..., None] * b_blocks[:, :, :, None, :]
    ).astype(jnp.bfloat16)
    block_states = jnp.einsum(
        "csgjp,csgjn->cgjpn", x_blocks, weighted, preferred_element_type=jnp.float32
    )
    block_decay = cumul[:, -1]
    running = jnp.zeros((groups, per_group, HEAD_DIM, STATE), jnp.float32)
    local_in = []
    for block_index in range(block_count):
        local_in.append(running)
        running = (
            jnp.exp(block_decay[block_index])[..., None, None] * running + block_states[block_index]
        )
    slab_decay = jnp.sum(block_decay, axis=0)
    state_shape = (groups * per_group, HEAD_DIM, STATE)
    decay_tile = jnp.broadcast_to(slab_decay.reshape(groups * per_group, 1), (groups * per_group, STATE))
    entering = state_scan(running.reshape(state_shape), decay_tile).reshape(running.shape)
    leading = jnp.cumsum(block_decay, axis=0) - block_decay
    state_in = (
        jnp.exp(leading)[..., None, None] * entering[None] + jnp.stack(local_in, axis=0)
    ).astype(jnp.bfloat16)
    width = per_group * HEAD_DIM
    y_pre = y_local + skip_gain.reshape(groups, per_group)[:, :, None] * x_blocks
    chunk_count = 1
    per_chunk = block_count // chunk_count
    outs = []
    for chunk in range(chunk_count):
        part = slice(chunk * per_chunk, (chunk + 1) * per_chunk)
        rows = per_chunk * BLOCK
        y_carry = jnp.exp(cumul[part])[..., None] * jnp.einsum(
            "ctgn,cgjpn->ctgjp", c_blocks[part], state_in[part], preferred_element_type=jnp.float32
        )
        y_all = y_pre[part] + y_carry
        gate_rows = gate_input[chunk * rows : (chunk + 1) * rows]
        gated = y_all.reshape(rows, groups, width) * jax.nn.silu(
            gate_rows.reshape(rows, groups, width).astype(jnp.float32)
        )
        square_mean = jnp.mean(gated * gated, axis=-1, keepdims=True)
        normed = (
            (gated * lax.rsqrt(square_mean + epsilon) * norm_gain.reshape(groups, width))
            .astype(jnp.bfloat16)
            .reshape(rows, head_count * HEAD_DIM)
        )
        outs.append(ring_projection(normed.T, out_weight))
    return jnp.concatenate(outs, axis=0)


def solution(mesh):
    return jax.shard_map(
        local,
        mesh=mesh,
        in_specs=(
            P("seq", "chan"),
            P("seq", None, "chan", None),
            P("seq", "chan"),
            P("seq", "chan"),
            P("chan"),
            P("chan"),
            P("chan"),
            P(None, "chan"),
            P(None, None, "chan", None),
            P("chan"),
            P("chan", None),
        ),
        out_specs=P("seq", "chan"),
        check_vma=False,
    )
```

```python
import functools

import jax
import jax.numpy as jnp
from jax import lax
from jax.experimental import pallas as pl
from jax.experimental.pallas import tpu as pltpu
from jax.sharding import PartitionSpec as P

HEADS = 128
HEAD_DIM = 64
STATE = 128
NGROUPS = 8
BLOCK = 256


step_limit = 0.5
epsilon = 1e-05


def passed_along(x, axis, by):
    count = lax.axis_size(axis)
    pairs = [(i, i + by) for i in range(count) if 0 <= i + by < count]
    return lax.ppermute(x, axis, pairs)


def conv_silu(padded, kernel, length):
    acc = jnp.zeros((length,) + padded.shape[1:], jnp.float32)
    for offset in range(kernel.shape[0]):
        acc = acc + kernel[offset] * padded[offset : offset + length].astype(jnp.float32)
    return jax.nn.silu(acc).astype(jnp.bfloat16)


MESH = pl.DeviceIdType.MESH


def scan_distances(count):
    distances = []
    distance = 1
    while distance < count:
        distances.append(distance)
        distance *= 2
    return distances


def scale_add(out, decay, incoming, base):
    for head in range(out.shape[0]):
        out[head] = jnp.exp(decay[head : head + 1, :]) * incoming[head] + base[head]


def state_scan_kernel(
    count, state_ref, decay_ref, out_ref,
    own_s, own_d, pair_s, pair_d, cur_s, cur_d, send_s, send_d, recv_s, recv_d, back_s, ssem, rsem,
):
    me = lax.axis_index("seq")
    chan = lax.axis_index("chan")
    core = me % 2
    chip = me // 2
    chips = count // 2
    half = state_ref.shape[0] // 2
    partner = me + 1 - 2 * core
    distances = scan_distances(chips)

    barrier = pltpu.get_barrier_semaphore()
    pl.semaphore_signal(barrier, 1, device_id=(partner, chan), device_id_type=MESH)
    peers = jnp.int32(1)
    for distance in distances:
        for target in (chip + distance, chip - distance):
            valid = jnp.logical_and(target >= 0, target < chips)

            @pl.when(valid)
            def _(target=target):
                pl.semaphore_signal(
                    barrier, 1, device_id=(2 * target + core, chan), device_id_type=MESH
                )

            peers = peers + valid.astype(jnp.int32)
    pl.semaphore_wait(barrier, peers)

    def remote(src, dst, slot, part, target):
        return pltpu.make_async_remote_copy(
            src_ref=src, dst_ref=dst, send_sem=ssem.at[slot, part], recv_sem=rsem.at[slot, part],
            device_id=(target, chan), device_id_type=MESH,
        )

    own_s[...] = state_ref[...].astype(jnp.bfloat16)
    own_d[...] = decay_ref[...]
    first = [
        lambda t: remote(own_s, pair_s, 0, 0, t),
        lambda t: remote(own_s.at[0:half], pair_s.at[0:half], 0, 0, t),
    ]
    first_d = lambda t: remote(own_d, pair_d, 0, 1, t)

    @pl.when(core == 0)
    def _():
        first[0](partner).start()
        first_d(partner).start()
        first[1](partner).wait_recv()
        first_d(partner).wait_recv()
        cur_d[...] = own_d[0:half] + pair_d[0:half]
        scale_add(cur_s, pair_d[0:half], state_ref.at[0:half], pair_s[0:half].astype(jnp.float32))

    @pl.when(core == 1)
    def _():
        first[1](partner).start()
        first_d(partner).start()
        first[0](partner).wait_recv()
        first_d(partner).wait_recv()
        cur_d[...] = own_d[half:] + pair_d[half:]
        scale_add(
            cur_s, own_d[half:], pair_s[half:].astype(jnp.float32), state_ref.at[half:]
        )

    rounds = [[1, 2]] + [[distance] for distance in distances[1:]]
    outgoing = []
    slot = 0
    for index, round_distances in enumerate(rounds):
        send_s[index] = cur_s[...].astype(jnp.bfloat16)
        send_d[index] = cur_d[...]
        start = slot
        for distance in round_distances:
            makers = (
                lambda t, index=index, slot=slot: remote(send_s.at[index], recv_s.at[slot], slot + 1, 0, t),
                lambda t, index=index, slot=slot: remote(send_d.at[index], recv_d.at[slot], slot + 1, 1, t),
            )
            sends = chip + distance < chips

            @pl.when(sends)
            def _(makers=makers, distance=distance):
                for make in makers:
                    make(2 * (chip + distance) + core).start()

            outgoing.append((sends, makers, distance))
            slot += 1
        for at in range(start, slot):
            sends, makers, distance = outgoing[at]
            receives = chip - distance >= 0
            opening = index == 0 and distance == 1

            @pl.when(receives)
            def _(makers=makers, distance=distance, at=at, opening=opening):
                for make in makers:
                    make(2 * (chip - distance) + core).wait_recv()
                if opening:
                    cur_s[...] = recv_s[at].astype(jnp.float32)
                    cur_d[...] = recv_d[at]
                else:
                    scale_add(cur_s, cur_d[...], recv_s.at[at], cur_s)
                    cur_d[...] = recv_d[at] + cur_d[...]

            if opening:

                @pl.when(jnp.logical_not(receives))
                def _():
                    cur_s[...] = jnp.zeros_like(cur_s)
                    cur_d[...] = jnp.zeros_like(cur_d)

    last = len(outgoing) + 1
    own_half = send_s.at[len(rounds)]
    own_half[...] = cur_s[...].astype(jnp.bfloat16)
    final = remote(own_half, back_s, last, 0, partner)
    final.start()
    final.wait_recv()

    @pl.when(core == 0)
    def _():
        out_ref[0:half] = cur_s[...]
        out_ref[half:] = back_s[...].astype(jnp.float32)

    @pl.when(core == 1)
    def _():
        out_ref[0:half] = back_s[...].astype(jnp.float32)
        out_ref[half:] = cur_s[...]
        scale_add(out_ref, pair_d[...], out_ref, pair_s)

    final.wait_send()

    @pl.when(core == 0)
    def _():
        first[0](partner).wait_send()
        first_d(partner).wait_send()

    @pl.when(core == 1)
    def _():
        first[1](partner).wait_send()
        first_d(partner).wait_send()

    for sends, makers, distance in outgoing:

        @pl.when(sends)
        def _(makers=makers, distance=distance):
            for make in makers:
                make(2 * (chip + distance) + core).wait_send()


def state_scan(state, decay):
    count = lax.axis_size("seq")
    rounds = len(scan_distances(count // 2))
    heads = state.shape[0]
    half_shape = (heads // 2,) + state.shape[1:]
    half_decay = (heads // 2,) + decay.shape[1:]
    return pl.pallas_call(
        functools.partial(state_scan_kernel, count),
        out_shape=jax.ShapeDtypeStruct(state.shape, jnp.float32),
        in_specs=[pl.BlockSpec(memory_space=pltpu.VMEM)] * 2,
        out_specs=pl.BlockSpec(memory_space=pltpu.VMEM),
        scratch_shapes=[
            pltpu.VMEM(state.shape, jnp.bfloat16),
            pltpu.VMEM(decay.shape, jnp.float32),
            pltpu.VMEM(state.shape, jnp.bfloat16),
            pltpu.VMEM(decay.shape, jnp.float32),
            pltpu.VMEM(half_shape, jnp.float32),
            pltpu.VMEM(half_decay, jnp.float32),
            pltpu.VMEM((rounds + 1,) + half_shape, jnp.bfloat16),
            pltpu.VMEM((rounds,) + half_decay, jnp.float32),
            pltpu.VMEM((rounds + 1,) + half_shape, jnp.bfloat16),
            pltpu.VMEM((rounds + 1,) + half_decay, jnp.float32),
            pltpu.VMEM(half_shape, jnp.bfloat16),
            pltpu.SemaphoreType.DMA((rounds + 3, 2)),
            pltpu.SemaphoreType.DMA((rounds + 3, 2)),
        ],
        compiler_params=pltpu.CompilerParams(collective_id=0, has_side_effects=True),
        name="state_scan",
    )(state, decay)

def ring_kernel(count, pieces, normed_ref, weight_ref, out_ref, send_buf, recv_buf, ssem, rsem):
    me = lax.axis_index("chan")
    seq = lax.axis_index("seq")
    width = out_ref.shape[1]
    rows = normed_ref.shape[1] // (2 * pieces)
    targets = (lax.rem(me + 1, count), lax.rem(me + count - 1, count))

    barrier = pltpu.get_barrier_semaphore()
    for target in targets:
        pl.semaphore_signal(barrier, 1, device_id=(seq, target), device_id_type=MESH)
    pl.semaphore_wait(barrier, 2)

    def copy(direction, step, piece):
        return pltpu.make_async_remote_copy(
            src_ref=send_buf.at[direction, step, piece],
            dst_ref=recv_buf.at[direction, step, piece],
            send_sem=ssem.at[direction, step, piece],
            recv_sem=rsem.at[direction, step, piece],
            device_id=(seq, targets[direction]),
            device_id_type=MESH,
        )

    def block(direction, step):
        if direction == 0:
            return lax.rem(me + 2 * count - 1 - step, count)
        return lax.rem(me + 1 + step, count)

    def partial(direction, step, piece):
        start = (direction * pieces + piece) * rows
        column = pl.multiple_of(block(direction, step) * width, width)
        return lax.dot_general(
            normed_ref[:, pl.ds(start, rows)],
            weight_ref[:, pl.ds(column, width)],
            (((0,), (0,)), ((), ())),
            preferred_element_type=jnp.float32,
        )

    def run_step(step, first, last):
        for piece in range(pieces):
            for direction in range(2):
                value = partial(direction, step, piece)
                if not first:
                    copy(direction, step - 1, piece).wait_recv()
                    value = value + recv_buf[direction, step - 1, piece].astype(jnp.float32)
                if last:
                    start = (direction * pieces + piece) * rows
                    out_ref[pl.ds(start, rows), :] = value.astype(out_ref.dtype)
                else:
                    send_buf[direction, step, piece] = value.astype(send_buf.dtype)
                    copy(direction, step, piece).start()

    run_step(0, True, False)

    def middle(step, carry):
        run_step(step, False, False)
        return carry

    lax.fori_loop(1, count - 1, middle, 0)
    run_step(count - 1, False, True)

    def drain(step, carry):
        for piece in range(pieces):
            for direction in range(2):
                copy(direction, step, piece).wait_send()
        return carry

    lax.fori_loop(0, count - 1, drain, 0)


def ring_projection(normed, weight):
    count = lax.axis_size("chan")
    pieces = 2
    tokens = normed.shape[1]
    width = weight.shape[1] // count
    rows = tokens // (2 * pieces)
    buffers = (2, count - 1, pieces, rows, width)
    return pl.pallas_call(
        functools.partial(ring_kernel, count, pieces),
        out_shape=jax.ShapeDtypeStruct((tokens, width), jnp.float32),
        in_specs=[pl.BlockSpec(memory_space=pltpu.VMEM)] * 2,
        out_specs=pl.BlockSpec(memory_space=pltpu.VMEM),
        scratch_shapes=[
            pltpu.VMEM(buffers, jnp.bfloat16),
            pltpu.VMEM(buffers, jnp.bfloat16),
            pltpu.SemaphoreType.DMA(buffers[:3]),
            pltpu.SemaphoreType.DMA(buffers[:3]),
        ],
        compiler_params=pltpu.CompilerParams(collective_id=1, has_side_effects=True),
        name="ring_projection",
    )(normed, weight)

def local(
    inner_input,
    state_maps,
    gate_input,
    step_input,
    log_decay_rate,
    step_bias,
    skip_gain,
    conv_kernel,
    map_kernel,
    norm_gain,
    out_weight,
):
    row_count = inner_input.shape[0]
    kernel_remainder = conv_kernel.shape[0] - 1
    groups = state_maps.shape[2]
    per_group = HEADS // NGROUPS
    head_count = groups * per_group
    block_count = row_count // BLOCK
    map_width = state_maps.shape[1] * state_maps.shape[2] * state_maps.shape[3]
    tails = passed_along(
        jnp.concatenate(
            (
                inner_input[row_count - kernel_remainder :],
                state_maps[row_count - kernel_remainder :].reshape(kernel_remainder, map_width),
            ),
            axis=1,
        ),
        "seq",
        1,
    )
    tail_inner = tails[:, : inner_input.shape[1]]
    tail_maps = tails[:, inner_input.shape[1] :].reshape((kernel_remainder,) + state_maps.shape[1:])
    inner_conv = conv_silu(
        jnp.concatenate((tail_inner, inner_input), axis=0), conv_kernel, row_count
    )
    maps_conv = conv_silu(jnp.concatenate((tail_maps, state_maps), axis=0), map_kernel, row_count)
    step = jnp.minimum(jax.nn.softplus(step_input + step_bias), step_limit)
    log_step = step * -jnp.exp(log_decay_rate)
    step_blocks = step.reshape(block_count, BLOCK, groups, per_group)
    cumul = jnp.cumsum(log_step.reshape(block_count, BLOCK, groups, per_group), axis=1)
    x_blocks = inner_conv.reshape(block_count, BLOCK, groups, per_group, HEAD_DIM)
    b_blocks = maps_conv[:, 0].reshape(block_count, BLOCK, groups, STATE)
    c_blocks = maps_conv[:, 1].reshape(block_count, BLOCK, groups, STATE)
    scores = jnp.einsum("ctgn,csgn->cgts", c_blocks, b_blocks, preferred_element_type=jnp.float32)
    cumul_t = cumul.transpose(0, 2, 3, 1)
    gap = cumul_t[..., :, None] - cumul_t[..., None, :]
    row_ids = lax.broadcasted_iota(jnp.int32, (BLOCK, BLOCK), 0)
    col_ids = lax.broadcasted_iota(jnp.int32, (BLOCK, BLOCK), 1)
    decay = jnp.exp(jnp.where(row_ids >= col_ids, gap, -jnp.inf))
    mixing = (scores[:, :, None] * decay * step_blocks.transpose(0, 2, 3, 1)[..., None, :]).astype(
        jnp.bfloat16
    )
    y_local = jnp.einsum("cgjts,csgjp->ctgjp", mixing, x_blocks, preferred_element_type=jnp.float32)
    weighted = (
        (jnp.exp(cumul[:, -1:] - cumul) * step_blocks)[..., None] * b_blocks[:, :, :, None, :]
    ).astype(jnp.bfloat16)
    block_states = jnp.einsum(
        "csgjp,csgjn->cgjpn", x_blocks, weighted, preferred_element_type=jnp.float32
    )
    block_decay = cumul[:, -1]
    running = jnp.zeros((groups, per_group, HEAD_DIM, STATE), jnp.float32)
    local_in = []
    for block_index in range(block_count):
        local_in.append(running)
        running = (
            jnp.exp(block_decay[block_index])[..., None, None] * running + block_states[block_index]
        )
    slab_decay = jnp.sum(block_decay, axis=0)
    state_shape = (groups * per_group, HEAD_DIM, STATE)
    decay_tile = jnp.broadcast_to(slab_decay.reshape(groups * per_group, 1), (groups * per_group, STATE))
    entering = state_scan(running.reshape(state_shape), decay_tile).reshape(running.shape)
    leading = jnp.cumsum(block_decay, axis=0) - block_decay
    state_in = (
        jnp.exp(leading)[..., None, None] * entering[None] + jnp.stack(local_in, axis=0)
    ).astype(jnp.bfloat16)
    width = per_group * HEAD_DIM
    y_pre = lax.optimization_barrier(
        y_local + skip_gain.reshape(groups, per_group)[:, :, None] * x_blocks
    )
    chunk_count = 1
    per_chunk = block_count // chunk_count
    outs = []
    for chunk in range(chunk_count):
        part = slice(chunk * per_chunk, (chunk + 1) * per_chunk)
        rows = per_chunk * BLOCK
        y_carry = jnp.exp(cumul[part])[..., None] * jnp.einsum(
            "ctgn,cgjpn->ctgjp", c_blocks[part], state_in[part], preferred_element_type=jnp.float32
        )
        y_all = y_pre[part] + y_carry
        gate_rows = gate_input[chunk * rows : (chunk + 1) * rows]
        gated = y_all.reshape(rows, groups, width) * jax.nn.silu(
            gate_rows.reshape(rows, groups, width).astype(jnp.float32)
        )
        square_mean = jnp.mean(gated * gated, axis=-1, keepdims=True)
        normed = (
            (gated * lax.rsqrt(square_mean + epsilon) * norm_gain.reshape(groups, width))
            .astype(jnp.bfloat16)
            .reshape(rows, head_count * HEAD_DIM)
        )
        outs.append(ring_projection(normed.T, out_weight).astype(jnp.bfloat16))
    return jnp.concatenate(outs, axis=0)


def solution(mesh):
    return jax.shard_map(
        local,
        mesh=mesh,
        in_specs=(
            P("seq", "chan"),
            P("seq", None, "chan", None),
            P("seq", "chan"),
            P("seq", "chan"),
            P("chan"),
            P("chan"),
            P("chan"),
            P(None, "chan"),
            P(None, None, "chan", None),
            P("chan"),
            P("chan", None),
        ),
        out_specs=P("seq", "chan"),
        check_vma=False,
    )
```

```python
import functools

import jax
import jax.numpy as jnp
from jax import lax
from jax.experimental import pallas as pl
from jax.experimental.pallas import tpu as pltpu
from jax.sharding import PartitionSpec as P

HEADS = 128
HEAD_DIM = 64
STATE = 128
NGROUPS = 8
BLOCK = 256


step_limit = 0.5
epsilon = 1e-05


def passed_along(x, axis, by):
    count = lax.axis_size(axis)
    pairs = [(i, i + by) for i in range(count) if 0 <= i + by < count]
    return lax.ppermute(x, axis, pairs)


def conv_silu(padded, kernel, length):
    acc = jnp.zeros((length,) + padded.shape[1:], jnp.float32)
    for offset in range(kernel.shape[0]):
        acc = acc + kernel[offset] * padded[offset : offset + length].astype(jnp.float32)
    return jax.nn.silu(acc).astype(jnp.bfloat16)


MESH = pl.DeviceIdType.MESH


def scan_distances(count):
    distances = []
    distance = 1
    while distance < count:
        distances.append(distance)
        distance *= 2
    return distances


def scale_add(out, decay, incoming, base):
    for head in range(out.shape[0]):
        out[head] = jnp.exp(decay[head : head + 1, :]) * incoming[head] + base[head]


def state_scan_kernel(
    count, state_ref, decay_ref, out_ref,
    own_s, own_d, pair_s, pair_d, cur_s, cur_d, send_s, send_d, recv_s, recv_d, back_s, ssem, rsem,
):
    me = lax.axis_index("seq")
    chan = lax.axis_index("chan")
    core = me % 2
    chip = me // 2
    chips = count // 2
    half = state_ref.shape[0] // 2
    partner = me + 1 - 2 * core
    distances = scan_distances(chips)

    barrier = pltpu.get_barrier_semaphore()
    pl.semaphore_signal(barrier, 1, device_id=(partner, chan), device_id_type=MESH)
    peers = jnp.int32(1)
    for distance in distances:
        for target in (chip + distance, chip - distance):
            valid = jnp.logical_and(target >= 0, target < chips)

            @pl.when(valid)
            def _(target=target):
                pl.semaphore_signal(
                    barrier, 1, device_id=(2 * target + core, chan), device_id_type=MESH
                )

            peers = peers + valid.astype(jnp.int32)
    pl.semaphore_wait(barrier, peers)

    def remote(src, dst, slot, part, target):
        return pltpu.make_async_remote_copy(
            src_ref=src, dst_ref=dst, send_sem=ssem.at[slot, part], recv_sem=rsem.at[slot, part],
            device_id=(target, chan), device_id_type=MESH,
        )

    own_s[...] = state_ref[...].astype(jnp.bfloat16)
    own_d[...] = decay_ref[...]
    first = [
        lambda t: remote(own_s, pair_s, 0, 0, t),
        lambda t: remote(own_s.at[0:half], pair_s.at[0:half], 0, 0, t),
    ]
    first_d = lambda t: remote(own_d, pair_d, 0, 1, t)

    @pl.when(core == 0)
    def _():
        first[0](partner).start()
        first_d(partner).start()
        first[1](partner).wait_recv()
        first_d(partner).wait_recv()
        cur_d[...] = own_d[0:half] + pair_d[0:half]
        scale_add(cur_s, pair_d[0:half], state_ref.at[0:half], pair_s[0:half].astype(jnp.float32))

    @pl.when(core == 1)
    def _():
        first[1](partner).start()
        first_d(partner).start()
        first[0](partner).wait_recv()
        first_d(partner).wait_recv()
        cur_d[...] = own_d[half:] + pair_d[half:]
        scale_add(
            cur_s, own_d[half:], pair_s[half:].astype(jnp.float32), state_ref.at[half:]
        )

    rounds = [[1, 2]] + [[distance] for distance in distances[1:]]
    outgoing = []
    slot = 0
    for index, round_distances in enumerate(rounds):
        send_s[index] = cur_s[...].astype(jnp.bfloat16)
        send_d[index] = cur_d[...]
        start = slot
        for distance in round_distances:
            makers = (
                lambda t, index=index, slot=slot: remote(send_s.at[index], recv_s.at[slot], slot + 1, 0, t),
                lambda t, index=index, slot=slot: remote(send_d.at[index], recv_d.at[slot], slot + 1, 1, t),
            )
            sends = chip + distance < chips

            @pl.when(sends)
            def _(makers=makers, distance=distance):
                for make in makers:
                    make(2 * (chip + distance) + core).start()

            outgoing.append((sends, makers, distance))
            slot += 1
        for at in range(start, slot):
            sends, makers, distance = outgoing[at]
            receives = chip - distance >= 0
            opening = index == 0 and distance == 1

            @pl.when(receives)
            def _(makers=makers, distance=distance, at=at, opening=opening):
                for make in makers:
                    make(2 * (chip - distance) + core).wait_recv()
                if opening:
                    cur_s[...] = recv_s[at].astype(jnp.float32)
                    cur_d[...] = recv_d[at]
                else:
                    scale_add(cur_s, cur_d[...], recv_s.at[at], cur_s)
                    cur_d[...] = recv_d[at] + cur_d[...]

            if opening:

                @pl.when(jnp.logical_not(receives))
                def _():
                    cur_s[...] = jnp.zeros_like(cur_s)
                    cur_d[...] = jnp.zeros_like(cur_d)

    last = len(outgoing) + 1
    own_half = send_s.at[len(rounds)]
    own_half[...] = cur_s[...].astype(jnp.bfloat16)
    final = remote(own_half, back_s, last, 0, partner)
    final.start()
    final.wait_recv()

    @pl.when(core == 0)
    def _():
        out_ref[0:half] = cur_s[...]
        out_ref[half:] = back_s[...].astype(jnp.float32)

    @pl.when(core == 1)
    def _():
        out_ref[0:half] = back_s[...].astype(jnp.float32)
        out_ref[half:] = cur_s[...]
        scale_add(out_ref, pair_d[...], out_ref, pair_s)

    final.wait_send()

    @pl.when(core == 0)
    def _():
        first[0](partner).wait_send()
        first_d(partner).wait_send()

    @pl.when(core == 1)
    def _():
        first[1](partner).wait_send()
        first_d(partner).wait_send()

    for sends, makers, distance in outgoing:

        @pl.when(sends)
        def _(makers=makers, distance=distance):
            for make in makers:
                make(2 * (chip + distance) + core).wait_send()


def state_scan(state, decay):
    count = lax.axis_size("seq")
    rounds = len(scan_distances(count // 2))
    heads = state.shape[0]
    half_shape = (heads // 2,) + state.shape[1:]
    half_decay = (heads // 2,) + decay.shape[1:]
    return pl.pallas_call(
        functools.partial(state_scan_kernel, count),
        out_shape=jax.ShapeDtypeStruct(state.shape, jnp.float32),
        in_specs=[pl.BlockSpec(memory_space=pltpu.VMEM)] * 2,
        out_specs=pl.BlockSpec(memory_space=pltpu.VMEM),
        scratch_shapes=[
            pltpu.VMEM(state.shape, jnp.bfloat16),
            pltpu.VMEM(decay.shape, jnp.float32),
            pltpu.VMEM(state.shape, jnp.bfloat16),
            pltpu.VMEM(decay.shape, jnp.float32),
            pltpu.VMEM(half_shape, jnp.float32),
            pltpu.VMEM(half_decay, jnp.float32),
            pltpu.VMEM((rounds + 1,) + half_shape, jnp.bfloat16),
            pltpu.VMEM((rounds,) + half_decay, jnp.float32),
            pltpu.VMEM((rounds + 1,) + half_shape, jnp.bfloat16),
            pltpu.VMEM((rounds + 1,) + half_decay, jnp.float32),
            pltpu.VMEM(half_shape, jnp.bfloat16),
            pltpu.SemaphoreType.DMA((rounds + 3, 2)),
            pltpu.SemaphoreType.DMA((rounds + 3, 2)),
        ],
        compiler_params=pltpu.CompilerParams(collective_id=0, has_side_effects=True),
        name="state_scan",
    )(state, decay)

def ring_kernel(count, pieces, normed_ref, weight_ref, out_ref, send_buf, recv_buf, ssem, rsem):
    me = lax.axis_index("chan")
    seq = lax.axis_index("seq")
    width = out_ref.shape[1]
    rows = normed_ref.shape[1] // (2 * pieces)
    targets = (lax.rem(me + 1, count), lax.rem(me + count - 1, count))

    barrier = pltpu.get_barrier_semaphore()
    for target in targets:
        pl.semaphore_signal(barrier, 1, device_id=(seq, target), device_id_type=MESH)
    pl.semaphore_wait(barrier, 2)

    def copy(direction, step, piece):
        return pltpu.make_async_remote_copy(
            src_ref=send_buf.at[direction, step, piece],
            dst_ref=recv_buf.at[direction, step, piece],
            send_sem=ssem.at[direction, step, piece],
            recv_sem=rsem.at[direction, step, piece],
            device_id=(seq, targets[direction]),
            device_id_type=MESH,
        )

    def block(direction, step):
        if direction == 0:
            return lax.rem(me + 2 * count - 1 - step, count)
        return lax.rem(me + 1 + step, count)

    def partial(direction, step, piece):
        start = (direction * pieces + piece) * rows
        column = pl.multiple_of(block(direction, step) * width, width)
        return lax.dot_general(
            normed_ref[:, pl.ds(start, rows)],
            weight_ref[:, pl.ds(column, width)],
            (((0,), (0,)), ((), ())),
            preferred_element_type=jnp.float32,
        )

    def run_step(step, first, last):
        for piece in range(pieces):
            for direction in range(2):
                value = partial(direction, step, piece)
                if not first:
                    copy(direction, step - 1, piece).wait_recv()
                    value = value + recv_buf[direction, step - 1, piece].astype(jnp.float32)
                if last:
                    start = (direction * pieces + piece) * rows
                    out_ref[pl.ds(start, rows), :] = value.astype(out_ref.dtype)
                else:
                    send_buf[direction, step, piece] = value.astype(send_buf.dtype)
                    copy(direction, step, piece).start()

    run_step(0, True, False)

    def middle(step, carry):
        run_step(step, False, False)
        return carry

    lax.fori_loop(1, count - 1, middle, 0)
    run_step(count - 1, False, True)

    def drain(step, carry):
        for piece in range(pieces):
            for direction in range(2):
                copy(direction, step, piece).wait_send()
        return carry

    lax.fori_loop(0, count - 1, drain, 0)


def ring_projection(normed, weight):
    count = lax.axis_size("chan")
    pieces = 1
    tokens = normed.shape[1]
    width = weight.shape[1] // count
    rows = tokens // (2 * pieces)
    buffers = (2, count - 1, pieces, rows, width)
    return pl.pallas_call(
        functools.partial(ring_kernel, count, pieces),
        out_shape=jax.ShapeDtypeStruct((tokens, width), jnp.bfloat16),
        in_specs=[pl.BlockSpec(memory_space=pltpu.VMEM)] * 2,
        out_specs=pl.BlockSpec(memory_space=pltpu.VMEM),
        scratch_shapes=[
            pltpu.VMEM(buffers, jnp.bfloat16),
            pltpu.VMEM(buffers, jnp.bfloat16),
            pltpu.SemaphoreType.DMA(buffers[:3]),
            pltpu.SemaphoreType.DMA(buffers[:3]),
        ],
        compiler_params=pltpu.CompilerParams(collective_id=1, has_side_effects=True),
        name="ring_projection",
    )(normed, weight)

def local(
    inner_input,
    state_maps,
    gate_input,
    step_input,
    log_decay_rate,
    step_bias,
    skip_gain,
    conv_kernel,
    map_kernel,
    norm_gain,
    out_weight,
):
    row_count = inner_input.shape[0]
    kernel_remainder = conv_kernel.shape[0] - 1
    groups = state_maps.shape[2]
    per_group = HEADS // NGROUPS
    head_count = groups * per_group
    block_count = row_count // BLOCK
    tail_inner, tail_maps = passed_along(
        (inner_input[row_count - kernel_remainder :], state_maps[row_count - kernel_remainder :]),
        "seq",
        1,
    )
    inner_conv = conv_silu(
        jnp.concatenate((tail_inner, inner_input), axis=0), conv_kernel, row_count
    )
    maps_conv = conv_silu(jnp.concatenate((tail_maps, state_maps), axis=0), map_kernel, row_count)
    step = jnp.minimum(jax.nn.softplus(step_input + step_bias), step_limit)
    log_step = step * -jnp.exp(log_decay_rate)
    step_blocks = step.reshape(block_count, BLOCK, groups, per_group)
    cumul = jnp.cumsum(log_step.reshape(block_count, BLOCK, groups, per_group), axis=1)
    x_blocks = inner_conv.reshape(block_count, BLOCK, groups, per_group, HEAD_DIM)
    b_blocks = maps_conv[:, 0].reshape(block_count, BLOCK, groups, STATE)
    c_blocks = maps_conv[:, 1].reshape(block_count, BLOCK, groups, STATE)
    scores = jnp.einsum("ctgn,csgn->cgts", c_blocks, b_blocks, preferred_element_type=jnp.float32)
    cumul_t = cumul.transpose(0, 2, 3, 1)
    gap = cumul_t[..., :, None] - cumul_t[..., None, :]
    row_ids = lax.broadcasted_iota(jnp.int32, (BLOCK, BLOCK), 0)
    col_ids = lax.broadcasted_iota(jnp.int32, (BLOCK, BLOCK), 1)
    decay = jnp.exp(jnp.where(row_ids >= col_ids, gap, -jnp.inf))
    mixing = (scores[:, :, None] * decay * step_blocks.transpose(0, 2, 3, 1)[..., None, :]).astype(
        jnp.bfloat16
    )
    y_local = jnp.einsum("cgjts,csgjp->ctgjp", mixing, x_blocks, preferred_element_type=jnp.float32)
    weighted = (
        (jnp.exp(cumul[:, -1:] - cumul) * step_blocks)[..., None] * b_blocks[:, :, :, None, :]
    ).astype(jnp.bfloat16)
    block_states = jnp.einsum(
        "csgjp,csgjn->cgjpn", x_blocks, weighted, preferred_element_type=jnp.float32
    )
    block_decay = cumul[:, -1]
    running = jnp.zeros((groups, per_group, HEAD_DIM, STATE), jnp.float32)
    local_in = []
    for block_index in range(block_count):
        local_in.append(running)
        running = (
            jnp.exp(block_decay[block_index])[..., None, None] * running + block_states[block_index]
        )
    slab_decay = jnp.sum(block_decay, axis=0)
    state_shape = (groups * per_group, HEAD_DIM, STATE)
    decay_tile = jnp.broadcast_to(slab_decay.reshape(groups * per_group, 1), (groups * per_group, STATE))
    entering = state_scan(running.reshape(state_shape), decay_tile).reshape(running.shape)
    leading = jnp.cumsum(block_decay, axis=0) - block_decay
    state_in = (
        jnp.exp(leading)[..., None, None] * entering[None] + jnp.stack(local_in, axis=0)
    ).astype(jnp.bfloat16)
    width = per_group * HEAD_DIM
    y_pre = lax.optimization_barrier(
        y_local + skip_gain.reshape(groups, per_group)[:, :, None] * x_blocks
    )
    chunk_count = 1
    per_chunk = block_count // chunk_count
    outs = []
    for chunk in range(chunk_count):
        part = slice(chunk * per_chunk, (chunk + 1) * per_chunk)
        rows = per_chunk * BLOCK
        y_carry = jnp.exp(cumul[part])[..., None] * jnp.einsum(
            "ctgn,cgjpn->ctgjp", c_blocks[part], state_in[part], preferred_element_type=jnp.float32
        )
        y_all = y_pre[part] + y_carry
        gate_rows = gate_input[chunk * rows : (chunk + 1) * rows]
        gated = y_all.reshape(rows, groups, width) * jax.nn.silu(
            gate_rows.reshape(rows, groups, width).astype(jnp.float32)
        )
        square_mean = jnp.mean(gated * gated, axis=-1, keepdims=True)
        normed = (
            (gated * lax.rsqrt(square_mean + epsilon) * norm_gain.reshape(groups, width))
            .astype(jnp.bfloat16)
            .reshape(rows, head_count * HEAD_DIM)
        )
        outs.append(ring_projection(normed.T, out_weight))
    return jnp.concatenate(outs, axis=0)


def solution(mesh):
    return jax.shard_map(
        local,
        mesh=mesh,
        in_specs=(
            P("seq", "chan"),
            P("seq", None, "chan", None),
            P("seq", "chan"),
            P("seq", "chan"),
            P("chan"),
            P("chan"),
            P("chan"),
            P(None, "chan"),
            P(None, None, "chan", None),
            P("chan"),
            P("chan", None),
        ),
        out_specs=P("seq", "chan"),
        check_vma=False,
    )
```

```python
import functools

import jax
import jax.numpy as jnp
from jax import lax
from jax.experimental import pallas as pl
from jax.experimental.pallas import tpu as pltpu
from jax.sharding import PartitionSpec as P

HEADS = 128
HEAD_DIM = 64
STATE = 128
NGROUPS = 8
BLOCK = 256


step_limit = 0.5
epsilon = 1e-05


def passed_along(x, axis, by):
    count = lax.axis_size(axis)
    pairs = [(i, i + by) for i in range(count) if 0 <= i + by < count]
    return lax.ppermute(x, axis, pairs)


def conv_silu(padded, kernel, length):
    acc = jnp.zeros((length,) + padded.shape[1:], jnp.float32)
    for offset in range(kernel.shape[0]):
        acc = acc + kernel[offset] * padded[offset : offset + length].astype(jnp.float32)
    return jax.nn.silu(acc).astype(jnp.bfloat16)


MESH = pl.DeviceIdType.MESH


def scan_distances(count):
    distances = []
    distance = 1
    while distance < count:
        distances.append(distance)
        distance *= 2
    return distances


def scale_add(out, decay, incoming, base):
    for head in range(out.shape[0]):
        out[head] = jnp.exp(decay[head : head + 1, :]) * incoming[head] + base[head]


def state_scan_kernel(
    count, state_ref, decay_ref, out_ref,
    own_s, own_d, pair_s, pair_d, cur_s, cur_d, send_s, send_d, recv_s, recv_d, back_s, ssem, rsem,
):
    me = lax.axis_index("seq")
    chan = lax.axis_index("chan")
    core = me % 2
    chip = me // 2
    chips = count // 2
    half = state_ref.shape[0] // 2
    partner = me + 1 - 2 * core
    distances = scan_distances(chips)

    barrier = pltpu.get_barrier_semaphore()
    pl.semaphore_signal(barrier, 1, device_id=(partner, chan), device_id_type=MESH)
    peers = jnp.int32(1)
    for distance in distances:
        for target in (chip + distance, chip - distance):
            valid = jnp.logical_and(target >= 0, target < chips)

            @pl.when(valid)
            def _(target=target):
                pl.semaphore_signal(
                    barrier, 1, device_id=(2 * target + core, chan), device_id_type=MESH
                )

            peers = peers + valid.astype(jnp.int32)
    pl.semaphore_wait(barrier, peers)

    def remote(src, dst, slot, part, target, piece=0):
        return pltpu.make_async_remote_copy(
            src_ref=src, dst_ref=dst, send_sem=ssem.at[slot, part, piece], recv_sem=rsem.at[slot, part, piece],
            device_id=(target, chan), device_id_type=MESH,
        )

    own_s[...] = state_ref[...].astype(jnp.bfloat16)
    own_d[...] = decay_ref[...]
    first = [
        lambda t: remote(own_s, pair_s, 0, 0, t),
        lambda t: remote(own_s.at[0:half], pair_s.at[0:half], 0, 0, t),
    ]
    first_d = lambda t: remote(own_d, pair_d, 0, 1, t)

    @pl.when(core == 0)
    def _():
        first[0](partner).start()
        first_d(partner).start()
        first[1](partner).wait_recv()
        first_d(partner).wait_recv()
        for piece in range(cur_d.shape[0]):
            rows = slice(piece * cur_d.shape[1], (piece + 1) * cur_d.shape[1])
            cur_d[piece] = own_d[rows] + pair_d[rows]
        scale_add(cur_s, pair_d[0:half], state_ref.at[0:half], pair_s[0:half].astype(jnp.float32))

    @pl.when(core == 1)
    def _():
        first[1](partner).start()
        first_d(partner).start()
        first[0](partner).wait_recv()
        first_d(partner).wait_recv()
        for piece in range(cur_d.shape[0]):
            rows = slice(half + piece * cur_d.shape[1], half + (piece + 1) * cur_d.shape[1])
            cur_d[piece] = own_d[rows] + pair_d[rows]
        scale_add(
            cur_s, own_d[half:], pair_s[half:].astype(jnp.float32), state_ref.at[half:]
        )

    rounds = [[1, 2]] + [[distance] for distance in distances[1:]]
    pieces = cur_d.shape[0]
    per_piece = half // pieces
    plan = []
    slot = 0
    for index, round_distances in enumerate(rounds):
        plan.append([(distance, slot + offset) for offset, distance in enumerate(round_distances)])
        slot += len(round_distances)
    outgoing = []

    def makers(index, at, piece):
        heads = slice(piece * per_piece, (piece + 1) * per_piece)
        return (
            lambda t: remote(send_s.at[index, heads], recv_s.at[at, heads], at + 1, 0, t, piece),
            lambda t: remote(send_d.at[index, piece], recv_d.at[at, piece], at + 1, 1, t, piece),
        )

    def send(index, piece):
        heads = slice(piece * per_piece, (piece + 1) * per_piece)
        send_s[index, heads] = cur_s[heads].astype(jnp.bfloat16)
        send_d[index, piece] = cur_d[piece]
        for distance, at in plan[index]:
            pair = makers(index, at, piece)
            sends = chip + distance < chips

            @pl.when(sends)
            def _(pair=pair, distance=distance):
                for make in pair:
                    make(2 * (chip + distance) + core).start()

            outgoing.append((sends, pair, distance))

    def receive(index, piece):
        heads = slice(piece * per_piece, (piece + 1) * per_piece)
        for distance, at in plan[index]:
            pair = makers(index, at, piece)
            receives = chip - distance >= 0
            opening = index == 0 and distance == 1

            @pl.when(receives)
            def _(pair=pair, distance=distance, at=at, opening=opening):
                for make in pair:
                    make(2 * (chip - distance) + core).wait_recv()
                if opening:
                    cur_s[heads] = recv_s[at, heads].astype(jnp.float32)
                    cur_d[piece] = recv_d[at, piece]
                else:
                    scale_add(cur_s.at[heads], cur_d[piece], recv_s.at[at, heads], cur_s.at[heads])
                    cur_d[piece] = recv_d[at, piece] + cur_d[piece]

            if opening:

                @pl.when(jnp.logical_not(receives))
                def _():
                    cur_s[heads] = jnp.zeros((per_piece,) + cur_s.shape[1:], jnp.float32)
                    cur_d[piece] = jnp.zeros(cur_d.shape[1:], jnp.float32)

    for piece in range(pieces):
        send(0, piece)
    for index in range(len(rounds)):
        for piece in range(pieces):
            receive(index, piece)
            if index + 1 < len(rounds):
                send(index + 1, piece)

    last = slot + 1
    own_half = send_s.at[len(rounds)]
    own_half[...] = cur_s[...].astype(jnp.bfloat16)
    final = remote(own_half, back_s, last, 0, partner)
    final.start()
    final.wait_recv()

    @pl.when(core == 0)
    def _():
        out_ref[0:half] = cur_s[...]
        out_ref[half:] = back_s[...].astype(jnp.float32)

    @pl.when(core == 1)
    def _():
        out_ref[0:half] = back_s[...].astype(jnp.float32)
        out_ref[half:] = cur_s[...]
        scale_add(out_ref, pair_d[...], out_ref, pair_s)

    final.wait_send()

    @pl.when(core == 0)
    def _():
        first[0](partner).wait_send()
        first_d(partner).wait_send()

    @pl.when(core == 1)
    def _():
        first[1](partner).wait_send()
        first_d(partner).wait_send()

    for sends, makers, distance in outgoing:

        @pl.when(sends)
        def _(makers=makers, distance=distance):
            for make in makers:
                make(2 * (chip + distance) + core).wait_send()


def state_scan(state, decay):
    count = lax.axis_size("seq")
    rounds = len(scan_distances(count // 2))
    heads = state.shape[0]
    half_shape = (heads // 2,) + state.shape[1:]
    half_decay = (2, heads // 4) + decay.shape[1:]
    return pl.pallas_call(
        functools.partial(state_scan_kernel, count),
        out_shape=jax.ShapeDtypeStruct(state.shape, jnp.float32),
        in_specs=[pl.BlockSpec(memory_space=pltpu.VMEM)] * 2,
        out_specs=pl.BlockSpec(memory_space=pltpu.VMEM),
        scratch_shapes=[
            pltpu.VMEM(state.shape, jnp.bfloat16),
            pltpu.VMEM(decay.shape, jnp.float32),
            pltpu.VMEM(state.shape, jnp.bfloat16),
            pltpu.VMEM(decay.shape, jnp.float32),
            pltpu.VMEM(half_shape, jnp.float32),
            pltpu.VMEM(half_decay, jnp.float32),
            pltpu.VMEM((rounds + 1,) + half_shape, jnp.bfloat16),
            pltpu.VMEM((rounds,) + half_decay, jnp.float32),
            pltpu.VMEM((rounds + 1,) + half_shape, jnp.bfloat16),
            pltpu.VMEM((rounds + 1,) + half_decay, jnp.float32),
            pltpu.VMEM(half_shape, jnp.bfloat16),
            pltpu.SemaphoreType.DMA((rounds + 3, 2, 2)),
            pltpu.SemaphoreType.DMA((rounds + 3, 2, 2)),
        ],
        compiler_params=pltpu.CompilerParams(collective_id=0, has_side_effects=True),
        name="state_scan",
    )(state, decay)

def ring_kernel(count, pieces, normed_ref, weight_ref, out_ref, send_buf, recv_buf, ssem, rsem):
    me = lax.axis_index("chan")
    seq = lax.axis_index("seq")
    width = out_ref.shape[1]
    rows = normed_ref.shape[1] // (2 * pieces)
    targets = (lax.rem(me + 1, count), lax.rem(me + count - 1, count))

    barrier = pltpu.get_barrier_semaphore()
    for target in targets:
        pl.semaphore_signal(barrier, 1, device_id=(seq, target), device_id_type=MESH)
    pl.semaphore_wait(barrier, 2)

    def copy(direction, step, piece):
        return pltpu.make_async_remote_copy(
            src_ref=send_buf.at[direction, step, piece],
            dst_ref=recv_buf.at[direction, step, piece],
            send_sem=ssem.at[direction, step, piece],
            recv_sem=rsem.at[direction, step, piece],
            device_id=(seq, targets[direction]),
            device_id_type=MESH,
        )

    def block(direction, step):
        if direction == 0:
            return lax.rem(me + 2 * count - 1 - step, count)
        return lax.rem(me + 1 + step, count)

    def partial(direction, step, piece):
        start = (direction * pieces + piece) * rows
        column = pl.multiple_of(block(direction, step) * width, width)
        return lax.dot_general(
            normed_ref[:, pl.ds(start, rows)],
            weight_ref[:, pl.ds(column, width)],
            (((0,), (0,)), ((), ())),
            preferred_element_type=jnp.float32,
        )

    def run_step(step, first, last):
        for piece in range(pieces):
            for direction in range(2):
                value = partial(direction, step, piece)
                if not first:
                    copy(direction, step - 1, piece).wait_recv()
                    value = value + recv_buf[direction, step - 1, piece].astype(jnp.float32)
                if last:
                    start = (direction * pieces + piece) * rows
                    out_ref[pl.ds(start, rows), :] = value.astype(out_ref.dtype)
                else:
                    send_buf[direction, step, piece] = value.astype(send_buf.dtype)
                    copy(direction, step, piece).start()

    run_step(0, True, False)

    def middle(step, carry):
        run_step(step, False, False)
        return carry

    lax.fori_loop(1, count - 1, middle, 0)
    run_step(count - 1, False, True)

    def drain(step, carry):
        for piece in range(pieces):
            for direction in range(2):
                copy(direction, step, piece).wait_send()
        return carry

    lax.fori_loop(0, count - 1, drain, 0)


def ring_projection(normed, weight):
    count = lax.axis_size("chan")
    pieces = 2
    tokens = normed.shape[1]
    width = weight.shape[1] // count
    rows = tokens // (2 * pieces)
    buffers = (2, count - 1, pieces, rows, width)
    return pl.pallas_call(
        functools.partial(ring_kernel, count, pieces),
        out_shape=jax.ShapeDtypeStruct((tokens, width), jnp.bfloat16),
        in_specs=[pl.BlockSpec(memory_space=pltpu.VMEM)] * 2,
        out_specs=pl.BlockSpec(memory_space=pltpu.VMEM),
        scratch_shapes=[
            pltpu.VMEM(buffers, jnp.bfloat16),
            pltpu.VMEM(buffers, jnp.bfloat16),
            pltpu.SemaphoreType.DMA(buffers[:3]),
            pltpu.SemaphoreType.DMA(buffers[:3]),
        ],
        compiler_params=pltpu.CompilerParams(collective_id=1, has_side_effects=True),
        name="ring_projection",
    )(normed, weight)

def local(
    inner_input,
    state_maps,
    gate_input,
    step_input,
    log_decay_rate,
    step_bias,
    skip_gain,
    conv_kernel,
    map_kernel,
    norm_gain,
    out_weight,
):
    row_count = inner_input.shape[0]
    kernel_remainder = conv_kernel.shape[0] - 1
    groups = state_maps.shape[2]
    per_group = HEADS // NGROUPS
    head_count = groups * per_group
    block_count = row_count // BLOCK
    tail_inner, tail_maps = passed_along(
        (inner_input[row_count - kernel_remainder :], state_maps[row_count - kernel_remainder :]),
        "seq",
        1,
    )
    inner_conv = conv_silu(
        jnp.concatenate((tail_inner, inner_input), axis=0), conv_kernel, row_count
    )
    maps_conv = conv_silu(jnp.concatenate((tail_maps, state_maps), axis=0), map_kernel, row_count)
    step = jnp.minimum(jax.nn.softplus(step_input + step_bias), step_limit)
    log_step = step * -jnp.exp(log_decay_rate)
    step_blocks = step.reshape(block_count, BLOCK, groups, per_group)
    cumul = jnp.cumsum(log_step.reshape(block_count, BLOCK, groups, per_group), axis=1)
    x_blocks = inner_conv.reshape(block_count, BLOCK, groups, per_group, HEAD_DIM)
    b_blocks = maps_conv[:, 0].reshape(block_count, BLOCK, groups, STATE)
    c_blocks = maps_conv[:, 1].reshape(block_count, BLOCK, groups, STATE)
    scores = jnp.einsum("ctgn,csgn->cgts", c_blocks, b_blocks, preferred_element_type=jnp.float32)
    cumul_t = cumul.transpose(0, 2, 3, 1)
    gap = cumul_t[..., :, None] - cumul_t[..., None, :]
    row_ids = lax.broadcasted_iota(jnp.int32, (BLOCK, BLOCK), 0)
    col_ids = lax.broadcasted_iota(jnp.int32, (BLOCK, BLOCK), 1)
    decay = jnp.exp(jnp.where(row_ids >= col_ids, gap, -jnp.inf))
    mixing = (scores[:, :, None] * decay * step_blocks.transpose(0, 2, 3, 1)[..., None, :]).astype(
        jnp.bfloat16
    )
    y_local = jnp.einsum("cgjts,csgjp->ctgjp", mixing, x_blocks, preferred_element_type=jnp.float32)
    weighted = (
        (jnp.exp(cumul[:, -1:] - cumul) * step_blocks)[..., None] * b_blocks[:, :, :, None, :]
    ).astype(jnp.bfloat16)
    block_states = jnp.einsum(
        "csgjp,csgjn->cgjpn", x_blocks, weighted, preferred_element_type=jnp.float32
    )
    block_decay = cumul[:, -1]
    running = jnp.zeros((groups, per_group, HEAD_DIM, STATE), jnp.float32)
    local_in = []
    for block_index in range(block_count):
        local_in.append(running)
        running = (
            jnp.exp(block_decay[block_index])[..., None, None] * running + block_states[block_index]
        )
    slab_decay = jnp.sum(block_decay, axis=0)
    state_shape = (groups * per_group, HEAD_DIM, STATE)
    decay_tile = jnp.broadcast_to(slab_decay.reshape(groups * per_group, 1), (groups * per_group, STATE))
    entering = state_scan(running.reshape(state_shape), decay_tile).reshape(running.shape)
    leading = jnp.cumsum(block_decay, axis=0) - block_decay
    state_in = (
        jnp.exp(leading)[..., None, None] * entering[None] + jnp.stack(local_in, axis=0)
    ).astype(jnp.bfloat16)
    width = per_group * HEAD_DIM
    y_pre = lax.optimization_barrier(
        y_local + skip_gain.reshape(groups, per_group)[:, :, None] * x_blocks
    )
    chunk_count = 1
    per_chunk = block_count // chunk_count
    outs = []
    for chunk in range(chunk_count):
        part = slice(chunk * per_chunk, (chunk + 1) * per_chunk)
        rows = per_chunk * BLOCK
        y_carry = jnp.exp(cumul[part])[..., None] * jnp.einsum(
            "ctgn,cgjpn->ctgjp", c_blocks[part], state_in[part], preferred_element_type=jnp.float32
        )
        y_all = y_pre[part] + y_carry
        gate_rows = gate_input[chunk * rows : (chunk + 1) * rows]
        gated = y_all.reshape(rows, groups, width) * jax.nn.silu(
            gate_rows.reshape(rows, groups, width).astype(jnp.float32)
        )
        square_mean = jnp.mean(gated * gated, axis=-1, keepdims=True)
        normed = (
            (gated * lax.rsqrt(square_mean + epsilon) * norm_gain.reshape(groups, width))
            .astype(jnp.bfloat16)
            .reshape(rows, head_count * HEAD_DIM)
        )
        outs.append(ring_projection(normed.T, out_weight))
    return jnp.concatenate(outs, axis=0)


def solution(mesh):
    return jax.shard_map(
        local,
        mesh=mesh,
        in_specs=(
            P("seq", "chan"),
            P("seq", None, "chan", None),
            P("seq", "chan"),
            P("seq", "chan"),
            P("chan"),
            P("chan"),
            P("chan"),
            P(None, "chan"),
            P(None, None, "chan", None),
            P("chan"),
            P("chan", None),
        ),
        out_specs=P("seq", "chan"),
        check_vma=False,
    )
```

```python
import functools

import jax
import jax.numpy as jnp
from jax import lax
from jax.experimental import pallas as pl
from jax.experimental.pallas import tpu as pltpu
from jax.sharding import PartitionSpec as P

HEADS = 128
HEAD_DIM = 64
STATE = 128
NGROUPS = 8
BLOCK = 256


step_limit = 0.5
epsilon = 1e-05


def passed_along(x, axis, by):
    count = lax.axis_size(axis)
    pairs = [(i, i + by) for i in range(count) if 0 <= i + by < count]
    return lax.ppermute(x, axis, pairs)


def conv_silu(padded, kernel, length):
    acc = jnp.zeros((length,) + padded.shape[1:], jnp.float32)
    for offset in range(kernel.shape[0]):
        acc = acc + kernel[offset] * padded[offset : offset + length].astype(jnp.float32)
    return jax.nn.silu(acc).astype(jnp.bfloat16)


MESH = pl.DeviceIdType.MESH


def scan_distances(count):
    distances = []
    distance = 1
    while distance < count:
        distances.append(distance)
        distance *= 2
    return distances


def scale_add(out, decay, incoming, base):
    for head in range(out.shape[0]):
        out[head] = jnp.exp(decay[head : head + 1, :]) * incoming[head] + base[head]


def state_scan_kernel(
    count, state_ref, decay_ref, out_ref,
    own_s, own_d, pair_s, pair_d, cur_s, cur_d, send_s, send_d, recv_s, recv_d, back_s, ssem, rsem,
):
    me = lax.axis_index("seq")
    chan = lax.axis_index("chan")
    core = me % 2
    chip = me // 2
    chips = count // 2
    half = state_ref.shape[0] // 2
    partner = me + 1 - 2 * core
    distances = scan_distances(chips)

    barrier = pltpu.get_barrier_semaphore()
    pl.semaphore_signal(barrier, 1, device_id=(partner, chan), device_id_type=MESH)
    peers = jnp.int32(1)
    for distance in distances:
        for target in (chip + distance, chip - distance):
            valid = jnp.logical_and(target >= 0, target < chips)

            @pl.when(valid)
            def _(target=target):
                pl.semaphore_signal(
                    barrier, 1, device_id=(2 * target + core, chan), device_id_type=MESH
                )

            peers = peers + valid.astype(jnp.int32)
    pl.semaphore_wait(barrier, peers)

    def remote(src, dst, slot, part, target, piece=0):
        return pltpu.make_async_remote_copy(
            src_ref=src, dst_ref=dst, send_sem=ssem.at[slot, part, piece], recv_sem=rsem.at[slot, part, piece],
            device_id=(target, chan), device_id_type=MESH,
        )

    own_s[...] = state_ref[...].astype(jnp.bfloat16)
    own_d[...] = decay_ref[...]
    first = [
        lambda t: remote(own_s, pair_s, 0, 0, t),
        lambda t: remote(own_s.at[0:half], pair_s.at[0:half], 0, 0, t),
    ]
    first_d = lambda t: remote(own_d, pair_d, 0, 1, t)

    @pl.when(core == 0)
    def _():
        first[0](partner).start()
        first_d(partner).start()
        first[1](partner).wait_recv()
        first_d(partner).wait_recv()
        for piece in range(cur_d.shape[0]):
            rows = slice(piece * cur_d.shape[1], (piece + 1) * cur_d.shape[1])
            cur_d[piece] = own_d[rows] + pair_d[rows]
        scale_add(cur_s, pair_d[0:half], state_ref.at[0:half], pair_s[0:half].astype(jnp.float32))

    @pl.when(core == 1)
    def _():
        first[1](partner).start()
        first_d(partner).start()
        first[0](partner).wait_recv()
        first_d(partner).wait_recv()
        for piece in range(cur_d.shape[0]):
            rows = slice(half + piece * cur_d.shape[1], half + (piece + 1) * cur_d.shape[1])
            cur_d[piece] = own_d[rows] + pair_d[rows]
        scale_add(
            cur_s, own_d[half:], pair_s[half:].astype(jnp.float32), state_ref.at[half:]
        )

    rounds = [[1, 2]] + [[distance] for distance in distances[1:]]
    pieces = cur_d.shape[0]
    per_piece = half // pieces
    plan = []
    slot = 0
    for index, round_distances in enumerate(rounds):
        plan.append([(distance, slot + offset) for offset, distance in enumerate(round_distances)])
        slot += len(round_distances)
    outgoing = []

    def makers(index, at, piece):
        heads = slice(piece * per_piece, (piece + 1) * per_piece)
        return (
            lambda t: remote(send_s.at[index, heads], recv_s.at[at, heads], at + 1, 0, t, piece),
            lambda t: remote(send_d.at[index, piece], recv_d.at[at, piece], at + 1, 1, t, piece),
        )

    def send(index, piece):
        heads = slice(piece * per_piece, (piece + 1) * per_piece)
        send_s[index, heads] = cur_s[heads].astype(jnp.bfloat16)
        send_d[index, piece] = cur_d[piece]
        for distance, at in plan[index]:
            pair = makers(index, at, piece)
            sends = chip + distance < chips

            @pl.when(sends)
            def _(pair=pair, distance=distance):
                for make in pair:
                    make(2 * (chip + distance) + core).start()

            outgoing.append((sends, pair, distance))

    def receive(index, piece):
        heads = slice(piece * per_piece, (piece + 1) * per_piece)
        for distance, at in plan[index]:
            pair = makers(index, at, piece)
            receives = chip - distance >= 0
            opening = index == 0 and distance == 1

            @pl.when(receives)
            def _(pair=pair, distance=distance, at=at, opening=opening):
                for make in pair:
                    make(2 * (chip - distance) + core).wait_recv()
                if opening:
                    cur_s[heads] = recv_s[at, heads].astype(jnp.float32)
                    cur_d[piece] = recv_d[at, piece]
                else:
                    scale_add(cur_s.at[heads], cur_d[piece], recv_s.at[at, heads], cur_s.at[heads])
                    cur_d[piece] = recv_d[at, piece] + cur_d[piece]

            if opening:

                @pl.when(jnp.logical_not(receives))
                def _():
                    cur_s[heads] = jnp.zeros((per_piece,) + cur_s.shape[1:], jnp.float32)
                    cur_d[piece] = jnp.zeros(cur_d.shape[1:], jnp.float32)

    for piece in range(pieces):
        send(0, piece)
    for index in range(len(rounds)):
        for piece in range(pieces):
            receive(index, piece)
            if index + 1 < len(rounds):
                send(index + 1, piece)

    last = slot + 1
    own_half = send_s.at[len(rounds)]
    own_half[...] = cur_s[...].astype(jnp.bfloat16)
    final = remote(own_half, back_s, last, 0, partner)
    final.start()
    final.wait_recv()

    @pl.when(core == 0)
    def _():
        out_ref[0:half] = cur_s[...]
        out_ref[half:] = back_s[...].astype(jnp.float32)

    @pl.when(core == 1)
    def _():
        out_ref[0:half] = back_s[...].astype(jnp.float32)
        out_ref[half:] = cur_s[...]
        scale_add(out_ref, pair_d[...], out_ref, pair_s)

    final.wait_send()

    @pl.when(core == 0)
    def _():
        first[0](partner).wait_send()
        first_d(partner).wait_send()

    @pl.when(core == 1)
    def _():
        first[1](partner).wait_send()
        first_d(partner).wait_send()

    for sends, makers, distance in outgoing:

        @pl.when(sends)
        def _(makers=makers, distance=distance):
            for make in makers:
                make(2 * (chip + distance) + core).wait_send()


def state_scan(state, decay):
    count = lax.axis_size("seq")
    rounds = len(scan_distances(count // 2))
    heads = state.shape[0]
    half_shape = (heads // 2,) + state.shape[1:]
    half_decay = (2, heads // 4) + decay.shape[1:]
    return pl.pallas_call(
        functools.partial(state_scan_kernel, count),
        out_shape=jax.ShapeDtypeStruct(state.shape, jnp.float32),
        in_specs=[pl.BlockSpec(memory_space=pltpu.VMEM)] * 2,
        out_specs=pl.BlockSpec(memory_space=pltpu.VMEM),
        scratch_shapes=[
            pltpu.VMEM(state.shape, jnp.bfloat16),
            pltpu.VMEM(decay.shape, jnp.float32),
            pltpu.VMEM(state.shape, jnp.bfloat16),
            pltpu.VMEM(decay.shape, jnp.float32),
            pltpu.VMEM(half_shape, jnp.float32),
            pltpu.VMEM(half_decay, jnp.float32),
            pltpu.VMEM((rounds + 1,) + half_shape, jnp.bfloat16),
            pltpu.VMEM((rounds,) + half_decay, jnp.float32),
            pltpu.VMEM((rounds + 1,) + half_shape, jnp.bfloat16),
            pltpu.VMEM((rounds + 1,) + half_decay, jnp.float32),
            pltpu.VMEM(half_shape, jnp.bfloat16),
            pltpu.SemaphoreType.DMA((rounds + 3, 2, 2)),
            pltpu.SemaphoreType.DMA((rounds + 3, 2, 2)),
        ],
        compiler_params=pltpu.CompilerParams(collective_id=0, has_side_effects=True),
        name="state_scan",
    )(state, decay)

def ring_kernel(count, pieces, normed_ref, weight_ref, out_ref, send_buf, recv_buf, ssem, rsem):
    me = lax.axis_index("chan")
    seq = lax.axis_index("seq")
    width = out_ref.shape[1]
    rows = normed_ref.shape[2]
    targets = (lax.rem(me + 1, count), lax.rem(me + count - 1, count))

    barrier = pltpu.get_barrier_semaphore()
    for target in targets:
        pl.semaphore_signal(barrier, 1, device_id=(seq, target), device_id_type=MESH)
    pl.semaphore_wait(barrier, 2)

    def copy(direction, step, piece):
        return pltpu.make_async_remote_copy(
            src_ref=send_buf.at[direction, step, piece],
            dst_ref=recv_buf.at[direction, step, piece],
            send_sem=ssem.at[direction, step, piece],
            recv_sem=rsem.at[direction, step, piece],
            device_id=(seq, targets[direction]),
            device_id_type=MESH,
        )

    def block(direction, step):
        if direction == 0:
            return lax.rem(me + 2 * count - 1 - step, count)
        return lax.rem(me + 1 + step, count)

    def partial(direction, step, piece):
        start = (direction * pieces + piece) * rows
        column = pl.multiple_of(block(direction, step) * width, width)
        return lax.dot_general(
            normed_ref[direction * pieces + piece],
            weight_ref[:, pl.ds(column, width)],
            (((0,), (0,)), ((), ())),
            preferred_element_type=jnp.float32,
        )

    def run_step(step, first, last):
        for piece in range(pieces):
            for direction in range(2):
                value = partial(direction, step, piece)
                if not first:
                    copy(direction, step - 1, piece).wait_recv()
                    value = value + recv_buf[direction, step - 1, piece].astype(jnp.float32)
                if last:
                    start = (direction * pieces + piece) * rows
                    out_ref[pl.ds(start, rows), :] = value.astype(out_ref.dtype)
                else:
                    send_buf[direction, step, piece] = value.astype(send_buf.dtype)
                    copy(direction, step, piece).start()

    run_step(0, True, False)

    def middle(step, carry):
        run_step(step, False, False)
        return carry

    lax.fori_loop(1, count - 1, middle, 0)
    run_step(count - 1, False, True)

    def drain(step, carry):
        for piece in range(pieces):
            for direction in range(2):
                copy(direction, step, piece).wait_send()
        return carry

    lax.fori_loop(0, count - 1, drain, 0)


def ring_projection(normed, weight):
    count = lax.axis_size("chan")
    pieces = normed.shape[0] // 2
    tokens = normed.shape[0] * normed.shape[2]
    width = weight.shape[1] // count
    rows = tokens // (2 * pieces)
    buffers = (2, count - 1, pieces, rows, width)
    return pl.pallas_call(
        functools.partial(ring_kernel, count, pieces),
        out_shape=jax.ShapeDtypeStruct((tokens, width), jnp.bfloat16),
        in_specs=[pl.BlockSpec(memory_space=pltpu.VMEM)] * 2,
        out_specs=pl.BlockSpec(memory_space=pltpu.VMEM),
        scratch_shapes=[
            pltpu.VMEM(buffers, jnp.bfloat16),
            pltpu.VMEM(buffers, jnp.bfloat16),
            pltpu.SemaphoreType.DMA(buffers[:3]),
            pltpu.SemaphoreType.DMA(buffers[:3]),
        ],
        compiler_params=pltpu.CompilerParams(collective_id=1, has_side_effects=True),
        name="ring_projection",
    )(normed, weight)

def local(
    inner_input,
    state_maps,
    gate_input,
    step_input,
    log_decay_rate,
    step_bias,
    skip_gain,
    conv_kernel,
    map_kernel,
    norm_gain,
    out_weight,
):
    row_count = inner_input.shape[0]
    kernel_remainder = conv_kernel.shape[0] - 1
    groups = state_maps.shape[2]
    per_group = HEADS // NGROUPS
    head_count = groups * per_group
    block_count = row_count // BLOCK
    tail_inner, tail_maps = passed_along(
        (inner_input[row_count - kernel_remainder :], state_maps[row_count - kernel_remainder :]),
        "seq",
        1,
    )
    inner_conv = conv_silu(
        jnp.concatenate((tail_inner, inner_input), axis=0), conv_kernel, row_count
    )
    maps_conv = conv_silu(jnp.concatenate((tail_maps, state_maps), axis=0), map_kernel, row_count)
    step = jnp.minimum(jax.nn.softplus(step_input + step_bias), step_limit)
    log_step = step * -jnp.exp(log_decay_rate)
    step_blocks = step.reshape(block_count, BLOCK, groups, per_group)
    cumul = jnp.cumsum(log_step.reshape(block_count, BLOCK, groups, per_group), axis=1)
    x_blocks = inner_conv.reshape(block_count, BLOCK, groups, per_group, HEAD_DIM)
    b_blocks = maps_conv[:, 0].reshape(block_count, BLOCK, groups, STATE)
    c_blocks = maps_conv[:, 1].reshape(block_count, BLOCK, groups, STATE)
    scores = jnp.einsum("ctgn,csgn->cgts", c_blocks, b_blocks, preferred_element_type=jnp.float32)
    cumul_t = cumul.transpose(0, 2, 3, 1)
    gap = cumul_t[..., :, None] - cumul_t[..., None, :]
    row_ids = lax.broadcasted_iota(jnp.int32, (BLOCK, BLOCK), 0)
    col_ids = lax.broadcasted_iota(jnp.int32, (BLOCK, BLOCK), 1)
    decay = jnp.exp(jnp.where(row_ids >= col_ids, gap, -jnp.inf))
    mixing = (scores[:, :, None] * decay * step_blocks.transpose(0, 2, 3, 1)[..., None, :]).astype(
        jnp.bfloat16
    )
    y_local = jnp.einsum("cgjts,csgjp->ctgjp", mixing, x_blocks, preferred_element_type=jnp.float32)
    weighted = (
        (jnp.exp(cumul[:, -1:] - cumul) * step_blocks)[..., None] * b_blocks[:, :, :, None, :]
    ).astype(jnp.bfloat16)
    block_states = jnp.einsum(
        "csgjp,csgjn->cgjpn", x_blocks, weighted, preferred_element_type=jnp.float32
    )
    block_decay = cumul[:, -1]
    running = jnp.zeros((groups, per_group, HEAD_DIM, STATE), jnp.float32)
    local_in = []
    for block_index in range(block_count):
        local_in.append(running)
        running = (
            jnp.exp(block_decay[block_index])[..., None, None] * running + block_states[block_index]
        )
    slab_decay = jnp.sum(block_decay, axis=0)
    state_shape = (groups * per_group, HEAD_DIM, STATE)
    decay_tile = jnp.broadcast_to(slab_decay.reshape(groups * per_group, 1), (groups * per_group, STATE))
    entering = state_scan(running.reshape(state_shape), decay_tile).reshape(running.shape)
    leading = jnp.cumsum(block_decay, axis=0) - block_decay
    state_in = (
        jnp.exp(leading)[..., None, None] * entering[None] + jnp.stack(local_in, axis=0)
    ).astype(jnp.bfloat16)
    width = per_group * HEAD_DIM
    y_pre = lax.optimization_barrier(
        y_local + skip_gain.reshape(groups, per_group)[:, :, None] * x_blocks
    )
    chunk_count = 1
    per_chunk = block_count // chunk_count
    outs = []
    for chunk in range(chunk_count):
        part = slice(chunk * per_chunk, (chunk + 1) * per_chunk)
        rows = per_chunk * BLOCK
        y_carry = jnp.exp(cumul[part])[..., None] * jnp.einsum(
            "ctgn,cgjpn->ctgjp", c_blocks[part], state_in[part], preferred_element_type=jnp.float32
        )
        y_all = y_pre[part] + y_carry
        gate_rows = gate_input[chunk * rows : (chunk + 1) * rows]
        blocks_here = rows // BLOCK
        y_cols = y_all.reshape(blocks_here, BLOCK, groups, width).transpose(0, 2, 3, 1)
        gate_cols = gate_rows.reshape(blocks_here, BLOCK, groups, width).transpose(0, 2, 3, 1)
        gated = y_cols * jax.nn.silu(gate_cols.astype(jnp.float32))
        square_mean = jnp.mean(gated * gated, axis=2, keepdims=True)
        normed_blocks = (
            (gated * lax.rsqrt(square_mean + epsilon) * norm_gain.reshape(groups, width, 1))
            .astype(jnp.bfloat16)
            .reshape(blocks_here, head_count * HEAD_DIM, BLOCK)
        )
        outs.append(ring_projection(normed_blocks, out_weight))
    return jnp.concatenate(outs, axis=0)


def solution(mesh):
    return jax.shard_map(
        local,
        mesh=mesh,
        in_specs=(
            P("seq", "chan"),
            P("seq", None, "chan", None),
            P("seq", "chan"),
            P("seq", "chan"),
            P("chan"),
            P("chan"),
            P("chan"),
            P(None, "chan"),
            P(None, None, "chan", None),
            P("chan"),
            P("chan", None),
        ),
        out_specs=P("seq", "chan"),
        check_vma=False,
    )
```

```python
import functools

import jax
import jax.numpy as jnp
from jax import lax
from jax.experimental import pallas as pl
from jax.experimental.pallas import tpu as pltpu
from jax.sharding import PartitionSpec as P

HEADS = 128
HEAD_DIM = 64
STATE = 128
NGROUPS = 8
BLOCK = 256


step_limit = 0.5
epsilon = 1e-05


def passed_along(x, axis, by):
    count = lax.axis_size(axis)
    pairs = [(i, i + by) for i in range(count) if 0 <= i + by < count]
    return lax.ppermute(x, axis, pairs)


def conv_silu(padded, kernel, length):
    acc = jnp.zeros((length,) + padded.shape[1:], jnp.float32)
    for offset in range(kernel.shape[0]):
        acc = acc + kernel[offset] * padded[offset : offset + length].astype(jnp.float32)
    return jax.nn.silu(acc).astype(jnp.bfloat16)


MESH = pl.DeviceIdType.MESH


def scan_distances(count):
    distances = []
    distance = 1
    while distance < count:
        distances.append(distance)
        distance *= 2
    return distances


def scale_add(out, decay, incoming, base):
    for head in range(out.shape[0]):
        out[head] = jnp.exp(decay[head : head + 1, :]) * incoming[head] + base[head]


def state_scan_kernel(
    count, state_ref, decay_ref, out_ref,
    own_s, own_d, pair_s, pair_d, cur_s, cur_d, send_s, send_d, recv_s, recv_d, back_s, ssem, rsem,
):
    me = lax.axis_index("seq")
    chan = lax.axis_index("chan")
    core = me % 2
    chip = me // 2
    chips = count // 2
    half = state_ref.shape[0] // 2
    partner = me + 1 - 2 * core
    distances = scan_distances(chips)

    barrier = pltpu.get_barrier_semaphore()
    pl.semaphore_signal(barrier, 1, device_id=(partner, chan), device_id_type=MESH)
    peers = jnp.int32(1)
    for distance in distances:
        for target in (chip + distance, chip - distance):
            valid = jnp.logical_and(target >= 0, target < chips)

            @pl.when(valid)
            def _(target=target):
                pl.semaphore_signal(
                    barrier, 1, device_id=(2 * target + core, chan), device_id_type=MESH
                )

            peers = peers + valid.astype(jnp.int32)
    pl.semaphore_wait(barrier, peers)

    def remote(src, dst, slot, part, target, piece=0):
        return pltpu.make_async_remote_copy(
            src_ref=src, dst_ref=dst, send_sem=ssem.at[slot, part, piece], recv_sem=rsem.at[slot, part, piece],
            device_id=(target, chan), device_id_type=MESH,
        )

    own_s[...] = state_ref[...].astype(jnp.bfloat16)
    own_d[...] = decay_ref[...]
    first = [
        lambda t: remote(own_s, pair_s, 0, 0, t),
        lambda t: remote(own_s.at[0:half], pair_s.at[0:half], 0, 0, t),
    ]
    first_d = lambda t: remote(own_d, pair_d, 0, 1, t)

    @pl.when(core == 0)
    def _():
        first[0](partner).start()
        first_d(partner).start()
        first[1](partner).wait_recv()
        first_d(partner).wait_recv()
        for piece in range(cur_d.shape[0]):
            rows = slice(piece * cur_d.shape[1], (piece + 1) * cur_d.shape[1])
            cur_d[piece] = own_d[rows] + pair_d[rows]
        scale_add(cur_s, pair_d[0:half], state_ref.at[0:half], pair_s[0:half].astype(jnp.float32))

    @pl.when(core == 1)
    def _():
        first[1](partner).start()
        first_d(partner).start()
        first[0](partner).wait_recv()
        first_d(partner).wait_recv()
        for piece in range(cur_d.shape[0]):
            rows = slice(half + piece * cur_d.shape[1], half + (piece + 1) * cur_d.shape[1])
            cur_d[piece] = own_d[rows] + pair_d[rows]
        scale_add(
            cur_s, own_d[half:], pair_s[half:].astype(jnp.float32), state_ref.at[half:]
        )

    rounds = [[1, 2]] + [[distance] for distance in distances[1:]]
    pieces = cur_d.shape[0]
    per_piece = half // pieces
    plan = []
    slot = 0
    for index, round_distances in enumerate(rounds):
        plan.append([(distance, slot + offset) for offset, distance in enumerate(round_distances)])
        slot += len(round_distances)
    outgoing = []

    def makers(index, at, piece):
        heads = slice(piece * per_piece, (piece + 1) * per_piece)
        return (
            lambda t: remote(send_s.at[index, heads], recv_s.at[at, heads], at + 1, 0, t, piece),
            lambda t: remote(send_d.at[index, piece], recv_d.at[at, piece], at + 1, 1, t, piece),
        )

    def send(index, piece):
        heads = slice(piece * per_piece, (piece + 1) * per_piece)
        send_s[index, heads] = cur_s[heads].astype(jnp.bfloat16)
        send_d[index, piece] = cur_d[piece]
        for distance, at in plan[index]:
            pair = makers(index, at, piece)
            sends = chip + distance < chips

            @pl.when(sends)
            def _(pair=pair, distance=distance):
                for make in pair:
                    make(2 * (chip + distance) + core).start()

            outgoing.append((sends, pair, distance))

    def receive(index, piece):
        heads = slice(piece * per_piece, (piece + 1) * per_piece)
        for distance, at in plan[index]:
            pair = makers(index, at, piece)
            receives = chip - distance >= 0
            opening = index == 0 and distance == 1

            @pl.when(receives)
            def _(pair=pair, distance=distance, at=at, opening=opening):
                for make in pair:
                    make(2 * (chip - distance) + core).wait_recv()
                if opening:
                    cur_s[heads] = recv_s[at, heads].astype(jnp.float32)
                    cur_d[piece] = recv_d[at, piece]
                else:
                    scale_add(cur_s.at[heads], cur_d[piece], recv_s.at[at, heads], cur_s.at[heads])
                    cur_d[piece] = recv_d[at, piece] + cur_d[piece]

            if opening:

                @pl.when(jnp.logical_not(receives))
                def _():
                    cur_s[heads] = jnp.zeros((per_piece,) + cur_s.shape[1:], jnp.float32)
                    cur_d[piece] = jnp.zeros(cur_d.shape[1:], jnp.float32)

    for piece in range(pieces):
        send(0, piece)
    for index in range(len(rounds)):
        for piece in range(pieces):
            receive(index, piece)
            if index + 1 < len(rounds):
                send(index + 1, piece)

    last = slot + 1
    own_half = send_s.at[len(rounds)]
    own_half[...] = cur_s[...].astype(jnp.bfloat16)
    final = remote(own_half, back_s, last, 0, partner)
    final.start()
    final.wait_recv()

    @pl.when(core == 0)
    def _():
        out_ref[0:half] = cur_s[...]
        out_ref[half:] = back_s[...].astype(jnp.float32)

    @pl.when(core == 1)
    def _():
        out_ref[0:half] = back_s[...].astype(jnp.float32)
        out_ref[half:] = cur_s[...]
        scale_add(out_ref, pair_d[...], out_ref, pair_s)

    final.wait_send()

    @pl.when(core == 0)
    def _():
        first[0](partner).wait_send()
        first_d(partner).wait_send()

    @pl.when(core == 1)
    def _():
        first[1](partner).wait_send()
        first_d(partner).wait_send()

    for sends, makers, distance in outgoing:

        @pl.when(sends)
        def _(makers=makers, distance=distance):
            for make in makers:
                make(2 * (chip + distance) + core).wait_send()


def state_scan(state, decay):
    count = lax.axis_size("seq")
    rounds = len(scan_distances(count // 2))
    heads = state.shape[0]
    half_shape = (heads // 2,) + state.shape[1:]
    half_decay = (2, heads // 4) + decay.shape[1:]
    return pl.pallas_call(
        functools.partial(state_scan_kernel, count),
        out_shape=jax.ShapeDtypeStruct(state.shape, jnp.float32),
        in_specs=[pl.BlockSpec(memory_space=pltpu.VMEM)] * 2,
        out_specs=pl.BlockSpec(memory_space=pltpu.VMEM),
        scratch_shapes=[
            pltpu.VMEM(state.shape, jnp.bfloat16),
            pltpu.VMEM(decay.shape, jnp.float32),
            pltpu.VMEM(state.shape, jnp.bfloat16),
            pltpu.VMEM(decay.shape, jnp.float32),
            pltpu.VMEM(half_shape, jnp.float32),
            pltpu.VMEM(half_decay, jnp.float32),
            pltpu.VMEM((rounds + 1,) + half_shape, jnp.bfloat16),
            pltpu.VMEM((rounds,) + half_decay, jnp.float32),
            pltpu.VMEM((rounds + 1,) + half_shape, jnp.bfloat16),
            pltpu.VMEM((rounds + 1,) + half_decay, jnp.float32),
            pltpu.VMEM(half_shape, jnp.bfloat16),
            pltpu.SemaphoreType.DMA((rounds + 3, 2, 2)),
            pltpu.SemaphoreType.DMA((rounds + 3, 2, 2)),
        ],
        compiler_params=pltpu.CompilerParams(collective_id=0, has_side_effects=True),
        name="state_scan",
    )(state, decay)

def ring_kernel(count, pieces, normed_ref, weight_ref, out_ref, send_buf, recv_buf, ssem, rsem):
    me = lax.axis_index("chan")
    seq = lax.axis_index("seq")
    width = out_ref.shape[1]
    rows = normed_ref.shape[1] // (2 * pieces)
    targets = (lax.rem(me + 1, count), lax.rem(me + count - 1, count))

    barrier = pltpu.get_barrier_semaphore()
    for target in targets:
        pl.semaphore_signal(barrier, 1, device_id=(seq, target), device_id_type=MESH)

    def copy(direction, step, piece):
        return pltpu.make_async_remote_copy(
            src_ref=send_buf.at[direction, step, piece],
            dst_ref=recv_buf.at[direction, step, piece],
            send_sem=ssem.at[direction, step, piece],
            recv_sem=rsem.at[direction, step, piece],
            device_id=(seq, targets[direction]),
            device_id_type=MESH,
        )

    def block(direction, step):
        if direction == 0:
            return lax.rem(me + 2 * count - 1 - step, count)
        return lax.rem(me + 1 + step, count)

    def partial(direction, step, piece):
        start = (direction * pieces + piece) * rows
        column = pl.multiple_of(block(direction, step) * width, width)
        return lax.dot_general(
            normed_ref[:, pl.ds(start, rows)],
            weight_ref[:, pl.ds(column, width)],
            (((0,), (0,)), ((), ())),
            preferred_element_type=jnp.float32,
        )

    def run_step(step, first, last):
        for piece in range(pieces):
            for direction in range(2):
                value = partial(direction, step, piece)
                if not first:
                    copy(direction, step - 1, piece).wait_recv()
                    value = value + recv_buf[direction, step - 1, piece].astype(jnp.float32)
                if last:
                    start = (direction * pieces + piece) * rows
                    out_ref[pl.ds(start, rows), :] = value.astype(out_ref.dtype)
                else:
                    send_buf[direction, step, piece] = value.astype(send_buf.dtype)
                    copy(direction, step, piece).start()

    for piece in range(pieces):
        for direction in range(2):
            send_buf[direction, 0, piece] = partial(direction, 0, piece).astype(send_buf.dtype)
    pl.semaphore_wait(barrier, 2)
    for piece in range(pieces):
        for direction in range(2):
            copy(direction, 0, piece).start()

    def middle(step, carry):
        run_step(step, False, False)
        return carry

    lax.fori_loop(1, count - 1, middle, 0)
    run_step(count - 1, False, True)

    def drain(step, carry):
        for piece in range(pieces):
            for direction in range(2):
                copy(direction, step, piece).wait_send()
        return carry

    lax.fori_loop(0, count - 1, drain, 0)


def ring_projection(normed, weight):
    count = lax.axis_size("chan")
    pieces = 2
    tokens = normed.shape[1]
    width = weight.shape[1] // count
    rows = tokens // (2 * pieces)
    buffers = (2, count - 1, pieces, rows, width)
    return pl.pallas_call(
        functools.partial(ring_kernel, count, pieces),
        out_shape=jax.ShapeDtypeStruct((tokens, width), jnp.bfloat16),
        in_specs=[pl.BlockSpec(memory_space=pltpu.VMEM)] * 2,
        out_specs=pl.BlockSpec(memory_space=pltpu.VMEM),
        scratch_shapes=[
            pltpu.VMEM(buffers, jnp.bfloat16),
            pltpu.VMEM(buffers, jnp.bfloat16),
            pltpu.SemaphoreType.DMA(buffers[:3]),
            pltpu.SemaphoreType.DMA(buffers[:3]),
        ],
        compiler_params=pltpu.CompilerParams(collective_id=1, has_side_effects=True),
        name="ring_projection",
    )(normed, weight)

def local(
    inner_input,
    state_maps,
    gate_input,
    step_input,
    log_decay_rate,
    step_bias,
    skip_gain,
    conv_kernel,
    map_kernel,
    norm_gain,
    out_weight,
):
    row_count = inner_input.shape[0]
    kernel_remainder = conv_kernel.shape[0] - 1
    groups = state_maps.shape[2]
    per_group = HEADS // NGROUPS
    head_count = groups * per_group
    block_count = row_count // BLOCK
    tail_inner, tail_maps = passed_along(
        (inner_input[row_count - kernel_remainder :], state_maps[row_count - kernel_remainder :]),
        "seq",
        1,
    )
    inner_conv = conv_silu(
        jnp.concatenate((tail_inner, inner_input), axis=0), conv_kernel, row_count
    )
    maps_conv = conv_silu(jnp.concatenate((tail_maps, state_maps), axis=0), map_kernel, row_count)
    step = jnp.minimum(jax.nn.softplus(step_input + step_bias), step_limit)
    log_step = step * -jnp.exp(log_decay_rate)
    step_blocks = step.reshape(block_count, BLOCK, groups, per_group)
    cumul = jnp.cumsum(log_step.reshape(block_count, BLOCK, groups, per_group), axis=1)
    x_blocks = inner_conv.reshape(block_count, BLOCK, groups, per_group, HEAD_DIM)
    b_blocks = maps_conv[:, 0].reshape(block_count, BLOCK, groups, STATE)
    c_blocks = maps_conv[:, 1].reshape(block_count, BLOCK, groups, STATE)
    scores = jnp.einsum("ctgn,csgn->cgts", c_blocks, b_blocks, preferred_element_type=jnp.float32)
    cumul_t = cumul.transpose(0, 2, 3, 1)
    gap = cumul_t[..., :, None] - cumul_t[..., None, :]
    row_ids = lax.broadcasted_iota(jnp.int32, (BLOCK, BLOCK), 0)
    col_ids = lax.broadcasted_iota(jnp.int32, (BLOCK, BLOCK), 1)
    decay = jnp.exp(jnp.where(row_ids >= col_ids, gap, -jnp.inf))
    mixing = (scores[:, :, None] * decay * step_blocks.transpose(0, 2, 3, 1)[..., None, :]).astype(
        jnp.bfloat16
    )
    y_local = jnp.einsum("cgjts,csgjp->ctgjp", mixing, x_blocks, preferred_element_type=jnp.float32)
    weighted = (
        (jnp.exp(cumul[:, -1:] - cumul) * step_blocks)[..., None] * b_blocks[:, :, :, None, :]
    ).astype(jnp.bfloat16)
    block_states = jnp.einsum(
        "csgjp,csgjn->cgjpn", x_blocks, weighted, preferred_element_type=jnp.float32
    )
    block_decay = cumul[:, -1]
    running = jnp.zeros((groups, per_group, HEAD_DIM, STATE), jnp.float32)
    local_in = []
    for block_index in range(block_count):
        local_in.append(running)
        running = (
            jnp.exp(block_decay[block_index])[..., None, None] * running + block_states[block_index]
        )
    slab_decay = jnp.sum(block_decay, axis=0)
    state_shape = (groups * per_group, HEAD_DIM, STATE)
    decay_tile = jnp.broadcast_to(slab_decay.reshape(groups * per_group, 1), (groups * per_group, STATE))
    entering = state_scan(running.reshape(state_shape), decay_tile).reshape(running.shape)
    leading = jnp.cumsum(block_decay, axis=0) - block_decay
    state_in = (
        jnp.exp(leading)[..., None, None] * entering[None] + jnp.stack(local_in, axis=0)
    ).astype(jnp.bfloat16)
    width = per_group * HEAD_DIM
    y_pre = lax.optimization_barrier(
        y_local + skip_gain.reshape(groups, per_group)[:, :, None] * x_blocks
    )
    chunk_count = 1
    per_chunk = block_count // chunk_count
    outs = []
    for chunk in range(chunk_count):
        part = slice(chunk * per_chunk, (chunk + 1) * per_chunk)
        rows = per_chunk * BLOCK
        y_carry = jnp.exp(cumul[part])[..., None] * jnp.einsum(
            "ctgn,cgjpn->ctgjp", c_blocks[part], state_in[part], preferred_element_type=jnp.float32
        )
        y_all = y_pre[part] + y_carry
        gate_rows = gate_input[chunk * rows : (chunk + 1) * rows]
        gated = y_all.reshape(rows, groups, width) * jax.nn.silu(
            gate_rows.reshape(rows, groups, width).astype(jnp.float32)
        )
        square_mean = jnp.mean(gated * gated, axis=-1, keepdims=True)
        normed = (
            (gated * lax.rsqrt(square_mean + epsilon) * norm_gain.reshape(groups, width))
            .astype(jnp.bfloat16)
            .reshape(rows, head_count * HEAD_DIM)
        )
        outs.append(ring_projection(normed.T, out_weight))
    return jnp.concatenate(outs, axis=0)


def solution(mesh):
    return jax.shard_map(
        local,
        mesh=mesh,
        in_specs=(
            P("seq", "chan"),
            P("seq", None, "chan", None),
            P("seq", "chan"),
            P("seq", "chan"),
            P("chan"),
            P("chan"),
            P("chan"),
            P(None, "chan"),
            P(None, None, "chan", None),
            P("chan"),
            P("chan", None),
        ),
        out_specs=P("seq", "chan"),
        check_vma=False,
    )
```

```python
import functools

import jax
import jax.numpy as jnp
from jax import lax
from jax.experimental import pallas as pl
from jax.experimental.pallas import tpu as pltpu
from jax.sharding import PartitionSpec as P

HEADS = 128
HEAD_DIM = 64
STATE = 128
NGROUPS = 8
BLOCK = 256


step_limit = 0.5
epsilon = 1e-05


def passed_along(x, axis, by):
    count = lax.axis_size(axis)
    pairs = [(i, i + by) for i in range(count) if 0 <= i + by < count]
    return lax.ppermute(x, axis, pairs)


def conv_silu(padded, kernel, length):
    acc = jnp.zeros((length,) + padded.shape[1:], jnp.float32)
    for offset in range(kernel.shape[0]):
        acc = acc + kernel[offset] * padded[offset : offset + length].astype(jnp.float32)
    return jax.nn.silu(acc).astype(jnp.bfloat16)


MESH = pl.DeviceIdType.MESH


def scan_distances(count):
    distances = []
    distance = 1
    while distance < count:
        distances.append(distance)
        distance *= 2
    return distances


def scale_add(out, decay, incoming, base):
    for head in range(out.shape[0]):
        out[head] = jnp.exp(decay[head : head + 1, :]) * incoming[head] + base[head]


def state_scan_kernel(
    count, state_ref, decay_ref, out_ref,
    own_s, own_d, pair_s, pair_d, cur_s, cur_d, send_s, send_d, recv_s, recv_d, back_s, ssem, rsem,
):
    me = lax.axis_index("seq")
    chan = lax.axis_index("chan")
    core = me % 2
    chip = me // 2
    chips = count // 2
    half = state_ref.shape[0] // 2
    partner = me + 1 - 2 * core
    distances = scan_distances(chips)

    barrier = pltpu.get_barrier_semaphore()
    pl.semaphore_signal(barrier, 1, device_id=(partner, chan), device_id_type=MESH)
    peers = jnp.int32(1)
    for distance in distances:
        for target in (chip + distance, chip - distance):
            valid = jnp.logical_and(target >= 0, target < chips)

            @pl.when(valid)
            def _(target=target):
                pl.semaphore_signal(
                    barrier, 1, device_id=(2 * target + core, chan), device_id_type=MESH
                )

            peers = peers + valid.astype(jnp.int32)
    own_s[...] = state_ref[...].astype(jnp.bfloat16)
    own_d[...] = decay_ref[...]
    pl.semaphore_wait(barrier, peers)

    def remote(src, dst, slot, part, target, piece=0):
        return pltpu.make_async_remote_copy(
            src_ref=src, dst_ref=dst, send_sem=ssem.at[slot, part, piece], recv_sem=rsem.at[slot, part, piece],
            device_id=(target, chan), device_id_type=MESH,
        )

    first = [
        lambda t: remote(own_s, pair_s, 0, 0, t),
        lambda t: remote(own_s.at[0:half], pair_s.at[0:half], 0, 0, t),
    ]
    first_d = lambda t: remote(own_d, pair_d, 0, 1, t)

    @pl.when(core == 0)
    def _():
        first[0](partner).start()
        first_d(partner).start()
        first[1](partner).wait_recv()
        first_d(partner).wait_recv()
        for piece in range(cur_d.shape[0]):
            rows = slice(piece * cur_d.shape[1], (piece + 1) * cur_d.shape[1])
            cur_d[piece] = own_d[rows] + pair_d[rows]
        scale_add(cur_s, pair_d[0:half], state_ref.at[0:half], pair_s[0:half].astype(jnp.float32))

    @pl.when(core == 1)
    def _():
        first[1](partner).start()
        first_d(partner).start()
        first[0](partner).wait_recv()
        first_d(partner).wait_recv()
        for piece in range(cur_d.shape[0]):
            rows = slice(half + piece * cur_d.shape[1], half + (piece + 1) * cur_d.shape[1])
            cur_d[piece] = own_d[rows] + pair_d[rows]
        scale_add(
            cur_s, own_d[half:], pair_s[half:].astype(jnp.float32), state_ref.at[half:]
        )

    rounds = [[1, 2]] + [[distance] for distance in distances[1:]]
    pieces = cur_d.shape[0]
    per_piece = half // pieces
    plan = []
    slot = 0
    for index, round_distances in enumerate(rounds):
        plan.append([(distance, slot + offset) for offset, distance in enumerate(round_distances)])
        slot += len(round_distances)
    outgoing = []

    def makers(index, at, piece):
        heads = slice(piece * per_piece, (piece + 1) * per_piece)
        return (
            lambda t: remote(send_s.at[index, heads], recv_s.at[at, heads], at + 1, 0, t, piece),
            lambda t: remote(send_d.at[index, piece], recv_d.at[at, piece], at + 1, 1, t, piece),
        )

    def send(index, piece):
        heads = slice(piece * per_piece, (piece + 1) * per_piece)
        send_s[index, heads] = cur_s[heads].astype(jnp.bfloat16)
        send_d[index, piece] = cur_d[piece]
        for distance, at in plan[index]:
            pair = makers(index, at, piece)
            sends = chip + distance < chips

            @pl.when(sends)
            def _(pair=pair, distance=distance):
                for make in pair:
                    make(2 * (chip + distance) + core).start()

            outgoing.append((sends, pair, distance))

    def receive(index, piece):
        heads = slice(piece * per_piece, (piece + 1) * per_piece)
        for distance, at in plan[index]:
            pair = makers(index, at, piece)
            receives = chip - distance >= 0
            opening = index == 0 and distance == 1

            @pl.when(receives)
            def _(pair=pair, distance=distance, at=at, opening=opening):
                for make in pair:
                    make(2 * (chip - distance) + core).wait_recv()
                if opening:
                    cur_s[heads] = recv_s[at, heads].astype(jnp.float32)
                    cur_d[piece] = recv_d[at, piece]
                else:
                    scale_add(cur_s.at[heads], cur_d[piece], recv_s.at[at, heads], cur_s.at[heads])
                    cur_d[piece] = recv_d[at, piece] + cur_d[piece]

            if opening:

                @pl.when(jnp.logical_not(receives))
                def _():
                    cur_s[heads] = jnp.zeros((per_piece,) + cur_s.shape[1:], jnp.float32)
                    cur_d[piece] = jnp.zeros(cur_d.shape[1:], jnp.float32)

    for piece in range(pieces):
        send(0, piece)
    for index in range(len(rounds)):
        for piece in range(pieces):
            receive(index, piece)
            if index + 1 < len(rounds):
                send(index + 1, piece)

    last = slot + 1
    own_half = send_s.at[len(rounds)]
    own_half[...] = cur_s[...].astype(jnp.bfloat16)
    final = remote(own_half, back_s, last, 0, partner)
    final.start()
    final.wait_recv()

    @pl.when(core == 0)
    def _():
        out_ref[0:half] = cur_s[...]
        out_ref[half:] = back_s[...].astype(jnp.float32)

    @pl.when(core == 1)
    def _():
        out_ref[0:half] = back_s[...].astype(jnp.float32)
        out_ref[half:] = cur_s[...]
        scale_add(out_ref, pair_d[...], out_ref, pair_s)

    final.wait_send()

    @pl.when(core == 0)
    def _():
        first[0](partner).wait_send()
        first_d(partner).wait_send()

    @pl.when(core == 1)
    def _():
        first[1](partner).wait_send()
        first_d(partner).wait_send()

    for sends, makers, distance in outgoing:

        @pl.when(sends)
        def _(makers=makers, distance=distance):
            for make in makers:
                make(2 * (chip + distance) + core).wait_send()


def state_scan(state, decay):
    count = lax.axis_size("seq")
    rounds = len(scan_distances(count // 2))
    heads = state.shape[0]
    half_shape = (heads // 2,) + state.shape[1:]
    half_decay = (2, heads // 4) + decay.shape[1:]
    return pl.pallas_call(
        functools.partial(state_scan_kernel, count),
        out_shape=jax.ShapeDtypeStruct(state.shape, jnp.float32),
        in_specs=[pl.BlockSpec(memory_space=pltpu.VMEM)] * 2,
        out_specs=pl.BlockSpec(memory_space=pltpu.VMEM),
        scratch_shapes=[
            pltpu.VMEM(state.shape, jnp.bfloat16),
            pltpu.VMEM(decay.shape, jnp.float32),
            pltpu.VMEM(state.shape, jnp.bfloat16),
            pltpu.VMEM(decay.shape, jnp.float32),
            pltpu.VMEM(half_shape, jnp.float32),
            pltpu.VMEM(half_decay, jnp.float32),
            pltpu.VMEM((rounds + 1,) + half_shape, jnp.bfloat16),
            pltpu.VMEM((rounds,) + half_decay, jnp.float32),
            pltpu.VMEM((rounds + 1,) + half_shape, jnp.bfloat16),
            pltpu.VMEM((rounds + 1,) + half_decay, jnp.float32),
            pltpu.VMEM(half_shape, jnp.bfloat16),
            pltpu.SemaphoreType.DMA((rounds + 3, 2, 2)),
            pltpu.SemaphoreType.DMA((rounds + 3, 2, 2)),
        ],
        compiler_params=pltpu.CompilerParams(collective_id=0, has_side_effects=True),
        name="state_scan",
    )(state, decay)

def ring_kernel(count, pieces, normed_ref, weight_ref, out_ref, send_buf, recv_buf, ssem, rsem):
    me = lax.axis_index("chan")
    seq = lax.axis_index("seq")
    width = out_ref.shape[1]
    rows = normed_ref.shape[1] // (2 * pieces)
    targets = (lax.rem(me + 1, count), lax.rem(me + count - 1, count))

    barrier = pltpu.get_barrier_semaphore()
    for target in targets:
        pl.semaphore_signal(barrier, 1, device_id=(seq, target), device_id_type=MESH)
    pl.semaphore_wait(barrier, 2)

    def copy(direction, step, piece):
        return pltpu.make_async_remote_copy(
            src_ref=send_buf.at[direction, step, piece],
            dst_ref=recv_buf.at[direction, step, piece],
            send_sem=ssem.at[direction, step, piece],
            recv_sem=rsem.at[direction, step, piece],
            device_id=(seq, targets[direction]),
            device_id_type=MESH,
        )

    def block(direction, step):
        if direction == 0:
            return lax.rem(me + 2 * count - 1 - step, count)
        return lax.rem(me + 1 + step, count)

    def partial(direction, step, piece):
        start = (direction * pieces + piece) * rows
        column = pl.multiple_of(block(direction, step) * width, width)
        return lax.dot_general(
            normed_ref[:, pl.ds(start, rows)],
            weight_ref[:, pl.ds(column, width)],
            (((0,), (0,)), ((), ())),
            preferred_element_type=jnp.float32,
        )

    def run_step(step, first, last):
        for piece in range(pieces):
            for direction in range(2):
                value = partial(direction, step, piece)
                if not first:
                    copy(direction, step - 1, piece).wait_recv()
                    value = value + recv_buf[direction, step - 1, piece].astype(jnp.float32)
                if last:
                    start = (direction * pieces + piece) * rows
                    out_ref[pl.ds(start, rows), :] = value.astype(out_ref.dtype)
                else:
                    send_buf[direction, step, piece] = value.astype(send_buf.dtype)
                    copy(direction, step, piece).start()

    run_step(0, True, False)

    def middle(step, carry):
        run_step(step, False, False)
        return carry

    lax.fori_loop(1, count - 1, middle, 0)
    run_step(count - 1, False, True)

    def drain(step, carry):
        for piece in range(pieces):
            for direction in range(2):
                copy(direction, step, piece).wait_send()
        return carry

    lax.fori_loop(0, count - 1, drain, 0)


def ring_projection(normed, weight):
    count = lax.axis_size("chan")
    pieces = 2
    tokens = normed.shape[1]
    width = weight.shape[1] // count
    rows = tokens // (2 * pieces)
    buffers = (2, count - 1, pieces, rows, width)
    return pl.pallas_call(
        functools.partial(ring_kernel, count, pieces),
        out_shape=jax.ShapeDtypeStruct((tokens, width), jnp.bfloat16),
        in_specs=[pl.BlockSpec(memory_space=pltpu.VMEM)] * 2,
        out_specs=pl.BlockSpec(memory_space=pltpu.VMEM),
        scratch_shapes=[
            pltpu.VMEM(buffers, jnp.bfloat16),
            pltpu.VMEM(buffers, jnp.bfloat16),
            pltpu.SemaphoreType.DMA(buffers[:3]),
            pltpu.SemaphoreType.DMA(buffers[:3]),
        ],
        compiler_params=pltpu.CompilerParams(collective_id=1, has_side_effects=True),
        name="ring_projection",
    )(normed, weight)

def local(
    inner_input,
    state_maps,
    gate_input,
    step_input,
    log_decay_rate,
    step_bias,
    skip_gain,
    conv_kernel,
    map_kernel,
    norm_gain,
    out_weight,
):
    row_count = inner_input.shape[0]
    kernel_remainder = conv_kernel.shape[0] - 1
    groups = state_maps.shape[2]
    per_group = HEADS // NGROUPS
    head_count = groups * per_group
    block_count = row_count // BLOCK
    tail_inner, tail_maps = passed_along(
        (inner_input[row_count - kernel_remainder :], state_maps[row_count - kernel_remainder :]),
        "seq",
        1,
    )
    inner_conv = conv_silu(
        jnp.concatenate((tail_inner, inner_input), axis=0), conv_kernel, row_count
    )
    maps_conv = conv_silu(jnp.concatenate((tail_maps, state_maps), axis=0), map_kernel, row_count)
    step = jnp.minimum(jax.nn.softplus(step_input + step_bias), step_limit)
    log_step = step * -jnp.exp(log_decay_rate)
    step_blocks = step.reshape(block_count, BLOCK, groups, per_group)
    cumul = jnp.cumsum(log_step.reshape(block_count, BLOCK, groups, per_group), axis=1)
    x_blocks = inner_conv.reshape(block_count, BLOCK, groups, per_group, HEAD_DIM)
    b_blocks = maps_conv[:, 0].reshape(block_count, BLOCK, groups, STATE)
    c_blocks = maps_conv[:, 1].reshape(block_count, BLOCK, groups, STATE)
    scores = jnp.einsum("ctgn,csgn->cgts", c_blocks, b_blocks, preferred_element_type=jnp.float32)
    cumul_t = cumul.transpose(0, 2, 3, 1)
    gap = cumul_t[..., :, None] - cumul_t[..., None, :]
    row_ids = lax.broadcasted_iota(jnp.int32, (BLOCK, BLOCK), 0)
    col_ids = lax.broadcasted_iota(jnp.int32, (BLOCK, BLOCK), 1)
    decay = jnp.exp(jnp.where(row_ids >= col_ids, gap, -jnp.inf))
    mixing = (scores[:, :, None] * decay * step_blocks.transpose(0, 2, 3, 1)[..., None, :]).astype(
        jnp.bfloat16
    )
    y_local = jnp.einsum("cgjts,csgjp->ctgjp", mixing, x_blocks, preferred_element_type=jnp.float32)
    weighted = (
        (jnp.exp(cumul[:, -1:] - cumul) * step_blocks)[..., None] * b_blocks[:, :, :, None, :]
    ).astype(jnp.bfloat16)
    block_states = jnp.einsum(
        "csgjp,csgjn->cgjpn", x_blocks, weighted, preferred_element_type=jnp.float32
    )
    block_decay = cumul[:, -1]
    running = jnp.zeros((groups, per_group, HEAD_DIM, STATE), jnp.float32)
    local_in = []
    for block_index in range(block_count):
        local_in.append(running)
        running = (
            jnp.exp(block_decay[block_index])[..., None, None] * running + block_states[block_index]
        )
    slab_decay = jnp.sum(block_decay, axis=0)
    state_shape = (groups * per_group, HEAD_DIM, STATE)
    decay_tile = jnp.broadcast_to(slab_decay.reshape(groups * per_group, 1), (groups * per_group, STATE))
    entering = state_scan(running.reshape(state_shape), decay_tile).reshape(running.shape)
    leading = jnp.cumsum(block_decay, axis=0) - block_decay
    state_in = (
        jnp.exp(leading)[..., None, None] * entering[None] + jnp.stack(local_in, axis=0)
    ).astype(jnp.bfloat16)
    width = per_group * HEAD_DIM
    y_pre = lax.optimization_barrier(
        y_local + skip_gain.reshape(groups, per_group)[:, :, None] * x_blocks
    )
    chunk_count = 1
    per_chunk = block_count // chunk_count
    outs = []
    for chunk in range(chunk_count):
        part = slice(chunk * per_chunk, (chunk + 1) * per_chunk)
        rows = per_chunk * BLOCK
        y_carry = jnp.exp(cumul[part])[..., None] * jnp.einsum(
            "ctgn,cgjpn->ctgjp", c_blocks[part], state_in[part], preferred_element_type=jnp.float32
        )
        y_all = y_pre[part] + y_carry
        gate_rows = gate_input[chunk * rows : (chunk + 1) * rows]
        gated = y_all.reshape(rows, groups, width) * jax.nn.silu(
            gate_rows.reshape(rows, groups, width).astype(jnp.float32)
        )
        square_mean = jnp.mean(gated * gated, axis=-1, keepdims=True)
        normed = (
            (gated * lax.rsqrt(square_mean + epsilon) * norm_gain.reshape(groups, width))
            .astype(jnp.bfloat16)
            .reshape(rows, head_count * HEAD_DIM)
        )
        outs.append(ring_projection(normed.T, out_weight))
    return jnp.concatenate(outs, axis=0)


def solution(mesh):
    return jax.shard_map(
        local,
        mesh=mesh,
        in_specs=(
            P("seq", "chan"),
            P("seq", None, "chan", None),
            P("seq", "chan"),
            P("seq", "chan"),
            P("chan"),
            P("chan"),
            P("chan"),
            P(None, "chan"),
            P(None, None, "chan", None),
            P("chan"),
            P("chan", None),
        ),
        out_specs=P("seq", "chan"),
        check_vma=False,
    )
```

```python
import functools

import jax
import jax.numpy as jnp
from jax import lax
from jax.experimental import pallas as pl
from jax.experimental.pallas import tpu as pltpu
from jax.sharding import PartitionSpec as P

HEADS = 128
HEAD_DIM = 64
STATE = 128
NGROUPS = 8
BLOCK = 256


step_limit = 0.5
epsilon = 1e-05


def passed_along(x, axis, by):
    count = lax.axis_size(axis)
    pairs = [(i, i + by) for i in range(count) if 0 <= i + by < count]
    return lax.ppermute(x, axis, pairs)


def conv_silu(padded, kernel, length):
    acc = jnp.zeros((length,) + padded.shape[1:], jnp.float32)
    for offset in range(kernel.shape[0]):
        acc = acc + kernel[offset] * padded[offset : offset + length].astype(jnp.float32)
    return jax.nn.silu(acc).astype(jnp.bfloat16)


MESH = pl.DeviceIdType.MESH


def scan_distances(count):
    distances = []
    distance = 1
    while distance < count:
        distances.append(distance)
        distance *= 2
    return distances


def scale_add(out, decay, incoming, base):
    for head in range(out.shape[0]):
        out[head] = jnp.exp(decay[head : head + 1, :]) * incoming[head] + base[head]


def state_scan_kernel(
    count, state_ref, decay_ref, out_ref,
    own_s, own_d, pair_s, pair_d, cur_s, cur_d, send_s, send_d, recv_s, recv_d, back_s, ssem, rsem,
):
    me = lax.axis_index("seq")
    chan = lax.axis_index("chan")
    core = me % 2
    chip = me // 2
    chips = count // 2
    half = state_ref.shape[0] // 2
    partner = me + 1 - 2 * core
    distances = scan_distances(chips)

    barrier = pltpu.get_barrier_semaphore()
    pl.semaphore_signal(barrier, 1, device_id=(partner, chan), device_id_type=MESH)
    peers = jnp.int32(1)
    for distance in distances:
        for target in (chip + distance, chip - distance):
            valid = jnp.logical_and(target >= 0, target < chips)

            @pl.when(valid)
            def _(target=target):
                pl.semaphore_signal(
                    barrier, 1, device_id=(2 * target + core, chan), device_id_type=MESH
                )

            peers = peers + valid.astype(jnp.int32)
    own_s[...] = state_ref[...].astype(jnp.bfloat16)
    own_d[...] = decay_ref[...]
    pl.semaphore_wait(barrier, peers)

    def remote(src, dst, slot, part, target, piece=0):
        return pltpu.make_async_remote_copy(
            src_ref=src, dst_ref=dst, send_sem=ssem.at[slot, part, piece], recv_sem=rsem.at[slot, part, piece],
            device_id=(target, chan), device_id_type=MESH,
        )

    first = [
        lambda t: remote(own_s, pair_s, 0, 0, t),
        lambda t: remote(own_s.at[0:half], pair_s.at[0:half], 0, 0, t),
    ]
    first_d = lambda t: remote(own_d, pair_d, 0, 1, t)

    @pl.when(core == 0)
    def _():
        first[0](partner).start()
        first_d(partner).start()
        first[1](partner).wait_recv()
        first_d(partner).wait_recv()
        for piece in range(cur_d.shape[0]):
            rows = slice(piece * cur_d.shape[1], (piece + 1) * cur_d.shape[1])
            cur_d[piece] = own_d[rows] + pair_d[rows]
        scale_add(cur_s, pair_d[0:half], state_ref.at[0:half], pair_s[0:half].astype(jnp.float32))

    @pl.when(core == 1)
    def _():
        first[1](partner).start()
        first_d(partner).start()
        first[0](partner).wait_recv()
        first_d(partner).wait_recv()
        for piece in range(cur_d.shape[0]):
            rows = slice(half + piece * cur_d.shape[1], half + (piece + 1) * cur_d.shape[1])
            cur_d[piece] = own_d[rows] + pair_d[rows]
        scale_add(
            cur_s, own_d[half:], pair_s[half:].astype(jnp.float32), state_ref.at[half:]
        )

    rounds = [[1, 2]] + [[distance] for distance in distances[1:]]
    pieces = cur_d.shape[0]
    per_piece = half // pieces
    plan = []
    slot = 0
    for index, round_distances in enumerate(rounds):
        plan.append([(distance, slot + offset) for offset, distance in enumerate(round_distances)])
        slot += len(round_distances)
    outgoing = []

    def makers(index, at, piece):
        heads = slice(piece * per_piece, (piece + 1) * per_piece)
        return (
            lambda t: remote(send_s.at[index, heads], recv_s.at[at, heads], at + 1, 0, t, piece),
            lambda t: remote(send_d.at[index, piece], recv_d.at[at, piece], at + 1, 1, t, piece),
        )

    def send(index, piece):
        heads = slice(piece * per_piece, (piece + 1) * per_piece)
        send_s[index, heads] = cur_s[heads].astype(jnp.bfloat16)
        send_d[index, piece] = cur_d[piece]
        for distance, at in plan[index]:
            pair = makers(index, at, piece)
            sends = chip + distance < chips

            @pl.when(sends)
            def _(pair=pair, distance=distance):
                for make in pair:
                    make(2 * (chip + distance) + core).start()

            outgoing.append((sends, pair, distance))

    def receive(index, piece):
        heads = slice(piece * per_piece, (piece + 1) * per_piece)
        for distance, at in plan[index]:
            pair = makers(index, at, piece)
            receives = chip - distance >= 0
            opening = index == 0 and distance == 1

            @pl.when(receives)
            def _(pair=pair, distance=distance, at=at, opening=opening):
                for make in pair:
                    make(2 * (chip - distance) + core).wait_recv()
                if opening:
                    cur_s[heads] = recv_s[at, heads].astype(jnp.float32)
                    cur_d[piece] = recv_d[at, piece]
                else:
                    scale_add(cur_s.at[heads], cur_d[piece], recv_s.at[at, heads], cur_s.at[heads])
                    cur_d[piece] = recv_d[at, piece] + cur_d[piece]

            if opening:

                @pl.when(jnp.logical_not(receives))
                def _():
                    cur_s[heads] = jnp.zeros((per_piece,) + cur_s.shape[1:], jnp.float32)
                    cur_d[piece] = jnp.zeros(cur_d.shape[1:], jnp.float32)

    for piece in range(pieces):
        send(0, piece)
    for index in range(len(rounds)):
        for piece in range(pieces):
            receive(index, piece)
            if index + 1 < len(rounds):
                send(index + 1, piece)

    last = slot + 1
    own_half = send_s.at[len(rounds)]
    own_half[...] = cur_s[...].astype(jnp.bfloat16)
    final = remote(own_half, back_s, last, 0, partner)
    final.start()
    final.wait_recv()

    @pl.when(core == 0)
    def _():
        out_ref[0:half] = cur_s[...]
        out_ref[half:] = back_s[...].astype(jnp.float32)

    @pl.when(core == 1)
    def _():
        out_ref[0:half] = back_s[...].astype(jnp.float32)
        out_ref[half:] = cur_s[...]
        scale_add(out_ref, pair_d[...], out_ref, pair_s)

    final.wait_send()

    @pl.when(core == 0)
    def _():
        first[0](partner).wait_send()
        first_d(partner).wait_send()

    @pl.when(core == 1)
    def _():
        first[1](partner).wait_send()
        first_d(partner).wait_send()

    for sends, makers, distance in outgoing:

        @pl.when(sends)
        def _(makers=makers, distance=distance):
            for make in makers:
                make(2 * (chip + distance) + core).wait_send()


def state_scan(state, decay):
    count = lax.axis_size("seq")
    rounds = len(scan_distances(count // 2))
    heads = state.shape[0]
    half_shape = (heads // 2,) + state.shape[1:]
    half_decay = (2, heads // 4) + decay.shape[1:]
    return pl.pallas_call(
        functools.partial(state_scan_kernel, count),
        out_shape=jax.ShapeDtypeStruct(state.shape, jnp.float32),
        in_specs=[pl.BlockSpec(memory_space=pltpu.VMEM)] * 2,
        out_specs=pl.BlockSpec(memory_space=pltpu.VMEM),
        scratch_shapes=[
            pltpu.VMEM(state.shape, jnp.bfloat16),
            pltpu.VMEM(decay.shape, jnp.float32),
            pltpu.VMEM(state.shape, jnp.bfloat16),
            pltpu.VMEM(decay.shape, jnp.float32),
            pltpu.VMEM(half_shape, jnp.float32),
            pltpu.VMEM(half_decay, jnp.float32),
            pltpu.VMEM((rounds + 1,) + half_shape, jnp.bfloat16),
            pltpu.VMEM((rounds,) + half_decay, jnp.float32),
            pltpu.VMEM((rounds + 1,) + half_shape, jnp.bfloat16),
            pltpu.VMEM((rounds + 1,) + half_decay, jnp.float32),
            pltpu.VMEM(half_shape, jnp.bfloat16),
            pltpu.SemaphoreType.DMA((rounds + 3, 2, 2)),
            pltpu.SemaphoreType.DMA((rounds + 3, 2, 2)),
        ],
        compiler_params=pltpu.CompilerParams(collective_id=0, has_side_effects=True),
        name="state_scan",
    )(state, decay)

def ring_kernel(count, pieces, normed_ref, weight_ref, out_ref, send_buf, recv_buf, ssem, rsem):
    me = lax.axis_index("chan")
    seq = lax.axis_index("seq")
    width = out_ref.shape[1]
    rows = normed_ref.shape[1] // (2 * pieces)
    targets = (lax.rem(me + 1, count), lax.rem(me + count - 1, count))

    barrier = pltpu.get_barrier_semaphore()
    for target in targets:
        pl.semaphore_signal(barrier, 1, device_id=(seq, target), device_id_type=MESH)

    def copy(direction, step, piece):
        return pltpu.make_async_remote_copy(
            src_ref=send_buf.at[direction, step, piece],
            dst_ref=recv_buf.at[direction, step, piece],
            send_sem=ssem.at[direction, step, piece],
            recv_sem=rsem.at[direction, step, piece],
            device_id=(seq, targets[direction]),
            device_id_type=MESH,
        )

    def block(direction, step):
        if direction == 0:
            return lax.rem(me + 2 * count - 1 - step, count)
        return lax.rem(me + 1 + step, count)

    def partial(direction, step, piece):
        start = (direction * pieces + piece) * rows
        column = pl.multiple_of(block(direction, step) * width, width)
        return lax.dot_general(
            normed_ref[:, pl.ds(start, rows)],
            weight_ref[:, pl.ds(column, width)],
            (((0,), (0,)), ((), ())),
            preferred_element_type=jnp.float32,
        )

    def run_step(step, first, last):
        for piece in range(pieces):
            for direction in range(2):
                value = partial(direction, step, piece)
                if not first:
                    copy(direction, step - 1, piece).wait_recv()
                    value = value + recv_buf[direction, step - 1, piece].astype(jnp.float32)
                if last:
                    start = (direction * pieces + piece) * rows
                    out_ref[pl.ds(start, rows), :] = value.astype(out_ref.dtype)
                else:
                    send_buf[direction, step, piece] = value.astype(send_buf.dtype)
                    copy(direction, step, piece).start()

    for piece in range(pieces):
        for direction in range(2):
            send_buf[direction, 0, piece] = partial(direction, 0, piece).astype(send_buf.dtype)
    pl.semaphore_wait(barrier, 2)
    for piece in range(pieces):
        for direction in range(2):
            copy(direction, 0, piece).start()

    def middle(step, carry):
        run_step(step, False, False)
        return carry

    lax.fori_loop(1, count - 1, middle, 0)
    run_step(count - 1, False, True)

    def drain(step, carry):
        for piece in range(pieces):
            for direction in range(2):
                copy(direction, step, piece).wait_send()
        return carry

    lax.fori_loop(0, count - 1, drain, 0)


def ring_projection(normed, weight):
    count = lax.axis_size("chan")
    pieces = 2
    tokens = normed.shape[1]
    width = weight.shape[1] // count
    rows = tokens // (2 * pieces)
    buffers = (2, count - 1, pieces, rows, width)
    return pl.pallas_call(
        functools.partial(ring_kernel, count, pieces),
        out_shape=jax.ShapeDtypeStruct((tokens, width), jnp.bfloat16),
        in_specs=[pl.BlockSpec(memory_space=pltpu.VMEM)] * 2,
        out_specs=pl.BlockSpec(memory_space=pltpu.VMEM),
        scratch_shapes=[
            pltpu.VMEM(buffers, jnp.bfloat16),
            pltpu.VMEM(buffers, jnp.bfloat16),
            pltpu.SemaphoreType.DMA(buffers[:3]),
            pltpu.SemaphoreType.DMA(buffers[:3]),
        ],
        compiler_params=pltpu.CompilerParams(collective_id=1, has_side_effects=True),
        name="ring_projection",
    )(normed, weight)

def local(
    inner_input,
    state_maps,
    gate_input,
    step_input,
    log_decay_rate,
    step_bias,
    skip_gain,
    conv_kernel,
    map_kernel,
    norm_gain,
    out_weight,
):
    row_count = inner_input.shape[0]
    kernel_remainder = conv_kernel.shape[0] - 1
    groups = state_maps.shape[2]
    per_group = HEADS // NGROUPS
    head_count = groups * per_group
    block_count = row_count // BLOCK
    tail_inner, tail_maps = passed_along(
        (inner_input[row_count - kernel_remainder :], state_maps[row_count - kernel_remainder :]),
        "seq",
        1,
    )
    inner_conv = conv_silu(
        jnp.concatenate((tail_inner, inner_input), axis=0), conv_kernel, row_count
    )
    maps_conv = conv_silu(jnp.concatenate((tail_maps, state_maps), axis=0), map_kernel, row_count)
    step = jnp.minimum(jax.nn.softplus(step_input + step_bias), step_limit)
    log_step = step * -jnp.exp(log_decay_rate)
    step_blocks = step.reshape(block_count, BLOCK, groups, per_group)
    cumul = jnp.cumsum(log_step.reshape(block_count, BLOCK, groups, per_group), axis=1)
    x_blocks = inner_conv.reshape(block_count, BLOCK, groups, per_group, HEAD_DIM)
    b_blocks = maps_conv[:, 0].reshape(block_count, BLOCK, groups, STATE)
    c_blocks = maps_conv[:, 1].reshape(block_count, BLOCK, groups, STATE)
    scores = jnp.einsum("ctgn,csgn->cgts", c_blocks, b_blocks, preferred_element_type=jnp.float32)
    cumul_t = cumul.transpose(0, 2, 3, 1)
    gap = cumul_t[..., :, None] - cumul_t[..., None, :]
    row_ids = lax.broadcasted_iota(jnp.int32, (BLOCK, BLOCK), 0)
    col_ids = lax.broadcasted_iota(jnp.int32, (BLOCK, BLOCK), 1)
    decay = jnp.exp(jnp.where(row_ids >= col_ids, gap, -jnp.inf))
    mixing = (scores[:, :, None] * decay * step_blocks.transpose(0, 2, 3, 1)[..., None, :]).astype(
        jnp.bfloat16
    )
    y_local = jnp.einsum("cgjts,csgjp->ctgjp", mixing, x_blocks, preferred_element_type=jnp.float32)
    weighted = (
        (jnp.exp(cumul[:, -1:] - cumul) * step_blocks)[..., None] * b_blocks[:, :, :, None, :]
    ).astype(jnp.bfloat16)
    block_states = jnp.einsum(
        "csgjp,csgjn->cgjpn", x_blocks, weighted, preferred_element_type=jnp.float32
    )
    block_decay = cumul[:, -1]
    running = jnp.zeros((groups, per_group, HEAD_DIM, STATE), jnp.float32)
    local_in = []
    for block_index in range(block_count):
        local_in.append(running)
        running = (
            jnp.exp(block_decay[block_index])[..., None, None] * running + block_states[block_index]
        )
    slab_decay = jnp.sum(block_decay, axis=0)
    state_shape = (groups * per_group, HEAD_DIM, STATE)
    decay_tile = jnp.broadcast_to(slab_decay.reshape(groups * per_group, 1), (groups * per_group, STATE))
    entering = state_scan(running.reshape(state_shape), decay_tile).reshape(running.shape)
    leading = jnp.cumsum(block_decay, axis=0) - block_decay
    state_in = (
        jnp.exp(leading)[..., None, None] * entering[None] + jnp.stack(local_in, axis=0)
    ).astype(jnp.bfloat16)
    width = per_group * HEAD_DIM
    y_pre = lax.optimization_barrier(
        y_local + skip_gain.reshape(groups, per_group)[:, :, None] * x_blocks
    )
    chunk_count = 1
    per_chunk = block_count // chunk_count
    outs = []
    for chunk in range(chunk_count):
        part = slice(chunk * per_chunk, (chunk + 1) * per_chunk)
        rows = per_chunk * BLOCK
        y_carry = jnp.exp(cumul[part])[..., None] * jnp.einsum(
            "ctgn,cgjpn->ctgjp", c_blocks[part], state_in[part], preferred_element_type=jnp.float32
        )
        y_all = y_pre[part] + y_carry
        gate_rows = gate_input[chunk * rows : (chunk + 1) * rows]
        gated = y_all.reshape(rows, groups, width) * jax.nn.silu(
            gate_rows.reshape(rows, groups, width).astype(jnp.float32)
        )
        square_mean = jnp.mean(gated * gated, axis=-1, keepdims=True)
        normed = (
            (gated * lax.rsqrt(square_mean + epsilon) * norm_gain.reshape(groups, width))
            .astype(jnp.bfloat16)
            .reshape(rows, head_count * HEAD_DIM)
        )
        outs.append(ring_projection(normed.T, out_weight))
    return jnp.concatenate(outs, axis=0)


def solution(mesh):
    return jax.shard_map(
        local,
        mesh=mesh,
        in_specs=(
            P("seq", "chan"),
            P("seq", None, "chan", None),
            P("seq", "chan"),
            P("seq", "chan"),
            P("chan"),
            P("chan"),
            P("chan"),
            P(None, "chan"),
            P(None, None, "chan", None),
            P("chan"),
            P("chan", None),
        ),
        out_specs=P("seq", "chan"),
        check_vma=False,
    )
```
